256 devices in a mesh: row: 16 (over y, z_hi), col: 8 (over x, core), gz: 2 (over z_lo).
Axes of the slice: x: 4, y: 4, z: 8 (z_hi: 4, z_lo: 2; z = z_hi * 2 + z_lo), core: 2. Of those that a mesh axis runs over, the one named last changes fastest.
Arguments:
- source: float32 [2, 4, 1024, 1024], P(None, 'gz', 'row', 'col'), may hold values from -24 to 24
- cell_class: int32 [4, 1024, 1024], P('gz', 'row', 'col'), may hold values from 0 to 7
- coeff_table: float32 [8], replicated, may hold values from 0.5 to 8
- owner_cell: int32 [32768], P(('row', 'col', 'gz')), may hold values from 0 to 16383
- node_pos: float32 [3, 32768], P(None, ('row', 'col', 'gz')), may hold values from 0 to 1
- node_weight: float32 [32768], P(('row', 'col', 'gz')), may hold values from 0.002 to 0.02
Outputs:
- potential: float32 [2, 4, 1024, 1024], P(None, 'gz', 'row', 'col')
- boundary_values: float32 [2, 32768], P(None, ('row', 'col', 'gz'))
The draws below stay inside these ranges and needn't reach their ends.
Inputs may be any that keep to these rules, and one draw needn't show every extreme that they name: `owner_cell`: each boundary node names a cell of its own device's tile, a flat index over 2 x 64 x 128 cells with the layer slowest.
All inputs are finite; a program needn't handle non-finite values.
Results may differ from the reference program's by a relative error of at most 0.0003.
Values sent between devices are 32-bit elements; how exact they have to be, the bound alone decides.
No kernel may reach another device: no remote copies, remote signals or barrier semaphores. Data moves between devices by JAX's collectives and lax.ppermute only.
A program may use at most 64 MiB of HBM per device.

```python
import math
import jax
import jax.numpy as jnp
from jax import lax

IMG = 2
CZ = 2
CX = 64
CY = 128
BN_DEV = 128
SWEEPS = 4
CLASSES = 8
NZ = 4
NX = 1024
NY = 1024
BND = 32768
N_COL = 8
N_GZ = 2


def touch_ends(values, stream_key, smallest, high):
    longest = values.shape.index(max(values.shape))
    spots = []
    for shift in (0, 1):
        where = [jax.random.randint(jax.random.fold_in(stream_key, axis), (), 0, length) for axis, length in enumerate(values.shape)]
        where[longest] = (where[longest] + shift) % values.shape[longest]
        spots.append(tuple(where))
    return values.at[spots[0]].set(smallest).at[spots[1]].set(high)


def block_scale(stream_key, extent, shards, smallest, top_value):
    factor_of = 1.0
    for axis_at, blocks in shards:
        steps = jax.random.uniform(jax.random.fold_in(jax.random.fold_in(stream_key, 6), axis_at), (blocks,), jnp.float32, smallest / len(shards), top_value / len(shards))
        factor_of = factor_of * jnp.repeat(jnp.exp(steps), extent[axis_at] // blocks).reshape((-1,) + (1,) * (len(extent) - 1 - axis_at))
    return factor_of


def noise(rng, shape, width, reach, split=(), kind=jnp.bfloat16):
    gain = block_scale(rng, shape, split, -0.22, 0.18) if split else 1.0
    array = jax.random.normal(rng, shape, jnp.float32) * width * gain
    return jnp.minimum(jnp.maximum(array, -reach), reach).astype(kind)


def setup_inputs(seed: int = 0) -> dict:
    streams_of = jax.random.split(jax.random.key(seed), 7)
    return {
        "source": noise(streams_of[0], (IMG, NZ, NX, NY), 4.0, 24.0, ((1, 2), (2, 16), (3, 8)), jnp.float32),
        "cell_class": touch_ends(jax.random.randint(streams_of[1], (NZ, NX, NY), 0, CLASSES), jax.random.fold_in(streams_of[1], 1), 0, CLASSES - 1).astype(jnp.int32),
        "coeff_table": jnp.clip(jnp.exp(jax.random.uniform(streams_of[2], (CLASSES,), jnp.float32, math.log(0.5), math.log(8.0))), 0.5, 8.0),
        "owner_cell": touch_ends(jax.random.randint(streams_of[3], (BND,), 0, CZ * CX * CY), jax.random.fold_in(streams_of[3], 1), 0, (CZ * CX * CY) - 1).astype(jnp.int32),
        "node_pos": jnp.clip(1.0 * jax.random.uniform(streams_of[4], (3, BND), jnp.float32) ** block_scale(streams_of[4], (3, BND), ((1, 256),), -0.2, 0.2), 0.0, 1.0),
        "node_weight": jnp.clip(jnp.exp(math.log(0.02) - 2.30258502 * jax.random.uniform(streams_of[5], (BND,), jnp.float32) ** block_scale(streams_of[5], (BND,), ((0, 256),), -0.2, 0.2)), 0.002, 0.02),
    }


OMEGA = 0.8
RELAX = 0.5
SOFTEN = 0.01

def lookup_diagonal(cell_class, coeff_table):
    summed = jnp.zeros(cell_class.shape, jnp.float32)
    for class_level in range(coeff_table.shape[0]):
        summed = summed + jnp.where(cell_class == class_level, coeff_table[class_level], jnp.zeros((), coeff_table.dtype))
    return 6.0 + summed

def relax_field(field, forcing, diagonal):
    for repeat in range(SWEEPS):
        padded = jnp.pad(field, ((0, 0), (1, 1), (1, 1), (1, 1)))
        beside = padded[:, 2:, 1:-1, 1:-1] + padded[:, :-2, 1:-1, 1:-1]
        beside = beside + padded[:, 1:-1, 2:, 1:-1] + padded[:, 1:-1, :-2, 1:-1]
        beside = beside + padded[:, 1:-1, 1:-1, 2:] + padded[:, 1:-1, 1:-1, :-2]
        field = field + OMEGA * (forcing - (diagonal * field - beside)) / diagonal
    return field

def node_cells(owner_cell):
    nodes = jnp.arange(BND, dtype=jnp.int32)
    device = nodes // BN_DEV
    row_place = device // (N_COL * N_GZ)
    col_place = device // N_GZ % N_COL
    depth_place = device % N_GZ
    layer = owner_cell // (CX * CY)
    across = owner_cell // CY % CX
    along = owner_cell % CY
    flat = ((depth_place * CZ + layer) * NX + row_place * CX + across) * NY + col_place * CY + along
    return flat.astype(jnp.int32)

def boundary_sum(trace, node_pos, node_weight):
    block_rows = min(512, BND)
    targets = node_pos.reshape(3, BND // block_rows, block_rows).transpose(1, 0, 2)

    def block_sum(target):
        diff_x = target[0][:, None] - node_pos[0][None, :]
        diff_y = target[1][:, None] - node_pos[1][None, :]
        diff_z = target[2][:, None] - node_pos[2][None, :]
        inverse = lax.rsqrt(diff_x * diff_x + diff_y * diff_y + diff_z * diff_z + SOFTEN)
        kernel = node_weight[None, :] * diff_z * inverse * inverse * inverse
        return lax.dot_general(trace, kernel, (((1,), (1,)), ((), ())), precision=lax.Precision.HIGHEST, preferred_element_type=jnp.float32)
    pieces = lax.map(block_sum, targets)
    return pieces.transpose(1, 0, 2).reshape(trace.shape[0], BND)

def fk_round(forcing, first, second, diagonal, cells, node_pos, node_weight):
    first = relax_field(first, forcing, diagonal)
    images = first.shape[0]
    trace = first.reshape(images, -1)[:, cells]
    values = -0.5 * trace + boundary_sum(trace, node_pos, node_weight)
    spread = jnp.zeros((images, NZ * NX * NY), jnp.float32).at[:, cells].add(values).reshape(first.shape)
    second = relax_field(second, spread, diagonal)
    return (first, second, values)

def reference(source, cell_class, coeff_table, owner_cell, node_pos, node_weight):
    diagonal = lookup_diagonal(cell_class, coeff_table)
    cells = node_cells(owner_cell)
    first = jnp.zeros(source.shape, jnp.float32)
    second = jnp.zeros(source.shape, jnp.float32)
    first, second, values = fk_round(source, first, second, diagonal, cells, node_pos, node_weight)
    forcing = source - RELAX * (first + second)
    first, second, values = fk_round(forcing, first, second, diagonal, cells, node_pos, node_weight)
    return (first + second, values)
```

```python
import functools

import jax
import jax.numpy as jnp
from jax import lax
from jax.experimental import pallas as pl
from jax.experimental.pallas import tpu as pltpu
from jax.sharding import PartitionSpec as P

SWEEPS = 4
OMEGA = 0.8
RELAX = 0.5
SOFTEN = 0.01
H = 8
HIGH = lax.Precision.HIGHEST
F32 = jnp.float32


def iota(shape, axis):
    return lax.broadcasted_iota(jnp.int32, shape, axis)


def pick(flag, shape, yes, no):
    return jnp.where(jnp.full(shape, flag, jnp.int32) == 1, yes, no)


def place(me_ref, n_col):
    me = me_ref[0]
    gz = lax.rem(me, 2)
    col = lax.rem(me // 2, n_col)
    row = me // (2 * n_col)
    return row, col, gz


def layer_of(own_ref, other_ref, kind, z, gz, shape):
    mine = pick(gz, shape, 1, 0) == z // 2
    return jnp.where(mine, own_ref[kind, z % 2], other_ref[kind, z % 2])


def col_pack(n_col, me_ref, own_ref, other_ref, a_ref, b_ref):
    _, col, gz = place(me_ref, n_col)
    shape = own_ref.shape[2:]
    lane = iota(shape, 1)
    left = jnp.zeros(shape, F32)
    right = jnp.zeros(shape, F32)
    for s in range(12):
        cell = layer_of(own_ref, other_ref, s // 4, s % 4, gz, shape)
        here = (lane >= 8 * s) & (lane < 8 * s + 8)
        low = pltpu.roll(cell, 8 * s, 1) if s else cell
        left = jnp.where(here, low, left)
        right = jnp.where(here, pltpu.roll(cell, 8 * s + 8, 1), right)
    odd = lax.rem(col, 2)
    a_ref[...] = pick(odd, shape, left, right)
    b_ref[...] = pick(odd, shape, right, left)


def row_pack(n_col, me_ref, own_ref, other_ref, a_in, b_in, ext_ref, a_ref, b_ref):
    row, col, gz = place(me_ref, n_col)
    shape = own_ref.shape[2:]
    rows, lanes = shape
    lane = iota(shape, 1)
    odd_col = lax.rem(col, 2)
    from_right = pick(odd_col, shape, b_in[...], a_in[...])
    from_left = pick(odd_col, shape, a_in[...], b_in[...])
    odd = lax.rem(row, 2)
    edge = (H, 2 * lanes)
    for s in range(12):
        cell = layer_of(own_ref, other_ref, s // 4, s % 4, gz, shape)
        low = pltpu.roll(from_right, lanes - 8 * s, 1) if s else from_right
        high = pltpu.roll(from_left, lanes - 8 - 8 * s, 1)
        side = jnp.where(lane < 8, low, jnp.where(lane >= lanes - 8, high, 0.0))
        ext_ref[s, :, 0:lanes] = cell
        ext_ref[s, :, lanes : 2 * lanes] = side
        top = ext_ref[s, 0:H, :]
        bottom = ext_ref[s, rows - H : rows, :]
        a_ref[s] = pick(odd, edge, top, bottom)
        b_ref[s] = pick(odd, edge, bottom, top)


def sweep(now_ref, next_ref, force_ref, weight_ref):
    rows, lanes = now_ref.shape[2:]

    def image(m, carry):
        for z in range(4):
            cell = now_ref[m, z]
            beside = pltpu.roll(cell, 1, 0) + pltpu.roll(cell, rows - 1, 0)
            beside = beside + (pltpu.roll(cell, 1, 1) + pltpu.roll(cell, lanes - 1, 1))
            if z > 0:
                beside = beside + now_ref[m, z - 1]
            if z < 3:
                beside = beside + now_ref[m, z + 1]
            next_ref[m, z] = (1.0 - OMEGA) * cell + (force_ref[m, z] + weight_ref[z] * beside)
        return carry

    lax.fori_loop(0, now_ref.shape[0], image, 0)


def read_trace(field_ref, owner_ref, node_ref, gz, t_ref, u_ref):
    owner = owner_ref[...]
    nodes = owner.shape[1]
    shape = (128, nodes)
    at_row = jnp.where(iota(shape, 0) == owner // 128, 1.0, 0.0).astype(F32)
    at_lane = iota(shape, 0) == lax.rem(owner, 128)
    for m in range(2):
        field = jnp.concatenate([field_ref[m, 2 * gz + k, H : H + 64, 0:128] for k in range(2)], 0)
        found = lax.dot_general(
            field, at_row, (((0,), (0,)), ((), ())), precision=HIGH, preferred_element_type=F32
        )
        trace = jnp.sum(jnp.where(at_lane, found, 0.0), axis=0, keepdims=True)
        t_ref[m : m + 1, :] = trace
        u_ref[m : m + 1, :] = trace * node_ref[...]


def first_relax(
    n_col, me_ref, ext_ref, a_in, b_in, owner_ref, node_ref, full_ref, first_ref, t_ref, u_ref, force, spare
):
    row, _, gz = place(me_ref, n_col)
    odd = lax.rem(row, 2)
    edge = a_in.shape[1:]
    for s in range(12):
        full_ref[s // 4, s % 4, 0:H, :] = pick(odd, edge, a_in[s], b_in[s])
        full_ref[s // 4, s % 4, H : H + 64, :] = ext_ref[s]
        full_ref[s // 4, s % 4, H + 64 : 2 * H + 64, :] = pick(odd, edge, b_in[s], a_in[s])
    weight = full_ref.at[2]
    for m in range(2):
        for z in range(4):
            force[m, z] = full_ref[m, z] * weight[z]
    sweep(force, first_ref, force, weight)
    sweep(first_ref, spare, force, weight)
    sweep(spare, first_ref, force, weight)
    read_trace(first_ref, owner_ref, node_ref, gz, t_ref, u_ref)


def load_spread(odd, spread_ref, a_in, b_in, weight, force):
    edge = a_in.shape[1:]
    for s in range(8):
        m, z = s // 4, s % 4
        force[m, z, 0:H, :] = pick(odd, edge, a_in[s], b_in[s]) * weight[z, 0:H]
        force[m, z, H : H + 64, :] = spread_ref[s] * weight[z, H : H + 64]
        force[m, z, H + 64 : 2 * H + 64, :] = pick(odd, edge, b_in[s], a_in[s]) * weight[z, H + 64 : 2 * H + 64]


def second_round(
    n_col, me_ref, full_ref, first_ref, spread_ref, a_in, b_in, owner_ref, node_ref,
    second_ref, keep_ref, t_ref, u_ref, force, spare, other,
):
    row, _, gz = place(me_ref, n_col)
    weight = full_ref.at[2]
    load_spread(lax.rem(row, 2), spread_ref, a_in, b_in, weight, force)
    sweep(force, second_ref, force, weight)
    sweep(second_ref, spare, force, weight)
    sweep(spare, second_ref, force, weight)
    for m in range(2):
        for z in range(4):
            force[m, z] = (full_ref[m, z] - RELAX * (first_ref[m, z] + second_ref[m, z])) * weight[z]
    sweep(first_ref, spare, force, weight)
    sweep(spare, other, force, weight)
    sweep(other, spare, force, weight)
    sweep(spare, other, force, weight)
    for m in range(2):
        for k in range(2):
            keep_ref[m, k] = other[m, 2 * gz + k, H : H + 64, 0:128]
    read_trace(other, owner_ref, node_ref, gz, t_ref, u_ref)


def last_relax(
    n_col, me_ref, full_ref, second_ref, spread_ref, a_in, b_in, keep_ref, out_ref, force, spare, other
):
    row, _, gz = place(me_ref, n_col)
    weight = full_ref.at[2]
    load_spread(lax.rem(row, 2), spread_ref, a_in, b_in, weight, force)
    sweep(second_ref, spare, force, weight)
    sweep(spare, other, force, weight)
    sweep(other, spare, force, weight)
    sweep(spare, other, force, weight)
    for m in range(2):
        for k in range(2):
            out_ref[m, k] = keep_ref[m, k] + other[m, 2 * gz + k, H : H + 64, 0:128]


def pair_kernel(source_ref, target_ref, out_ref):
    nodes = source_ref.shape[2]
    square = (nodes, nodes)
    at = [jnp.broadcast_to(source_ref[0, k : k + 1, :], square).T for k in range(3)]
    for t in range(target_ref.shape[0]):
        dx = target_ref[t, 0:1, :] - at[0]
        dy = target_ref[t, 1:2, :] - at[1]
        dz = target_ref[t, 2:3, :] - at[2]
        inverse = lax.rsqrt(dx * dx + dy * dy + (dz * dz + SOFTEN))
        out_ref[0, :, t * nodes : (t + 1) * nodes] = dz * inverse * (inverse * inverse)


def apply_kernel(n_col, steps, me_ref, u_ref, pair_ref, t_ref, out_ref, acc, lined):
    step = pl.program_id(0)
    _, col, gz = place(me_ref, n_col)
    nodes = u_ref.shape[2]
    square = (nodes, nodes)
    blocks = 2 * n_col

    @pl.when(step == 0)
    def _():
        acc[...] = jnp.zeros_like(acc)

    for k in range(pair_ref.shape[0]):
        at = [jnp.broadcast_to(u_ref[k, m : m + 1, :], square).T for m in range(2)]
        for t in range(blocks):
            pair = pair_ref[k, :, t * nodes : (t + 1) * nodes]
            for m in range(2):
                part = jnp.sum((pair * at[m]).reshape(nodes // 8, 8, nodes), axis=0)
                acc[m, t] = acc[m, t] + part

    @pl.when(step == steps - 1)
    def _():
        lined[...] = jnp.zeros_like(lined)
        for t in range(blocks):
            mine = jnp.where(2 * col + gz == t, -0.5, 0.0).astype(F32)
            for m in range(2):
                whole = jnp.sum(acc[m, t], axis=0, keepdims=True)
                lined[m, t + 2 : t + 3, :] = whole + mine * t_ref[m : m + 1, :]
        for c in range(n_col):
            for m in range(2):
                near = lined[m, 2 * c : 2 * c + 8, :]
                out_ref[2 * c, 8 * m : 8 * m + 8, :] = near
                out_ref[2 * c + 1, 8 * m : 8 * m + 8, :] = near


def spread_nodes(n_col, me_ref, part_ref, target_ref, spread_ref, a_ref, b_ref, value_ref):
    row, col, gz = place(me_ref, n_col)
    nodes = part_ref.shape[2]
    blocks = 2 * n_col
    value = part_ref[0]
    for k in range(1, blocks):
        value = value + part_ref[k]
    shape = (128, nodes)
    down = iota(shape, 0)
    weighted, lanes = [], []
    for b in range(6):
        at = jnp.clip(2 * col - 2 + b, 0, blocks - 1)
        owner = target_ref[at, 3:4, :].astype(jnp.int32)
        hit = down == owner // 128
        weighted.append(
            jnp.concatenate([jnp.where(hit, value[8 * m + b : 8 * m + b + 1, :], 0.0) for m in range(2)], 0)
        )
        lane = down == lax.rem(owner, 128)
        if b < 2:
            lane = lane & (down >= 128 - H)
        if b > 3:
            lane = lane & (down < H)
        lanes.append(jnp.where(lane, 1.0, 0.0).astype(F32))

    def product(a, b):
        return lax.dot_general(a, b, (((1,), (1,)), ((), ())), precision=HIGH, preferred_element_type=F32)

    for g in range(2):
        own = product(weighted[2 + g], lanes[2 + g])
        side = product(
            jnp.concatenate([weighted[g], weighted[4 + g]], 1), jnp.concatenate([lanes[g], lanes[4 + g]], 1)
        )
        for m in range(2):
            for k in range(2):
                start = 128 * m + 64 * k
                spread_ref[4 * m + 2 * g + k, :, 0:128] = own[start : start + 64]
                spread_ref[4 * m + 2 * g + k, :, 128:256] = side[start : start + 64]
    odd = lax.rem(row, 2)
    edge = (H, 256)
    for s in range(8):
        top = spread_ref[s, 0:H, :]
        bottom = spread_ref[s, 64 - H : 64, :]
        a_ref[s] = pick(odd, edge, top, bottom)
        b_ref[s] = pick(odd, edge, bottom, top)
    for m in range(2):
        value_ref[m : m + 1, :] = pick(
            gz, (1, nodes), value[8 * m + 3 : 8 * m + 4, :], value[8 * m + 2 : 8 * m + 3, :]
        )


SMEM = pl.BlockSpec(memory_space=pltpu.SMEM)
VMEM = pl.BlockSpec(memory_space=pltpu.VMEM)


def run(body, name, outs, args, scratch=(), flops=0):
    moved = sum(a.size * 4 for a in args) + sum(4 * functools.reduce(lambda a, b: a * b, o) for o in outs)
    return pl.pallas_call(
        body,
        name=name,
        out_shape=[jax.ShapeDtypeStruct(o, F32) for o in outs],
        in_specs=[SMEM] + [VMEM] * (len(args) - 1),
        out_specs=[VMEM] * len(outs),
        scratch_shapes=[pltpu.VMEM(s, F32) for s in scratch],
        compiler_params=pltpu.CompilerParams(vmem_limit_bytes=24 << 20),
        cost_estimate=pl.CostEstimate(flops=flops, bytes_accessed=moved, transcendentals=0),
    )(*args)


def on_device(
    n_row, n_col, source, cell_class, coeff_table, owner_cell, node_pos, node_weight
):
    everything = ("row", "col", "gz")
    nodes = owner_cell.shape[0]
    me = lax.axis_index(everything).reshape(1)

    def swaps(axis, size, a, b):
        first = [(i, i ^ 1) for i in range(size)]
        second = [(i + 1, i + 2) for i in range(0, size - 2, 2)]
        second = second + [(j, i) for i, j in second]
        return lax.ppermute(a, axis, first), lax.ppermute(b, axis, second)

    def gathered(x, axes, count):
        return lax.all_to_all(jnp.broadcast_to(x[None], (count,) + x.shape), axes, 0, 0)

    summed = jnp.zeros(cell_class.shape, F32)
    for level in range(coeff_table.shape[0]):
        summed = summed + jnp.where(cell_class == level, coeff_table[level], 0.0)
    packed = jnp.concatenate([source, (OMEGA / (6.0 + summed))[None]], 0)
    other = lax.ppermute(packed, "gz", [(0, 1), (1, 0)])
    owner = owner_cell[None, :]
    weight = node_weight[None, :]
    target = gathered(
        jnp.concatenate([node_pos, owner.astype(F32)], 0), ("col", "gz"), 2 * n_col
    )
    origin = gathered(node_pos, "row", n_row)

    a, b = run(functools.partial(col_pack, n_col), "col_pack", [(64, 128)] * 2, [me, packed, other])
    a, b = swaps("col", n_col, a, b)
    ext, a, b = run(
        functools.partial(row_pack, n_col),
        "row_pack",
        [(12, 64, 256), (12, H, 256), (12, H, 256)],
        [me, packed, other, a, b],
    )
    a, b = swaps("row", n_row, a, b)

    blocks = 2 * n_col
    pairs = pl.pallas_call(
        pair_kernel,
        name="pair_kernel",
        grid=(n_row,),
        out_shape=jax.ShapeDtypeStruct((n_row, nodes, blocks * nodes), F32),
        in_specs=[
            pl.BlockSpec((1, 3, nodes), lambda i: (i, 0, 0)),
            pl.BlockSpec((blocks, 4, nodes), lambda i: (0, 0, 0)),
        ],
        out_specs=pl.BlockSpec((1, nodes, blocks * nodes), lambda i: (i, 0, 0)),
        compiler_params=pltpu.CompilerParams(vmem_limit_bytes=16 << 20),
        cost_estimate=pl.CostEstimate(
            flops=14 * n_row * blocks * nodes * nodes,
            bytes_accessed=4 * n_row * blocks * nodes * nodes,
            transcendentals=n_row * blocks * nodes * nodes,
        ),
    )(origin, target)

    field = (2, 4, 64 + 2 * H, 256)
    full, first, trace, sent = run(
        functools.partial(first_relax, n_col),
        "first_relax",
        [(3, 4, 64 + 2 * H, 256), field, (2, nodes), (2, nodes)],
        [me, ext, a, b, owner, weight],
        [field] * 2,
    )

    group = 2

    def values_of(trace, sent):
        heard = gathered(sent, "row", n_row)
        partial = pl.pallas_call(
            functools.partial(apply_kernel, n_col, n_row // group),
            name="apply_kernel",
            grid=(n_row // group,),
            out_shape=jax.ShapeDtypeStruct((blocks, 16, nodes), F32),
            in_specs=[
                SMEM,
                pl.BlockSpec((group, 2, nodes), lambda i: (i, 0, 0)),
                pl.BlockSpec((group, nodes, blocks * nodes), lambda i: (i, 0, 0)),
                pl.BlockSpec((2, nodes), lambda i: (0, 0)),
            ],
            out_specs=pl.BlockSpec((blocks, 16, nodes), lambda i: (0, 0, 0)),
            scratch_shapes=[
                pltpu.VMEM((2, blocks, 8, nodes), F32),
                pltpu.VMEM((2, blocks + 8, nodes), F32),
            ],
            compiler_params=pltpu.CompilerParams(vmem_limit_bytes=24 << 20),
            cost_estimate=pl.CostEstimate(
                flops=4 * n_row * blocks * nodes * nodes,
                bytes_accessed=4 * n_row * blocks * nodes * nodes,
                transcendentals=0,
            ),
        )(me, heard, pairs, trace)
        partial = lax.all_to_all(partial, ("col", "gz"), 0, 0)
        spread, a, b, values = run(
            functools.partial(spread_nodes, n_col),
            "spread_nodes",
            [(8, 64, 256), (8, H, 256), (8, H, 256), (2, nodes)],
            [me, partial, target],
        )
        a, b = swaps("row", n_row, a, b)
        return spread, a, b, values

    spread, a, b, _ = values_of(trace, sent)
    second, keep, trace, sent = run(
        functools.partial(second_round, n_col),
        "second_round",
        [field, (2, 2, 64, 128), (2, nodes), (2, nodes)],
        [me, full, first, spread, a, b, owner, weight],
        [field] * 3,
    )
    spread, a, b, values = values_of(trace, sent)
    (potential,) = run(
        functools.partial(last_relax, n_col),
        "last_relax",
        [(2, 2, 64, 128)],
        [me, full, second, spread, a, b, keep],
        [field] * 3,
    )
    return potential, values


def solution(mesh):
    return jax.shard_map(
        functools.partial(on_device, mesh.shape["row"], mesh.shape["col"]),
        mesh=mesh,
        in_specs=(
            P(None, "gz", "row", "col"),
            P("gz", "row", "col"),
            P(),
            P(("row", "col", "gz")),
            P(None, ("row", "col", "gz")),
            P(("row", "col", "gz")),
        ),
        out_specs=(P(None, "gz", "row", "col"), P(None, ("row", "col", "gz"))),
        check_vma=False,
    )
```

```python
import functools

import jax
import jax.numpy as jnp
from jax import lax
from jax.experimental import pallas as pl
from jax.experimental.pallas import tpu as pltpu
from jax.sharding import PartitionSpec as P

SWEEPS = 4
OMEGA = 0.8
RELAX = 0.5
SOFTEN = 0.01
H = 8
HIGH = lax.Precision.HIGHEST
F32 = jnp.float32


def iota(shape, axis):
    return lax.broadcasted_iota(jnp.int32, shape, axis)


def pick(flag, shape, yes, no):
    return jnp.where(jnp.full(shape, flag, jnp.int32) == 1, yes, no)


def place(me_ref, n_col):
    me = me_ref[0]
    gz = lax.rem(me, 2)
    col = lax.rem(me // 2, n_col)
    row = me // (2 * n_col)
    return row, col, gz


def layer_of(own_ref, other_ref, kind, z, gz, shape):
    mine = pick(gz, shape, 1, 0) == z // 2
    return jnp.where(mine, own_ref[kind, z % 2], other_ref[kind, z % 2])


def col_pack(n_col, me_ref, own_ref, other_ref, a_ref, b_ref):
    _, col, gz = place(me_ref, n_col)
    shape = own_ref.shape[2:]
    lane = iota(shape, 1)
    left = jnp.zeros(shape, F32)
    right = jnp.zeros(shape, F32)
    for s in range(12):
        cell = layer_of(own_ref, other_ref, s // 4, s % 4, gz, shape)
        here = (lane >= 8 * s) & (lane < 8 * s + 8)
        low = pltpu.roll(cell, 8 * s, 1) if s else cell
        left = jnp.where(here, low, left)
        right = jnp.where(here, pltpu.roll(cell, 8 * s + 8, 1), right)
    odd = lax.rem(col, 2)
    a_ref[...] = pick(odd, shape, left, right)
    b_ref[...] = pick(odd, shape, right, left)


def row_pack(n_col, me_ref, own_ref, other_ref, a_in, b_in, info_ref, ext_ref, a_ref, b_ref, told_ref):
    row, col, gz = place(me_ref, n_col)
    shape = own_ref.shape[2:]
    rows, lanes = shape
    lane = iota(shape, 1)
    odd_col = lax.rem(col, 2)
    from_right = pick(odd_col, shape, b_in[...], a_in[...])
    from_left = pick(odd_col, shape, a_in[...], b_in[...])
    odd = lax.rem(row, 2)
    edge = (H, 2 * lanes)
    for s in range(12):
        cell = layer_of(own_ref, other_ref, s // 4, s % 4, gz, shape)
        low = pltpu.roll(from_right, lanes - 8 * s, 1) if s else from_right
        high = pltpu.roll(from_left, lanes - 8 - 8 * s, 1)
        side = jnp.where(lane < 8, low, jnp.where(lane >= lanes - 8, high, 0.0))
        ext_ref[s, :, 0:lanes] = cell
        ext_ref[s, :, lanes : 2 * lanes] = side
        top = ext_ref[s, 0:H, :]
        bottom = ext_ref[s, rows - H : rows, :]
        a_ref[s] = pick(odd, edge, top, bottom)
        b_ref[s] = pick(odd, edge, bottom, top)
    for k in range(told_ref.shape[0]):
        told_ref[k] = info_ref[...]


def sweep(now_ref, next_ref, force_ref, weight_ref):
    rows, lanes = now_ref.shape[2:]

    def image(m, carry):
        for z in range(4):
            cell = now_ref[m, z]
            beside = pltpu.roll(cell, 1, 0) + pltpu.roll(cell, rows - 1, 0)
            beside = beside + (pltpu.roll(cell, 1, 1) + pltpu.roll(cell, lanes - 1, 1))
            if z > 0:
                beside = beside + now_ref[m, z - 1]
            if z < 3:
                beside = beside + now_ref[m, z + 1]
            next_ref[m, z] = (1.0 - OMEGA) * cell + (force_ref[m, z] + weight_ref[z] * beside)
        return carry

    lax.fori_loop(0, now_ref.shape[0], image, 0)


def trace_of(rows, owner, first_row):
    span = rows.shape[0] // 2
    nodes = owner.shape[1]
    line = iota((2 * span, nodes), 0)
    line = line + first_row + jnp.where(line >= span, 64 - span, 0)
    at_row = jnp.where(line == owner // 128, 1.0, 0.0).astype(F32)
    at_lane = iota((128, nodes), 0) == lax.rem(owner, 128)
    found = lax.dot_general(rows, at_row, (((0,), (0,)), ((), ())), precision=HIGH, preferred_element_type=F32)
    return jnp.sum(jnp.where(at_lane, found, 0.0), axis=0, keepdims=True)


def two_layers(field_ref, m, gz, start, size):
    return jnp.concatenate([field_ref[m, 2 * gz + k, start : start + size, 0:128] for k in range(2)], 0)


def prepare(me_ref, table_ref, source_ref, class_ref, owner_ref, pos_ref, node_ref, pack_ref, info_ref):
    for k in range(2):
        level = class_ref[k]
        found = jnp.zeros(level.shape, F32)
        for n in range(table_ref.shape[0]):
            found = jnp.where(level == n, table_ref[n], found)
        pack_ref[2, k] = OMEGA / (6.0 + found)
        for m in range(2):
            pack_ref[m, k] = source_ref[m, k]
    info_ref[...] = jnp.zeros_like(info_ref)
    info_ref[2:5, :] = pos_ref[...]
    info_ref[5:6, :] = owner_ref[...].astype(F32)
    info_ref[6:7, :] = node_ref[...]


def first_relax(n_col, me_ref, ext_ref, a_in, b_in, info_ref, full_ref, first_ref, sent_ref, force, spare):
    row, _, gz = place(me_ref, n_col)
    odd = lax.rem(row, 2)
    edge = a_in.shape[1:]
    for s in range(12):
        full_ref[s // 4, s % 4, 0:H, :] = pick(odd, edge, a_in[s], b_in[s])
        full_ref[s // 4, s % 4, H : H + 64, :] = ext_ref[s]
        full_ref[s // 4, s % 4, H + 64 : 2 * H + 64, :] = pick(odd, edge, b_in[s], a_in[s])
    weight = full_ref.at[2]
    for m in range(2):
        for z in range(4):
            force[m, z] = full_ref[m, z] * weight[z]
    sweep(force, first_ref, force, weight)
    sweep(first_ref, spare, force, weight)
    sweep(spare, first_ref, force, weight)
    owner = info_ref[5:6, :].astype(jnp.int32)
    line = iota(info_ref.shape, 0)
    info = info_ref[...]
    for m in range(2):
        info = jnp.where(line == m, trace_of(two_layers(first_ref, m, gz, H, 64), owner, 0), info)
    for k in range(sent_ref.shape[0]):
        sent_ref[k] = info


def carry_relax(n_col, me_ref, full_ref, first_ref, info_ref, keep_ref, trace_ref, force, spare, other):
    _, _, gz = place(me_ref, n_col)
    weight = full_ref.at[2]
    for m in range(2):
        for z in range(4):
            force[m, z] = (full_ref[m, z] - RELAX * first_ref[m, z]) * weight[z]
    sweep(first_ref, spare, force, weight)
    sweep(spare, other, force, weight)
    sweep(other, spare, force, weight)
    sweep(spare, other, force, weight)
    owner = info_ref[5:6, :].astype(jnp.int32)
    for m in range(2):
        for k in range(2):
            keep_ref[m, k] = other[m, 2 * gz + k, H : H + 64, 0:128]
        trace_ref[m : m + 1, :] = trace_of(two_layers(other, m, gz, H, 64), owner, 0)


def columns(rows, count):
    nodes = rows.shape[1]
    return [jnp.broadcast_to(rows[k : k + 1, :], (nodes, nodes)).T for k in range(count)]


def finish_apply(n_col, col, gz, acc, lined, own, out_ref):
    lined[...] = jnp.zeros_like(lined)
    for t in range(2 * n_col):
        mine = jnp.where(2 * col + gz == t, -0.5, 0.0).astype(F32)
        for m in range(2):
            whole = jnp.sum(acc[m, t], axis=0, keepdims=True)
            lined[m, t + 2 : t + 3, :] = whole + mine * own[m : m + 1, :]
    for c in range(n_col):
        for m in range(2):
            near = lined[m, 2 * c : 2 * c + 8, :]
            out_ref[2 * c, 8 * m : 8 * m + 8, :] = near
            out_ref[2 * c + 1, 8 * m : 8 * m + 8, :] = near


def build_apply(n_col, n_row, me_ref, heard_ref, target_ref, pair_ref, out_ref, acc, lined):
    step = pl.program_id(0)
    row, col, gz = place(me_ref, n_col)
    nodes = heard_ref.shape[2]

    @pl.when(step == 0)
    def _():
        acc[...] = jnp.zeros_like(acc)

    heard = heard_ref[step]
    at = columns(heard[2:5, :], 3)
    by = columns(heard[0:2, :] * heard[6:7, :], 2)
    for t in range(target_ref.shape[0]):
        dx = target_ref[t, 2:3, :] - at[0]
        dy = target_ref[t, 3:4, :] - at[1]
        dz = target_ref[t, 4:5, :] - at[2]
        inverse = lax.rsqrt(dx * dx + dy * dy + (dz * dz + SOFTEN))
        pair = dz * inverse * (inverse * inverse)
        pair_ref[0, :, t * nodes : (t + 1) * nodes] = pair
        for m in range(2):
            acc[m, t] = acc[m, t] + jnp.sum((pair * by[m]).reshape(nodes // 8, 8, nodes), axis=0)

    @pl.when(step == n_row - 1)
    def _():
        finish_apply(n_col, col, gz, acc, lined, heard_ref[row], out_ref)


def reapply(n_col, steps, me_ref, heard_ref, info_ref, pair_ref, out_ref, acc, lined, trace):
    step = pl.program_id(0)
    row, col, gz = place(me_ref, n_col)
    nodes = heard_ref.shape[2]
    n_row = heard_ref.shape[0]

    @pl.when(step == 0)
    def _():
        acc[...] = jnp.zeros_like(acc)
        for k in range(n_row):
            whole = heard_ref[k, 0:2, :]
            if k + 1 < n_row:
                whole = whole + heard_ref[k + 1, 2:4, :]
            if k > 0:
                whole = whole + heard_ref[k - 1, 4:6, :]
            trace[k, 0:2, :] = whole
            trace[k, 2:4, :] = whole * info_ref[k, 6:7, :]

    for k in range(pair_ref.shape[0]):
        by = columns(trace[step * pair_ref.shape[0] + k, 2:4, :], 2)
        for t in range(2 * n_col):
            pair = pair_ref[k, :, t * nodes : (t + 1) * nodes]
            for m in range(2):
                acc[m, t] = acc[m, t] + jnp.sum((pair * by[m]).reshape(nodes // 8, 8, nodes), axis=0)

    @pl.when(step == steps - 1)
    def _():
        finish_apply(n_col, col, gz, acc, lined, trace[row], out_ref)


def spread_nodes(n_col, col, part_ref, target_ref, spread_ref):
    nodes = part_ref.shape[2]
    blocks = 2 * n_col
    value = part_ref[0]
    for k in range(1, blocks):
        value = value + part_ref[k]
    shape = (128, nodes)
    down = iota(shape, 0)
    weighted, lanes = [], []
    for b in range(6):
        at = jnp.clip(2 * col - 2 + b, 0, blocks - 1)
        owner = target_ref[at, 5:6, :].astype(jnp.int32)
        hit = down == owner // 128
        weighted.append(
            jnp.concatenate([jnp.where(hit, value[8 * m + b : 8 * m + b + 1, :], 0.0) for m in range(2)], 0)
        )
        lane = down == lax.rem(owner, 128)
        if b < 2:
            lane = lane & (down >= 128 - H)
        if b > 3:
            lane = lane & (down < H)
        lanes.append(jnp.where(lane, 1.0, 0.0).astype(F32))

    def product(a, b):
        return lax.dot_general(a, b, (((1,), (1,)), ((), ())), precision=HIGH, preferred_element_type=F32)

    for g in range(2):
        own = product(weighted[2 + g], lanes[2 + g])
        side = product(
            jnp.concatenate([weighted[g], weighted[4 + g]], 1), jnp.concatenate([lanes[g], lanes[4 + g]], 1)
        )
        for m in range(2):
            for k in range(2):
                start = 128 * m + 64 * k
                spread_ref[4 * m + 2 * g + k, :, 0:128] = own[start : start + 64]
                spread_ref[4 * m + 2 * g + k, :, 128:256] = side[start : start + 64]
    return value


def respond(
    n_col, n_row, me_ref, part_ref, target_ref, full_ref, heard_ref, kept_ref,
    spread_ref, sent_ref, force, spare, other,
):
    row, col, gz = place(me_ref, n_col)
    weight = full_ref.at[2]
    spread_nodes(n_col, col, part_ref, target_ref, spread_ref)
    empty = jnp.zeros((H, 256), F32)
    for m in range(2):
        for z in range(4):
            force[m, z, 0:H, :] = empty
            force[m, z, H : H + 64, :] = spread_ref[4 * m + z] * weight[z, H : H + 64]
            force[m, z, H + 64 : 2 * H + 64, :] = empty
    sweep(force, spare, force, weight)
    sweep(spare, other, force, weight)
    sweep(other, spare, force, weight)
    for m in range(2):
        for z in range(4):
            force[m, z] = (-RELAX * spare[m, z]) * weight[z]
    sweep(force, other, force, weight)
    sweep(other, spare, force, weight)
    sweep(spare, other, force, weight)
    own = heard_ref[row, 5:6, :].astype(jnp.int32)
    above = heard_ref[jnp.maximum(row - 1, 0), 5:6, :].astype(jnp.int32)
    below = heard_ref[jnp.minimum(row + 1, n_row - 1), 5:6, :].astype(jnp.int32)
    line = iota((8, own.shape[1]), 0)
    sent = jnp.zeros((8, own.shape[1]), F32)
    for m in range(2):
        here = trace_of(two_layers(other, m, gz, H, 64), own, 0) + kept_ref[m : m + 1, :]
        sent = jnp.where(line == m, here, sent)
        sent = jnp.where(line == 2 + m, trace_of(two_layers(other, m, gz, 0, H), above, 64 - H), sent)
        sent = jnp.where(line == 4 + m, trace_of(two_layers(other, m, gz, H + 64, H), below, 0), sent)
    for k in range(sent_ref.shape[0]):
        sent_ref[k] = sent


def last_spread(n_col, me_ref, part_ref, target_ref, before_ref, spread_ref, a_ref, b_ref, value_ref):
    row, col, gz = place(me_ref, n_col)
    value = spread_nodes(n_col, col, part_ref, target_ref, spread_ref)
    odd = lax.rem(row, 2)
    edge = (H, 256)
    for s in range(16):
        from_ref = before_ref if s < 8 else spread_ref
        top = from_ref[s % 8, 0:H, :]
        bottom = from_ref[s % 8, 64 - H : 64, :]
        a_ref[s] = pick(odd, edge, top, bottom)
        b_ref[s] = pick(odd, edge, bottom, top)
    for m in range(2):
        value_ref[m : m + 1, :] = pick(
            gz, (1, value.shape[1]), value[8 * m + 3 : 8 * m + 4, :], value[8 * m + 2 : 8 * m + 3, :]
        )


def last_relax(
    n_col, me_ref, full_ref, before_ref, spread_ref, a_in, b_in, keep_ref, out_ref, force, spare, other, later
):
    row, _, gz = place(me_ref, n_col)
    odd = lax.rem(row, 2)
    weight = full_ref.at[2]
    edge = (H, 256)
    for s in range(16):
        m, z = s % 8 // 4, s % 4
        into, own = (force, before_ref) if s < 8 else (later, spread_ref)
        into[m, z, 0:H, :] = pick(odd, edge, a_in[s], b_in[s]) * weight[z, 0:H]
        into[m, z, H : H + 64, :] = own[4 * m + z] * weight[z, H : H + 64]
        into[m, z, H + 64 : 2 * H + 64, :] = pick(odd, edge, b_in[s], a_in[s]) * weight[z, H + 64 : 2 * H + 64]
    sweep(force, spare, force, weight)
    sweep(spare, other, force, weight)
    sweep(other, spare, force, weight)
    for m in range(2):
        for z in range(4):
            later[m, z] = later[m, z] - (RELAX * spare[m, z]) * weight[z]
    sweep(spare, other, later, weight)
    sweep(other, spare, later, weight)
    sweep(spare, other, later, weight)
    sweep(other, spare, later, weight)
    for m in range(2):
        for k in range(2):
            out_ref[m, k] = keep_ref[m, k] + spare[m, 2 * gz + k, H : H + 64, 0:128]


SMEM = pl.BlockSpec(memory_space=pltpu.SMEM)
VMEM = pl.BlockSpec(memory_space=pltpu.VMEM)


def size_of(shape):
    return functools.reduce(lambda a, b: a * b, shape)


def run(body, name, outs, args, scratch=(), flops=0, scalars=1):
    moved = sum(a.size * 4 for a in args) + sum(4 * size_of(o) for o in outs)
    return pl.pallas_call(
        body,
        name=name,
        out_shape=[jax.ShapeDtypeStruct(o, F32) for o in outs],
        in_specs=[SMEM] * scalars + [VMEM] * (len(args) - scalars),
        out_specs=[VMEM] * len(outs),
        scratch_shapes=[pltpu.VMEM(s, F32) for s in scratch],
        compiler_params=pltpu.CompilerParams(vmem_limit_bytes=20 << 20),
        cost_estimate=pl.CostEstimate(flops=flops, bytes_accessed=moved, transcendentals=0),
    )(*args)


def on_device(n_row, n_col, source, cell_class, coeff_table, owner_cell, node_pos, node_weight):
    nodes = owner_cell.shape[0]
    blocks = 2 * n_col
    me = lax.axis_index(("row", "col", "gz")).reshape(1)

    def swaps(axis, size, a, b):
        first = [(i, i ^ 1) for i in range(size)]
        second = [(i + 1, i + 2) for i in range(0, size - 2, 2)]
        second = second + [(j, i) for i, j in second]
        return lax.ppermute(a, axis, first), lax.ppermute(b, axis, second)

    packed, info = run(
        prepare,
        "prepare",
        [(3, 2, 64, 128), (8, nodes)],
        [me, coeff_table, source, cell_class, owner_cell[None, :], node_pos, node_weight[None, :]],
        scalars=2,
    )
    other = lax.ppermute(packed, "gz", [(0, 1), (1, 0)])
    a, b = run(functools.partial(col_pack, n_col), "col_pack", [(64, 128)] * 2, [me, packed, other])
    a, b = swaps("col", n_col, a, b)
    ext, a, b, told = run(
        functools.partial(row_pack, n_col),
        "row_pack",
        [(12, 64, 256), (12, H, 256), (12, H, 256), (blocks, 8, nodes)],
        [me, packed, other, a, b, info],
    )
    a, b = swaps("row", n_row, a, b)
    target = lax.all_to_all(told, ("col", "gz"), 0, 0)

    field = (2, 4, 64 + 2 * H, 256)
    full, first, sent = run(
        functools.partial(first_relax, n_col),
        "first_relax",
        [(3, 4, 64 + 2 * H, 256), field, (n_row, 8, nodes)],
        [me, ext, a, b, info],
        [field] * 2,
    )
    heard = lax.all_to_all(sent, "row", 0, 0)
    keep, kept = run(
        functools.partial(carry_relax, n_col),
        "carry_relax",
        [(2, 2, 64, 128), (2, nodes)],
        [me, full, first, info],
        [field] * 3,
        flops=40 * size_of(field),
    )

    everything = lambda shape: pl.BlockSpec(shape, lambda i: (0,) * len(shape))
    work = n_row * blocks * nodes * nodes
    sums = [pltpu.VMEM((2, blocks, 8, nodes), F32), pltpu.VMEM((2, blocks + 8, nodes), F32)]
    pairs, partial = pl.pallas_call(
        functools.partial(build_apply, n_col, n_row),
        name="build_apply",
        grid=(n_row,),
        out_shape=[
            jax.ShapeDtypeStruct((n_row, nodes, blocks * nodes), F32),
            jax.ShapeDtypeStruct((blocks, 16, nodes), F32),
        ],
        in_specs=[SMEM, everything((n_row, 8, nodes)), everything((blocks, 8, nodes))],
        out_specs=[
            pl.BlockSpec((1, nodes, blocks * nodes), lambda i: (i, 0, 0)),
            everything((blocks, 16, nodes)),
        ],
        scratch_shapes=sums,
        compiler_params=pltpu.CompilerParams(vmem_limit_bytes=16 << 20),
        cost_estimate=pl.CostEstimate(flops=18 * work, bytes_accessed=4 * work, transcendentals=work),
    )(me, heard, target)
    partial = lax.all_to_all(partial, ("col", "gz"), 0, 0)
    before, sent = run(
        functools.partial(respond, n_col, n_row),
        "respond",
        [(8, 64, 256), (n_row, 8, nodes)],
        [me, partial, target, full, heard, kept],
        [field] * 3,
    )
    again = lax.all_to_all(sent, "row", 0, 0)
    group = 2
    partial = pl.pallas_call(
        functools.partial(reapply, n_col, n_row // group),
        name="reapply",
        grid=(n_row // group,),
        out_shape=jax.ShapeDtypeStruct((blocks, 16, nodes), F32),
        in_specs=[
            SMEM,
            everything((n_row, 8, nodes)),
            everything((n_row, 8, nodes)),
            pl.BlockSpec((group, nodes, blocks * nodes), lambda i: (i, 0, 0)),
        ],
        out_specs=everything((blocks, 16, nodes)),
        scratch_shapes=sums + [pltpu.VMEM((n_row, 8, nodes), F32)],
        compiler_params=pltpu.CompilerParams(vmem_limit_bytes=20 << 20),
        cost_estimate=pl.CostEstimate(flops=4 * work, bytes_accessed=4 * work, transcendentals=0),
    )(me, again, heard, pairs)
    partial = lax.all_to_all(partial, ("col", "gz"), 0, 0)
    spread, a, b, values = run(
        functools.partial(last_spread, n_col),
        "last_spread",
        [(8, 64, 256), (16, H, 256), (16, H, 256), (2, nodes)],
        [me, partial, target, before],
    )
    a, b = swaps("row", n_row, a, b)
    (potential,) = run(
        functools.partial(last_relax, n_col),
        "last_relax",
        [(2, 2, 64, 128)],
        [me, full, before, spread, a, b, keep],
        [field] * 4,
    )
    return potential, values


def solution(mesh):
    return jax.shard_map(
        functools.partial(on_device, mesh.shape["row"], mesh.shape["col"]),
        mesh=mesh,
        in_specs=(
            P(None, "gz", "row", "col"),
            P("gz", "row", "col"),
            P(),
            P(("row", "col", "gz")),
            P(None, ("row", "col", "gz")),
            P(("row", "col", "gz")),
        ),
        out_specs=(P(None, "gz", "row", "col"), P(None, ("row", "col", "gz"))),
        check_vma=False,
    )
```

```python
import functools

import jax
import jax.numpy as jnp
from jax import lax
from jax.experimental import pallas as pl
from jax.experimental.pallas import tpu as pltpu
from jax.sharding import PartitionSpec as P

SWEEPS = 4
OMEGA = 0.8
RELAX = 0.5
SOFTEN = 0.01
H = 8
HIGH = lax.Precision.HIGHEST
F32 = jnp.float32


def iota(shape, axis):
    return lax.broadcasted_iota(jnp.int32, shape, axis)


def pick(flag, shape, yes, no):
    return jnp.where(jnp.full(shape, flag, jnp.int32) == 1, yes, no)


def place(me_ref, n_col):
    me = me_ref[0]
    gz = lax.rem(me, 2)
    col = lax.rem(me // 2, n_col)
    row = me // (2 * n_col)
    return row, col, gz


def layer_of(own_ref, other_ref, kind, z, gz, shape):
    mine = pick(gz, shape, 1, 0) == z // 2
    return jnp.where(mine, own_ref[kind, z % 2], other_ref[kind, z % 2])


def col_pack(n_col, me_ref, own_ref, other_ref, a_ref, b_ref):
    _, col, gz = place(me_ref, n_col)
    shape = own_ref.shape[2:]
    lane = iota(shape, 1)
    left = jnp.zeros(shape, F32)
    right = jnp.zeros(shape, F32)
    for s in range(12):
        cell = layer_of(own_ref, other_ref, s // 4, s % 4, gz, shape)
        here = (lane >= 8 * s) & (lane < 8 * s + 8)
        low = pltpu.roll(cell, 8 * s, 1) if s else cell
        left = jnp.where(here, low, left)
        right = jnp.where(here, pltpu.roll(cell, 8 * s + 8, 1), right)
    odd = lax.rem(col, 2)
    a_ref[...] = pick(odd, shape, left, right)
    b_ref[...] = pick(odd, shape, right, left)


def edge_row(from_ref, s, gz):
    rows, lanes = from_ref.shape[1:]
    return pick(gz, (H, lanes), from_ref[s, rows - H : rows, :], from_ref[s, 0:H, :])


def halo_rows(came_ref, handed_ref, s, gz):
    came, handed = came_ref[s], handed_ref[s]
    return pick(gz, came.shape, handed, came), pick(gz, came.shape, came, handed)


def row_pack(n_col, me_ref, own_ref, other_ref, a_in, b_in, ext_ref, edge_ref):
    _, col, gz = place(me_ref, n_col)
    shape = own_ref.shape[2:]
    rows, lanes = shape
    lane = iota(shape, 1)
    odd_col = lax.rem(col, 2)
    from_right = pick(odd_col, shape, b_in[...], a_in[...])
    from_left = pick(odd_col, shape, a_in[...], b_in[...])
    for s in range(12):
        cell = layer_of(own_ref, other_ref, s // 4, s % 4, gz, shape)
        low = pltpu.roll(from_right, lanes - 8 * s, 1) if s else from_right
        high = pltpu.roll(from_left, lanes - 8 - 8 * s, 1)
        side = jnp.where(lane < 8, low, jnp.where(lane >= lanes - 8, high, 0.0))
        ext_ref[s, :, 0:lanes] = cell
        ext_ref[s, :, lanes : 2 * lanes] = side
        edge_ref[s] = edge_row(ext_ref, s, gz)


def sweep(now_ref, next_ref, force_ref, weight_ref):
    rows, lanes = now_ref.shape[2:]

    def image(m, carry):
        for z in range(4):
            cell = now_ref[m, z]
            beside = pltpu.roll(cell, 1, 0) + pltpu.roll(cell, rows - 1, 0)
            beside = beside + (pltpu.roll(cell, 1, 1) + pltpu.roll(cell, lanes - 1, 1))
            if z > 0:
                beside = beside + now_ref[m, z - 1]
            if z < 3:
                beside = beside + now_ref[m, z + 1]
            next_ref[m, z] = (1.0 - OMEGA) * cell + (force_ref[m, z] + weight_ref[z] * beside)
        return carry

    lax.fori_loop(0, now_ref.shape[0], image, 0)


def trace_of(rows, owner, first_row):
    span = rows.shape[0] // 2
    nodes = owner.shape[1]
    line = iota((2 * span, nodes), 0)
    line = line + first_row + jnp.where(line >= span, 64 - span, 0)
    at_row = jnp.where(line == owner // 128, 1.0, 0.0).astype(F32)
    at_lane = iota((128, nodes), 0) == lax.rem(owner, 128)
    found = lax.dot_general(rows, at_row, (((0,), (0,)), ((), ())), precision=HIGH, preferred_element_type=F32)
    return jnp.sum(jnp.where(at_lane, found, 0.0), axis=0, keepdims=True)


def two_layers(field_ref, m, gz, start, size):
    return jnp.concatenate([field_ref[m, 2 * gz + k, start : start + size, 0:128] for k in range(2)], 0)


def prepare(
    table_hbm, source_hbm, class_hbm, owner_hbm, pos_hbm, node_hbm, pack_ref, told_ref,
    table, level_ref, owner_ref, pos_ref, node_ref, sems,
):
    moves = [
        (class_hbm, level_ref),
        (table_hbm, table),
        (owner_hbm, owner_ref),
        (pos_hbm, pos_ref),
        (node_hbm, node_ref),
        (source_hbm, pack_ref.at[0:2]),
    ]
    copies = [pltpu.make_async_copy(a, b, sems.at[k]) for k, (a, b) in enumerate(moves)]
    for copy in copies:
        copy.start()
    for copy in copies:
        copy.wait()
    for k in range(2):
        level = level_ref[k]
        found = jnp.zeros(level.shape, F32)
        for n in range(table.shape[0]):
            found = jnp.where(level == n, table[n], found)
        pack_ref[2, k] = OMEGA / (6.0 + found)
    told_ref[0] = jnp.zeros(told_ref.shape[1:], F32)
    told_ref[0, 2:5, :] = pos_ref[...]
    told_ref[0, 5:6, :] = owner_ref[...].astype(F32)
    told_ref[0, 6:7, :] = node_ref[...]
    for k in range(1, told_ref.shape[0]):
        told_ref[k] = told_ref[0]


def stage(own_ref, out_ref):
    out_ref[...] = own_ref[...]


def first_relax(n_col, me_ref, ext_ref, a_in, b_in, target_ref, full_ref, first_ref, sent_ref, force, spare):
    _, col, gz = place(me_ref, n_col)
    for s in range(12):
        top, bottom = halo_rows(a_in, b_in, s, gz)
        full_ref[s // 4, s % 4, 0:H, :] = top
        full_ref[s // 4, s % 4, H : H + 64, :] = ext_ref[s]
        full_ref[s // 4, s % 4, H + 64 : 2 * H + 64, :] = bottom
    weight = full_ref.at[2]
    for m in range(2):
        for z in range(4):
            force[m, z] = full_ref[m, z] * weight[z]
    sweep(force, first_ref, force, weight)
    sweep(first_ref, spare, force, weight)
    sweep(spare, first_ref, force, weight)
    info = target_ref[2 * col + gz]
    owner = info[5:6, :].astype(jnp.int32)
    line = iota(info.shape, 0)
    for m in range(2):
        info = jnp.where(line == m, trace_of(two_layers(first_ref, m, gz, H, 64), owner, 0), info)
    for k in range(sent_ref.shape[0]):
        sent_ref[k] = info


def carry_relax(n_col, me_ref, full_ref, first_ref, target_ref, keep_ref, trace_ref, force, spare, other):
    _, col, gz = place(me_ref, n_col)
    weight = full_ref.at[2]
    for m in range(2):
        for z in range(4):
            force[m, z] = (full_ref[m, z] - RELAX * first_ref[m, z]) * weight[z]
    sweep(first_ref, spare, force, weight)
    sweep(spare, other, force, weight)
    sweep(other, spare, force, weight)
    sweep(spare, other, force, weight)
    owner = target_ref[2 * col + gz, 5:6, :].astype(jnp.int32)
    for m in range(2):
        for k in range(2):
            keep_ref[m, k] = other[m, 2 * gz + k, H : H + 64, 0:128]
        trace_ref[m : m + 1, :] = trace_of(two_layers(other, m, gz, H, 64), owner, 0)


def columns(rows, count):
    nodes = rows.shape[1]
    return [jnp.broadcast_to(rows[k : k + 1, :], (nodes, nodes)).T for k in range(count)]


def finish_apply(n_col, col, gz, acc, lined, own, out_ref):
    lined[...] = jnp.zeros_like(lined)
    for t in range(2 * n_col):
        mine = jnp.where(2 * col + gz == t, -0.5, 0.0).astype(F32)
        for m in range(2):
            whole = jnp.sum(acc[m, t], axis=0, keepdims=True)
            lined[m, t + 2 : t + 3, :] = whole + mine * own[m : m + 1, :]
    for c in range(n_col):
        for m in range(2):
            near = lined[m, 2 * c : 2 * c + 8, :]
            out_ref[2 * c, 8 * m : 8 * m + 8, :] = near
            out_ref[2 * c + 1, 8 * m : 8 * m + 8, :] = near


def build_apply(n_col, n_row, me_ref, heard_ref, target_ref, _, pair_ref, out_ref, acc, lined):
    step = pl.program_id(0)
    row, col, gz = place(me_ref, n_col)
    nodes = heard_ref.shape[2]

    @pl.when(step == 0)
    def _():
        acc[...] = jnp.zeros_like(acc)

    heard = heard_ref[step]
    at = columns(heard[2:5, :], 3)
    by = columns(heard[0:2, :] * heard[6:7, :], 2)
    for t in range(target_ref.shape[0]):
        dx = target_ref[t, 2:3, :] - at[0]
        dy = target_ref[t, 3:4, :] - at[1]
        dz = target_ref[t, 4:5, :] - at[2]
        inverse = lax.rsqrt(dx * dx + dy * dy + (dz * dz + SOFTEN))
        pair = dz * inverse * (inverse * inverse)
        pair_ref[0, :, t * nodes : (t + 1) * nodes] = pair
        for m in range(2):
            acc[m, t] = acc[m, t] + jnp.sum((pair * by[m]).reshape(nodes // 8, 8, nodes), axis=0)

    @pl.when(step == n_row - 1)
    def _():
        finish_apply(n_col, col, gz, acc, lined, heard_ref[row], out_ref)


def reapply(n_col, steps, me_ref, heard_ref, info_ref, pair_ref, out_ref, acc, lined, trace):
    step = pl.program_id(0)
    row, col, gz = place(me_ref, n_col)
    nodes = heard_ref.shape[2]
    n_row = heard_ref.shape[0]

    @pl.when(step == 0)
    def _():
        acc[...] = jnp.zeros_like(acc)
        for k in range(n_row):
            whole = heard_ref[k, 0:2, :]
            if k + 1 < n_row:
                whole = whole + heard_ref[k + 1, 2:4, :]
            if k > 0:
                whole = whole + heard_ref[k - 1, 4:6, :]
            trace[k, 0:2, :] = whole
            trace[k, 2:4, :] = whole * info_ref[k, 6:7, :]

    for k in range(pair_ref.shape[0]):
        by = columns(trace[step * pair_ref.shape[0] + k, 2:4, :], 2)
        for t in range(2 * n_col):
            pair = pair_ref[k, :, t * nodes : (t + 1) * nodes]
            for m in range(2):
                acc[m, t] = acc[m, t] + jnp.sum((pair * by[m]).reshape(nodes // 8, 8, nodes), axis=0)

    @pl.when(step == steps - 1)
    def _():
        finish_apply(n_col, col, gz, acc, lined, trace[row], out_ref)


def spread_nodes(n_col, col, part_ref, target_ref, spread_ref):
    nodes = part_ref.shape[2]
    blocks = 2 * n_col
    value = part_ref[0]
    for k in range(1, blocks):
        value = value + part_ref[k]
    shape = (128, nodes)
    down = iota(shape, 0)
    weighted, lanes = [], []
    for b in range(6):
        at = jnp.clip(2 * col - 2 + b, 0, blocks - 1)
        owner = target_ref[at, 5:6, :].astype(jnp.int32)
        hit = down == owner // 128
        weighted.append(
            jnp.concatenate([jnp.where(hit, value[8 * m + b : 8 * m + b + 1, :], 0.0) for m in range(2)], 0)
        )
        lane = down == lax.rem(owner, 128)
        if b < 2:
            lane = lane & (down >= 128 - H)
        if b > 3:
            lane = lane & (down < H)
        lanes.append(jnp.where(lane, 1.0, 0.0).astype(F32))

    def product(a, b):
        return lax.dot_general(a, b, (((1,), (1,)), ((), ())), precision=HIGH, preferred_element_type=F32)

    for g in range(2):
        own = product(weighted[2 + g], lanes[2 + g])
        side = product(
            jnp.concatenate([weighted[g], weighted[4 + g]], 1), jnp.concatenate([lanes[g], lanes[4 + g]], 1)
        )
        for m in range(2):
            for k in range(2):
                start = 128 * m + 64 * k
                spread_ref[4 * m + 2 * g + k, :, 0:128] = own[start : start + 64]
                spread_ref[4 * m + 2 * g + k, :, 128:256] = side[start : start + 64]
    return value


def respond(
    n_col, n_row, me_ref, part_ref, target_ref, full_ref, heard_ref, kept_ref,
    spread_ref, sent_ref, force, spare, other,
):
    row, col, gz = place(me_ref, n_col)
    weight = full_ref.at[2]
    spread_nodes(n_col, col, part_ref, target_ref, spread_ref)
    empty = jnp.zeros((H, 256), F32)
    for m in range(2):
        for z in range(4):
            force[m, z, 0:H, :] = empty
            force[m, z, H : H + 64, :] = spread_ref[4 * m + z] * weight[z, H : H + 64]
            force[m, z, H + 64 : 2 * H + 64, :] = empty
    sweep(force, spare, force, weight)
    sweep(spare, other, force, weight)
    sweep(other, spare, force, weight)
    for m in range(2):
        for z in range(4):
            force[m, z] = (-RELAX * spare[m, z]) * weight[z]
    sweep(force, other, force, weight)
    sweep(other, spare, force, weight)
    sweep(spare, other, force, weight)
    own = heard_ref[row, 5:6, :].astype(jnp.int32)
    above = heard_ref[jnp.maximum(row - 1, 0), 5:6, :].astype(jnp.int32)
    below = heard_ref[jnp.minimum(row + 1, n_row - 1), 5:6, :].astype(jnp.int32)
    line = iota((8, own.shape[1]), 0)
    sent = jnp.zeros((8, own.shape[1]), F32)
    for m in range(2):
        here = trace_of(two_layers(other, m, gz, H, 64), own, 0) + kept_ref[m : m + 1, :]
        sent = jnp.where(line == m, here, sent)
        sent = jnp.where(line == 2 + m, trace_of(two_layers(other, m, gz, 0, H), above, 64 - H), sent)
        sent = jnp.where(line == 4 + m, trace_of(two_layers(other, m, gz, H + 64, H), below, 0), sent)
    for k in range(sent_ref.shape[0]):
        sent_ref[k] = sent


def last_spread(n_col, me_ref, part_ref, target_ref, before_ref, spread_ref, edge_ref, value_ref):
    _, col, gz = place(me_ref, n_col)
    value = spread_nodes(n_col, col, part_ref, target_ref, spread_ref)
    for s in range(16):
        edge_ref[s] = edge_row(before_ref if s < 8 else spread_ref, s % 8, gz)
    for m in range(2):
        value_ref[m : m + 1, :] = pick(
            gz, (1, value.shape[1]), value[8 * m + 3 : 8 * m + 4, :], value[8 * m + 2 : 8 * m + 3, :]
        )


def last_relax(
    n_col, me_ref, full_ref, before_ref, spread_ref, a_in, b_in, keep_ref, out_ref, force, spare, other, later
):
    _, _, gz = place(me_ref, n_col)
    weight = full_ref.at[2]
    for s in range(16):
        m, z = s % 8 // 4, s % 4
        into, own = (force, before_ref) if s < 8 else (later, spread_ref)
        top, bottom = halo_rows(a_in, b_in, s, gz)
        into[m, z, 0:H, :] = top * weight[z, 0:H]
        into[m, z, H : H + 64, :] = own[4 * m + z] * weight[z, H : H + 64]
        into[m, z, H + 64 : 2 * H + 64, :] = bottom * weight[z, H + 64 : 2 * H + 64]
    sweep(force, spare, force, weight)
    sweep(spare, other, force, weight)
    sweep(other, spare, force, weight)
    for m in range(2):
        for z in range(4):
            later[m, z] = later[m, z] - (RELAX * spare[m, z]) * weight[z]
    sweep(spare, other, later, weight)
    sweep(other, spare, later, weight)
    sweep(spare, other, later, weight)
    sweep(other, spare, later, weight)
    for m in range(2):
        for k in range(2):
            out_ref[m, k] = keep_ref[m, k] + spare[m, 2 * gz + k, H : H + 64, 0:128]


SMEM = pl.BlockSpec(memory_space=pltpu.SMEM)
VMEM = pl.BlockSpec(memory_space=pltpu.VMEM)


def size_of(shape):
    return functools.reduce(lambda a, b: a * b, shape)


def run(body, name, outs, args, scratch=(), flops=0, scalars=1):
    moved = sum(a.size * 4 for a in args) + sum(4 * size_of(o) for o in outs)
    return pl.pallas_call(
        body,
        name=name,
        out_shape=[jax.ShapeDtypeStruct(o, F32) for o in outs],
        in_specs=[SMEM] * scalars + [VMEM] * (len(args) - scalars),
        out_specs=[VMEM] * len(outs),
        scratch_shapes=[pltpu.VMEM(s, F32) for s in scratch],
        compiler_params=pltpu.CompilerParams(vmem_limit_bytes=20 << 20),
        cost_estimate=pl.CostEstimate(flops=flops, bytes_accessed=moved, transcendentals=0),
    )(*args)


def on_device(n_row, n_col, source, cell_class, coeff_table, owner_cell, node_pos, node_weight):
    nodes = owner_cell.shape[0]
    blocks = 2 * n_col
    me = lax.axis_index(("row", "col", "gz")).reshape(1)

    def swaps(axis, size, a, b):
        first = [(i, i ^ 1) for i in range(size)]
        second = [(i + 1, i + 2) for i in range(0, size - 2, 2)]
        second = second + [(j, i) for i, j in second]
        return lax.ppermute(a, axis, first), lax.ppermute(b, axis, second)

    def beside(edge):
        came = [(2 * i + 1, 2 * i + 2) for i in range(n_row - 1)]
        came = lax.ppermute(edge, ("row", "gz"), came + [(j, i) for i, j in came])
        return came, lax.ppermute(came, "gz", [(0, 1), (1, 0)])

    packed, told = pl.pallas_call(
        prepare,
        name="prepare",
        out_shape=[jax.ShapeDtypeStruct(o, F32) for o in ((3, 2, 64, 128), (blocks, 8, nodes))],
        in_specs=[pl.BlockSpec(memory_space=pl.ANY)] * 6,
        out_specs=[VMEM] * 2,
        scratch_shapes=[
            pltpu.SMEM(coeff_table.shape, F32),
            pltpu.VMEM(cell_class.shape, jnp.int32),
            pltpu.VMEM((1, nodes), jnp.int32),
            pltpu.VMEM((3, nodes), F32),
            pltpu.VMEM((1, nodes), F32),
            pltpu.SemaphoreType.DMA((6,)),
        ],
        compiler_params=pltpu.CompilerParams(vmem_limit_bytes=60 << 20),
    )(coeff_table, source, cell_class, owner_cell[None, :], node_pos, node_weight[None, :])
    other = lax.ppermute(packed, "gz", [(0, 1), (1, 0)])
    target = lax.all_to_all(told, ("col", "gz"), 0, 0)
    (packed,) = run(stage, "stage", [packed.shape], [packed], scalars=0)
    a, b = run(functools.partial(col_pack, n_col), "col_pack", [(64, 128)] * 2, [me, packed, other])
    a, b = swaps("col", n_col, a, b)
    ext, edge = run(
        functools.partial(row_pack, n_col),
        "row_pack",
        [(12, 64, 256), (12, H, 256)],
        [me, packed, other, a, b],
    )
    a, b = beside(edge)

    field = (2, 4, 64 + 2 * H, 256)
    full, first, sent = run(
        functools.partial(first_relax, n_col),
        "first_relax",
        [(3, 4, 64 + 2 * H, 256), field, (n_row, 8, nodes)],
        [me, ext, a, b, target],
        [field] * 2,
    )
    heard = lax.all_to_all(sent, "row", 0, 0)
    keep, kept = run(
        functools.partial(carry_relax, n_col),
        "carry_relax",
        [(2, 2, 64, 128), (2, nodes)],
        [me, full, first, target],
        [field] * 3,
        flops=40 * size_of(field),
    )

    everything = lambda shape: pl.BlockSpec(shape, lambda i: (0,) * len(shape))
    work = n_row * blocks * nodes * nodes
    sums = [pltpu.VMEM((2, blocks, 8, nodes), F32), pltpu.VMEM((2, blocks + 8, nodes), F32)]
    pairs, partial = pl.pallas_call(
        functools.partial(build_apply, n_col, n_row),
        name="build_apply",
        grid=(n_row,),
        out_shape=[
            jax.ShapeDtypeStruct((n_row, nodes, blocks * nodes), F32),
            jax.ShapeDtypeStruct((blocks, 16, nodes), F32),
        ],
        in_specs=[SMEM, everything((n_row, 8, nodes)), everything((blocks, 8, nodes)), everything((2, nodes))],
        out_specs=[
            pl.BlockSpec((1, nodes, blocks * nodes), lambda i: (i, 0, 0)),
            everything((blocks, 16, nodes)),
        ],
        scratch_shapes=sums,
        compiler_params=pltpu.CompilerParams(vmem_limit_bytes=16 << 20),
        cost_estimate=pl.CostEstimate(flops=18 * work, bytes_accessed=4 * work, transcendentals=work),
    )(me, heard, target, kept)
    partial = lax.all_to_all(partial, ("col", "gz"), 0, 0)
    before, sent = run(
        functools.partial(respond, n_col, n_row),
        "respond",
        [(8, 64, 256), (n_row, 8, nodes)],
        [me, partial, target, full, heard, kept],
        [field] * 3,
    )
    again = lax.all_to_all(sent, "row", 0, 0)
    group = 2
    partial = pl.pallas_call(
        functools.partial(reapply, n_col, n_row // group),
        name="reapply",
        grid=(n_row // group,),
        out_shape=jax.ShapeDtypeStruct((blocks, 16, nodes), F32),
        in_specs=[
            SMEM,
            everything((n_row, 8, nodes)),
            everything((n_row, 8, nodes)),
            pl.BlockSpec((group, nodes, blocks * nodes), lambda i: (i, 0, 0)),
        ],
        out_specs=everything((blocks, 16, nodes)),
        scratch_shapes=sums + [pltpu.VMEM((n_row, 8, nodes), F32)],
        compiler_params=pltpu.CompilerParams(vmem_limit_bytes=20 << 20),
        cost_estimate=pl.CostEstimate(flops=4 * work, bytes_accessed=4 * work, transcendentals=0),
    )(me, again, heard, pairs)
    partial = lax.all_to_all(partial, ("col", "gz"), 0, 0)
    spread, edge, values = run(
        functools.partial(last_spread, n_col),
        "last_spread",
        [(8, 64, 256), (16, H, 256), (2, nodes)],
        [me, partial, target, before],
    )
    a, b = beside(edge)
    (potential,) = run(
        functools.partial(last_relax, n_col),
        "last_relax",
        [(2, 2, 64, 128)],
        [me, full, before, spread, a, b, keep],
        [field] * 4,
    )
    return potential, values


def solution(mesh):
    return jax.shard_map(
        functools.partial(on_device, mesh.shape["row"], mesh.shape["col"]),
        mesh=mesh,
        in_specs=(
            P(None, "gz", "row", "col"),
            P("gz", "row", "col"),
            P(),
            P(("row", "col", "gz")),
            P(None, ("row", "col", "gz")),
            P(("row", "col", "gz")),
        ),
        out_specs=(P(None, "gz", "row", "col"), P(None, ("row", "col", "gz"))),
        check_vma=False,
    )
```

```python
import functools

import jax
import jax.numpy as jnp
from jax import lax
from jax.experimental import pallas as pl
from jax.experimental.pallas import tpu as pltpu
from jax.sharding import PartitionSpec as P

SWEEPS = 4
OMEGA = 0.8
RELAX = 0.5
SOFTEN = 0.01
H = 8
HIGH = lax.Precision.HIGHEST
F32 = jnp.float32


def iota(shape, axis):
    return lax.broadcasted_iota(jnp.int32, shape, axis)


def pick(flag, shape, yes, no):
    return jnp.where(jnp.full(shape, flag, jnp.int32) == 1, yes, no)


def place(me_ref, n_col):
    me = me_ref[0]
    gz = lax.rem(me, 2)
    col = lax.rem(me // 2, n_col)
    row = me // (2 * n_col)
    return row, col, gz


def layer_of(own_ref, other_ref, kind, z, gz, shape):
    mine = pick(gz, shape, 1, 0) == z // 2
    return jnp.where(mine, own_ref[kind, z % 2], other_ref[kind, z % 2])


def col_pack(n_col, me_ref, own_ref, other_ref, a_ref, b_ref):
    _, col, gz = place(me_ref, n_col)
    shape = own_ref.shape[2:]
    lane = iota(shape, 1)
    left = jnp.zeros(shape, F32)
    right = jnp.zeros(shape, F32)
    for s in range(12):
        cell = layer_of(own_ref, other_ref, s // 4, s % 4, gz, shape)
        here = (lane >= 8 * s) & (lane < 8 * s + 8)
        low = pltpu.roll(cell, 8 * s, 1) if s else cell
        left = jnp.where(here, low, left)
        right = jnp.where(here, pltpu.roll(cell, 8 * s + 8, 1), right)
    odd = lax.rem(col, 2)
    a_ref[...] = pick(odd, shape, left, right)
    b_ref[...] = pick(odd, shape, right, left)


def edge_row(from_ref, s, gz):
    rows, lanes = from_ref.shape[1:]
    return pick(gz, (H, lanes), from_ref[s, rows - H : rows, :], from_ref[s, 0:H, :])


def tuck(side, s, into):
    lane = iota(side.shape, 1)
    moved = pltpu.roll(side, (16 * s + 8) % 128, 1)
    return jnp.where((lane >= 16 * s) & (lane < 16 * s + 16), moved, into)


def untuck(tile, s):
    lane = iota(tile.shape, 1)
    moved = pltpu.roll(tile, (128 - 16 * s - 8) % 128, 1)
    return jnp.where((lane < 8) | (lane >= 120), moved, 0.0)


def write_edges(edge_ref, start, from_ref, count, gz):
    for first in range(0, count, 8):
        side = jnp.zeros((H, 128), F32)
        for s in range(first, min(first + 8, count)):
            edge = edge_row(from_ref, s, gz)
            edge_ref[start + s] = edge[:, 0:128]
            side = tuck(edge[:, 128:256], s - first, side)
        edge_ref[start + count + first // 8] = side


def read_edge(ref, start, s, count):
    return jnp.concatenate([ref[start + s], untuck(ref[start + count + s // 8], s % 8)], 1)


def near_half(sent_gz):
    line = iota((H, 128), 0)
    return (line // 4) == jnp.full((H, 128), sent_gz, jnp.int32)


def halo_rows(came, handed, gz):
    return pick(gz, came.shape, handed, came), pick(gz, came.shape, came, handed)


def row_pack(n_col, me_ref, own_ref, other_ref, a_in, b_in, ext_ref, edge_ref):
    _, col, gz = place(me_ref, n_col)
    shape = own_ref.shape[2:]
    rows, lanes = shape
    lane = iota(shape, 1)
    odd_col = lax.rem(col, 2)
    from_right = pick(odd_col, shape, b_in[...], a_in[...])
    from_left = pick(odd_col, shape, a_in[...], b_in[...])
    for s in range(12):
        cell = layer_of(own_ref, other_ref, s // 4, s % 4, gz, shape)
        low = pltpu.roll(from_right, lanes - 8 * s, 1) if s else from_right
        high = pltpu.roll(from_left, lanes - 8 - 8 * s, 1)
        side = jnp.where(lane < 8, low, jnp.where(lane >= lanes - 8, high, 0.0))
        ext_ref[s, :, 0:lanes] = cell
        ext_ref[s, :, lanes : 2 * lanes] = side
    write_edges(edge_ref, 0, ext_ref, 12, gz)


def sweep(now_ref, next_ref, force_ref, weight_ref):
    rows, lanes = now_ref.shape[2:]

    def image(m, carry):
        for z in range(4):
            cell = now_ref[m, z]
            beside = pltpu.roll(cell, 1, 0) + pltpu.roll(cell, rows - 1, 0)
            beside = beside + (pltpu.roll(cell, 1, 1) + pltpu.roll(cell, lanes - 1, 1))
            if z > 0:
                beside = beside + now_ref[m, z - 1]
            if z < 3:
                beside = beside + now_ref[m, z + 1]
            next_ref[m, z] = (1.0 - OMEGA) * cell + (force_ref[m, z] + weight_ref[z] * beside)
        return carry

    lax.fori_loop(0, now_ref.shape[0], image, 0)


def trace_of(rows, owner, first_row):
    span = rows.shape[0] // 2
    nodes = owner.shape[1]
    line = iota((2 * span, nodes), 0)
    line = line + first_row + jnp.where(line >= span, 64 - span, 0)
    at_row = jnp.where(line == owner // 128, 1.0, 0.0).astype(F32)
    at_lane = iota((128, nodes), 0) == lax.rem(owner, 128)
    found = lax.dot_general(rows, at_row, (((0,), (0,)), ((), ())), precision=HIGH, preferred_element_type=F32)
    return jnp.sum(jnp.where(at_lane, found, 0.0), axis=0, keepdims=True)


def two_layers(field_ref, m, gz, start, size):
    return jnp.concatenate([field_ref[m, 2 * gz + k, start : start + size, 0:128] for k in range(2)], 0)


def prepare(
    table_hbm, source_hbm, class_hbm, owner_hbm, pos_hbm, node_hbm, pack_ref, told_ref,
    table, level_ref, owner_ref, pos_ref, node_ref, sems,
):
    moves = [
        (class_hbm, level_ref),
        (table_hbm, table),
        (owner_hbm, owner_ref),
        (pos_hbm, pos_ref),
        (node_hbm, node_ref),
        (source_hbm, pack_ref.at[0:2]),
    ]
    copies = [pltpu.make_async_copy(a, b, sems.at[k]) for k, (a, b) in enumerate(moves)]
    for copy in copies:
        copy.start()
    for copy in copies:
        copy.wait()
    for k in range(2):
        level = level_ref[k]
        found = jnp.zeros(level.shape, F32)
        for n in range(table.shape[0]):
            found = jnp.where(level == n, table[n], found)
        pack_ref[2, k] = OMEGA / (6.0 + found)
    told_ref[0] = jnp.zeros(told_ref.shape[1:], F32)
    centred = pos_ref[...] - 0.5
    told_ref[0, 2:5, :] = centred
    told_ref[0, 5:6, :] = owner_ref[...].astype(F32)
    told_ref[0, 6:7, :] = node_ref[...]
    told_ref[0, 7:8, :] = jnp.sum(centred * centred, axis=0, keepdims=True)
    for k in range(1, told_ref.shape[0]):
        told_ref[k] = told_ref[0]


def stage(own_ref, out_ref):
    out_ref[...] = own_ref[...]


def first_relax(n_col, me_ref, ext_ref, a_in, b_in, target_ref, full_ref, first_ref, sent_ref, force, spare):
    _, col, gz = place(me_ref, n_col)
    for s in range(12):
        top, bottom = halo_rows(read_edge(a_in, 0, s, 12), read_edge(b_in, 0, s, 12), gz)
        full_ref[s // 4, s % 4, 0:H, :] = top
        full_ref[s // 4, s % 4, H : H + 64, :] = ext_ref[s]
        full_ref[s // 4, s % 4, H + 64 : 2 * H + 64, :] = bottom
    weight = full_ref.at[2]
    for m in range(2):
        for z in range(4):
            force[m, z] = full_ref[m, z] * weight[z]
    sweep(force, first_ref, force, weight)
    sweep(first_ref, spare, force, weight)
    sweep(spare, first_ref, force, weight)
    info = target_ref[2 * col + gz]
    owner = info[5:6, :].astype(jnp.int32)
    line = iota(info.shape, 0)
    for m in range(2):
        info = jnp.where(line == m, trace_of(two_layers(first_ref, m, gz, H, 64), owner, 0), info)
    for k in range(sent_ref.shape[0]):
        sent_ref[k] = info


def carry_relax(n_col, me_ref, full_ref, first_ref, target_ref, keep_ref, trace_ref, force, spare, other):
    _, col, gz = place(me_ref, n_col)
    weight = full_ref.at[2]
    for m in range(2):
        for z in range(4):
            force[m, z] = (full_ref[m, z] - RELAX * first_ref[m, z]) * weight[z]
    sweep(first_ref, spare, force, weight)
    sweep(spare, other, force, weight)
    sweep(other, spare, force, weight)
    sweep(spare, other, force, weight)
    owner = target_ref[2 * col + gz, 5:6, :].astype(jnp.int32)
    for m in range(2):
        for k in range(2):
            keep_ref[m, k] = other[m, 2 * gz + k, H : H + 64, 0:128]
        trace_ref[m : m + 1, :] = trace_of(two_layers(other, m, gz, H, 64), owner, 0)


def columns(rows, count):
    nodes = rows.shape[1]
    return [jnp.broadcast_to(rows[k : k + 1, :], (nodes, nodes)).T for k in range(count)]


def finish_apply(n_col, col, gz, acc, lined, own, out_ref):
    lined[...] = jnp.zeros_like(lined)
    for t in range(2 * n_col):
        mine = jnp.where(2 * col + gz == t, -0.5, 0.0).astype(F32)
        for m in range(2):
            whole = jnp.sum(acc[m, t], axis=0, keepdims=True)
            lined[m, t + 2 : t + 3, :] = whole + mine * own[m : m + 1, :]
    for c in range(n_col):
        for m in range(2):
            near = lined[m, 2 * c : 2 * c + 8, :]
            out_ref[2 * c, 8 * m : 8 * m + 8, :] = near
            out_ref[2 * c + 1, 8 * m : 8 * m + 8, :] = near


def split(x):
    high = x.astype(jnp.bfloat16).astype(F32)
    rest = x - high
    middle = rest.astype(jnp.bfloat16).astype(F32)
    return high, middle, rest - middle


def build_apply(n_col, n_row, me_ref, heard_ref, target_ref, _, pair_ref, out_ref, acc, lined, goal):
    step = pl.program_id(0)
    row, col, gz = place(me_ref, n_col)
    nodes = heard_ref.shape[2]
    blocks = target_ref.shape[0]
    line = iota((8, nodes), 0)
    at_pos = (line >= 2) & (line <= 4)

    @pl.when(step == 0)
    def _():
        acc[...] = jnp.zeros_like(acc)
        for t in range(blocks):
            info = target_ref[t]
            norm = pltpu.roll(info, 1, 0) + SOFTEN
            base = jnp.where(line == 0, norm, jnp.where(at_pos, -2.0 * info, jnp.where(line == 7, 1.0, 0.0)))
            high, middle, low = split(base)
            rows = jnp.concatenate([high, middle, high, low, high, middle], 0)
            goal[:, t * nodes : (t + 1) * nodes] = rows.astype(jnp.bfloat16)

    heard = heard_ref[step]
    base = jnp.where(at_pos | (line == 7), heard, jnp.where(line == 0, 1.0, 0.0))
    high, middle, low = split(base)
    start = jnp.concatenate([high, high, middle, high, low, middle], 0).astype(jnp.bfloat16)
    z_at = columns(heard[4:5, :], 1)[0]
    by = columns(heard[0:2, :] * heard[6:7, :], 2)
    for t in range(0, blocks, 2):
        squares = lax.dot_general(
            start,
            goal[:, t * nodes : (t + 2) * nodes],
            (((0,), (0,)), ((), ())),
            preferred_element_type=F32,
        )
        for k in range(2):
            dz = target_ref[t + k, 4:5, :] - z_at
            inverse = lax.rsqrt(squares[:, k * nodes : (k + 1) * nodes])
            pair = dz * inverse * (inverse * inverse)
            pair_ref[0, :, (t + k) * nodes : (t + k + 1) * nodes] = pair
            for m in range(2):
                acc[m, t + k] = acc[m, t + k] + jnp.sum((pair * by[m]).reshape(nodes // 8, 8, nodes), axis=0)

    @pl.when(step == n_row - 1)
    def _():
        finish_apply(n_col, col, gz, acc, lined, heard_ref[row], out_ref)


def reapply(n_col, steps, me_ref, heard_ref, info_ref, pair_ref, out_ref, acc, lined, trace):
    step = pl.program_id(0)
    row, col, gz = place(me_ref, n_col)
    nodes = heard_ref.shape[2]
    n_row = heard_ref.shape[0]

    @pl.when(step == 0)
    def _():
        acc[...] = jnp.zeros_like(acc)
        for k in range(n_row):
            whole = heard_ref[k, 0:2, :]
            if k + 1 < n_row:
                whole = whole + heard_ref[k + 1, 2:4, :]
            if k > 0:
                whole = whole + heard_ref[k - 1, 4:6, :]
            trace[k, 0:2, :] = whole
            trace[k, 2:4, :] = whole * info_ref[k, 6:7, :]

    for k in range(pair_ref.shape[0]):
        by = columns(trace[step * pair_ref.shape[0] + k, 2:4, :], 2)
        for t in range(2 * n_col):
            pair = pair_ref[k, :, t * nodes : (t + 1) * nodes]
            for m in range(2):
                acc[m, t] = acc[m, t] + jnp.sum((pair * by[m]).reshape(nodes // 8, 8, nodes), axis=0)

    @pl.when(step == steps - 1)
    def _():
        finish_apply(n_col, col, gz, acc, lined, trace[row], out_ref)


def spread_nodes(n_col, col, part_ref, target_ref, spread_ref):
    nodes = part_ref.shape[2]
    blocks = 2 * n_col
    value = part_ref[0]
    for k in range(1, blocks):
        value = value + part_ref[k]
    shape = (128, nodes)
    down = iota(shape, 0)
    weighted, lanes = [], []
    for b in range(6):
        at = jnp.clip(2 * col - 2 + b, 0, blocks - 1)
        owner = target_ref[at, 5:6, :].astype(jnp.int32)
        hit = down == owner // 128
        weighted.append(
            jnp.concatenate([jnp.where(hit, value[8 * m + b : 8 * m + b + 1, :], 0.0) for m in range(2)], 0)
        )
        lane = down == lax.rem(owner, 128)
        if b < 2:
            lane = lane & (down >= 128 - H)
        if b > 3:
            lane = lane & (down < H)
        lanes.append(jnp.where(lane, 1.0, 0.0).astype(F32))

    def product(a, b):
        return lax.dot_general(a, b, (((1,), (1,)), ((), ())), precision=HIGH, preferred_element_type=F32)

    for g in range(2):
        own = product(weighted[2 + g], lanes[2 + g])
        side = product(
            jnp.concatenate([weighted[g], weighted[4 + g]], 1), jnp.concatenate([lanes[g], lanes[4 + g]], 1)
        )
        for m in range(2):
            for k in range(2):
                start = 128 * m + 64 * k
                spread_ref[4 * m + 2 * g + k, :, 0:128] = own[start : start + 64]
                spread_ref[4 * m + 2 * g + k, :, 128:256] = side[start : start + 64]
    return value


def respond(
    n_col, n_row, me_ref, part_ref, target_ref, full_ref, heard_ref, kept_ref,
    spread_ref, sent_ref, second_ref, force, spare, other,
):
    row, col, gz = place(me_ref, n_col)
    weight = full_ref.at[2]
    spread_nodes(n_col, col, part_ref, target_ref, spread_ref)
    empty = jnp.zeros((H, 256), F32)
    for m in range(2):
        for z in range(4):
            force[m, z, 0:H, :] = empty
            force[m, z, H : H + 64, :] = spread_ref[4 * m + z] * weight[z, H : H + 64]
            force[m, z, H + 64 : 2 * H + 64, :] = empty
    sweep(force, spare, force, weight)
    sweep(spare, other, force, weight)
    sweep(other, second_ref, force, weight)
    for m in range(2):
        for z in range(4):
            force[m, z] = (-RELAX * second_ref[m, z]) * weight[z]
    sweep(force, other, force, weight)
    sweep(other, spare, force, weight)
    sweep(spare, other, force, weight)
    own = heard_ref[row, 5:6, :].astype(jnp.int32)
    above = heard_ref[jnp.maximum(row - 1, 0), 5:6, :].astype(jnp.int32)
    below = heard_ref[jnp.minimum(row + 1, n_row - 1), 5:6, :].astype(jnp.int32)
    line = iota((8, own.shape[1]), 0)
    sent = jnp.zeros((8, own.shape[1]), F32)
    for m in range(2):
        here = trace_of(two_layers(other, m, gz, H, 64), own, 0) + kept_ref[m : m + 1, :]
        sent = jnp.where(line == m, here, sent)
        sent = jnp.where(line == 2 + m, trace_of(two_layers(other, m, gz, 0, H), above, 64 - H), sent)
        sent = jnp.where(line == 4 + m, trace_of(two_layers(other, m, gz, H + 64, H), below, 0), sent)
    for k in range(sent_ref.shape[0]):
        sent_ref[k] = sent


def last_spread(n_col, me_ref, part_ref, target_ref, before_ref, spread_ref, edge_ref, value_ref):
    _, col, gz = place(me_ref, n_col)
    value = spread_nodes(n_col, col, part_ref, target_ref, spread_ref)
    write_edges(edge_ref, 0, before_ref, 8, gz)
    near = near_half(gz)
    side = jnp.zeros((H, 128), F32)
    for s in range(0, 8, 2):
        one, two = edge_row(spread_ref, s, gz), edge_row(spread_ref, s + 1, gz)
        edge_ref[9 + s // 2] = jnp.where(near, one[:, 0:128], pltpu.roll(two[:, 0:128], 4, 0))
        side = tuck(one[:, 128:256], s, side)
        side = tuck(two[:, 128:256], s + 1, side)
    edge_ref[13] = side
    for m in range(2):
        value_ref[m : m + 1, :] = pick(
            gz, (1, value.shape[1]), value[8 * m + 3 : 8 * m + 4, :], value[8 * m + 2 : 8 * m + 3, :]
        )


def own_relax(n_col, me_ref, full_ref, second_ref, spread_ref, keep_ref, out_ref, force, spare, other):
    _, _, gz = place(me_ref, n_col)
    weight = full_ref.at[2]
    for m in range(2):
        for z in range(4):
            force[m, z] = (-RELAX * second_ref[m, z]) * weight[z]
            mid = force[m, z, H : H + 64, :]
            force[m, z, H : H + 64, :] = mid + spread_ref[4 * m + z] * weight[z, H : H + 64]
    sweep(second_ref, spare, force, weight)
    sweep(spare, other, force, weight)
    sweep(other, spare, force, weight)
    sweep(spare, other, force, weight)
    for m in range(2):
        for k in range(2):
            out_ref[m, k] = keep_ref[m, k] + other[m, 2 * gz + k, H : H + 64, 0:128]


def last_relax(
    n_col, me_ref, full_ref, came_ref, handed_ref, part_ref, out_ref, weight, force, later, spare, other
):
    _, _, gz = place(me_ref, n_col)
    empty = jnp.zeros((2 * H, 256), F32)
    for z in range(4):
        weight[z, 0 : 2 * H] = full_ref[2, z, 0 : 2 * H]
        weight[z, 2 * H : 4 * H] = full_ref[2, z, 64 : 64 + 2 * H]
    for s in range(8):
        m, z = s // 4, s % 4
        top, bottom = halo_rows(read_edge(came_ref, 0, s, 8), read_edge(handed_ref, 0, s, 8), gz)
        force[m, z, 0:H] = top * weight[z, 0:H]
        force[m, z, H : 3 * H] = empty
        force[m, z, 3 * H : 4 * H] = bottom * weight[z, 3 * H : 4 * H]
        ends = []
        for ref, sender in ((came_ref, 1 - gz), (handed_ref, gz)):
            tile = ref[9 + s // 2]
            main = jnp.where(near_half(sender), pltpu.roll(tile, 4, 0) if s % 2 else tile, 0.0)
            ends.append(jnp.concatenate([main, untuck(ref[13], s)], 1))
        top, bottom = halo_rows(ends[0], ends[1], gz)
        later[m, z, 0:H] = top * weight[z, 0:H]
        later[m, z, H : 3 * H] = empty
        later[m, z, 3 * H : 4 * H] = bottom * weight[z, 3 * H : 4 * H]
    sweep(force, spare, force, weight)
    sweep(spare, other, force, weight)
    sweep(other, spare, force, weight)
    for m in range(2):
        for z in range(4):
            later[m, z] = later[m, z] - (RELAX * spare[m, z]) * weight[z]
    sweep(spare, other, later, weight)
    sweep(other, spare, later, weight)
    sweep(spare, other, later, weight)
    sweep(other, spare, later, weight)
    for m in range(2):
        for k in range(2):
            found = spare.at[m, 2 * gz + k]
            out_ref[m, k, 0:H, :] = part_ref[m, k, 0:H, :] + found[H : 2 * H, 0:128]
            out_ref[m, k, H : 64 - H, :] = part_ref[m, k, H : 64 - H, :]
            out_ref[m, k, 64 - H : 64, :] = part_ref[m, k, 64 - H : 64, :] + found[2 * H : 3 * H, 0:128]


SMEM = pl.BlockSpec(memory_space=pltpu.SMEM)
VMEM = pl.BlockSpec(memory_space=pltpu.VMEM)


def size_of(shape):
    return functools.reduce(lambda a, b: a * b, shape)


def run(body, name, outs, args, scratch=(), flops=0, scalars=1):
    moved = sum(a.size * 4 for a in args) + sum(4 * size_of(o) for o in outs)
    return pl.pallas_call(
        body,
        name=name,
        out_shape=[jax.ShapeDtypeStruct(o, F32) for o in outs],
        in_specs=[SMEM] * scalars + [VMEM] * (len(args) - scalars),
        out_specs=[VMEM] * len(outs),
        scratch_shapes=[pltpu.VMEM(s, F32) for s in scratch],
        compiler_params=pltpu.CompilerParams(vmem_limit_bytes=20 << 20),
        cost_estimate=pl.CostEstimate(flops=flops, bytes_accessed=moved, transcendentals=0),
    )(*args)


def on_device(n_row, n_col, source, cell_class, coeff_table, owner_cell, node_pos, node_weight):
    nodes = owner_cell.shape[0]
    blocks = 2 * n_col
    me = lax.axis_index(("row", "col", "gz")).reshape(1)

    def swaps(axis, size, a, b):
        first = [(i, i ^ 1) for i in range(size)]
        second = [(i + 1, i + 2) for i in range(0, size - 2, 2)]
        second = second + [(j, i) for i, j in second]
        return lax.ppermute(a, axis, first), lax.ppermute(b, axis, second)

    def beside(edge):
        came = [(2 * i + 1, 2 * i + 2) for i in range(n_row - 1)]
        came = lax.ppermute(edge, ("row", "gz"), came + [(j, i) for i, j in came])
        return came, lax.ppermute(came, "gz", [(0, 1), (1, 0)])

    packed, told = pl.pallas_call(
        prepare,
        name="prepare",
        out_shape=[jax.ShapeDtypeStruct(o, F32) for o in ((3, 2, 64, 128), (blocks, 8, nodes))],
        in_specs=[pl.BlockSpec(memory_space=pl.ANY)] * 6,
        out_specs=[VMEM] * 2,
        scratch_shapes=[
            pltpu.SMEM(coeff_table.shape, F32),
            pltpu.VMEM(cell_class.shape, jnp.int32),
            pltpu.VMEM((1, nodes), jnp.int32),
            pltpu.VMEM((3, nodes), F32),
            pltpu.VMEM((1, nodes), F32),
            pltpu.SemaphoreType.DMA((6,)),
        ],
        compiler_params=pltpu.CompilerParams(vmem_limit_bytes=60 << 20),
    )(coeff_table, source, cell_class, owner_cell[None, :], node_pos, node_weight[None, :])
    other = lax.ppermute(packed, "gz", [(0, 1), (1, 0)])
    target = lax.all_to_all(told, ("col", "gz"), 0, 0)
    (packed,) = run(stage, "stage", [packed.shape], [packed], scalars=0)
    a, b = run(functools.partial(col_pack, n_col), "col_pack", [(64, 128)] * 2, [me, packed, other])
    a, b = swaps("col", n_col, a, b)
    ext, edge = run(
        functools.partial(row_pack, n_col),
        "row_pack",
        [(12, 64, 256), (14, H, 128)],
        [me, packed, other, a, b],
    )
    a, b = beside(edge)

    field = (2, 4, 64 + 2 * H, 256)
    full, first, sent = run(
        functools.partial(first_relax, n_col),
        "first_relax",
        [(3, 4, 64 + 2 * H, 256), field, (n_row, 8, nodes)],
        [me, ext, a, b, target],
        [field] * 2,
    )
    heard = lax.all_to_all(sent, "row", 0, 0)
    keep, kept = run(
        functools.partial(carry_relax, n_col),
        "carry_relax",
        [(2, 2, 64, 128), (2, nodes)],
        [me, full, first, target],
        [field] * 3,
        flops=40 * size_of(field),
    )

    everything = lambda shape: pl.BlockSpec(shape, lambda i: (0,) * len(shape))
    work = n_row * blocks * nodes * nodes
    sums = [pltpu.VMEM((2, blocks, 8, nodes), F32), pltpu.VMEM((2, blocks + 8, nodes), F32)]
    pairs, partial = pl.pallas_call(
        functools.partial(build_apply, n_col, n_row),
        name="build_apply",
        grid=(n_row,),
        out_shape=[
            jax.ShapeDtypeStruct((n_row, nodes, blocks * nodes), F32),
            jax.ShapeDtypeStruct((blocks, 16, nodes), F32),
        ],
        in_specs=[SMEM, everything((n_row, 8, nodes)), everything((blocks, 8, nodes)), everything((2, nodes))],
        out_specs=[
            pl.BlockSpec((1, nodes, blocks * nodes), lambda i: (i, 0, 0)),
            everything((blocks, 16, nodes)),
        ],
        scratch_shapes=sums + [pltpu.VMEM((48, blocks * nodes), jnp.bfloat16)],
        compiler_params=pltpu.CompilerParams(vmem_limit_bytes=16 << 20),
        cost_estimate=pl.CostEstimate(flops=18 * work, bytes_accessed=4 * work, transcendentals=work),
    )(me, heard, target, kept)
    partial = lax.all_to_all(partial, ("col", "gz"), 0, 0)
    before, sent, second = run(
        functools.partial(respond, n_col, n_row),
        "respond",
        [(8, 64, 256), (n_row, 8, nodes), field],
        [me, partial, target, full, heard, kept],
        [field] * 3,
    )
    again = lax.all_to_all(sent, "row", 0, 0)
    group = 2
    partial = pl.pallas_call(
        functools.partial(reapply, n_col, n_row // group),
        name="reapply",
        grid=(n_row // group,),
        out_shape=jax.ShapeDtypeStruct((blocks, 16, nodes), F32),
        in_specs=[
            SMEM,
            everything((n_row, 8, nodes)),
            everything((n_row, 8, nodes)),
            pl.BlockSpec((group, nodes, blocks * nodes), lambda i: (i, 0, 0)),
        ],
        out_specs=everything((blocks, 16, nodes)),
        scratch_shapes=sums + [pltpu.VMEM((n_row, 8, nodes), F32)],
        compiler_params=pltpu.CompilerParams(vmem_limit_bytes=20 << 20),
        cost_estimate=pl.CostEstimate(flops=4 * work, bytes_accessed=4 * work, transcendentals=0),
    )(me, again, heard, pairs)
    partial = lax.all_to_all(partial, ("col", "gz"), 0, 0)
    spread, edge, values = run(
        functools.partial(last_spread, n_col),
        "last_spread",
        [(8, 64, 256), (14, H, 128), (2, nodes)],
        [me, partial, target, before],
    )
    a, b = beside(edge)
    (part,) = run(
        functools.partial(own_relax, n_col),
        "own_relax",
        [(2, 2, 64, 128)],
        [me, full, second, spread, keep],
        [field] * 3,
        flops=40 * size_of(field),
    )
    strip = (2, 4, 4 * H, 256)
    (potential,) = run(
        functools.partial(last_relax, n_col),
        "last_relax",
        [(2, 2, 64, 128)],
        [me, full, a, b, part],
        [strip[1:]] + [strip] * 4,
    )
    return potential, values


def solution(mesh):
    return jax.shard_map(
        functools.partial(on_device, mesh.shape["row"], mesh.shape["col"]),
        mesh=mesh,
        in_specs=(
            P(None, "gz", "row", "col"),
            P("gz", "row", "col"),
            P(),
            P(("row", "col", "gz")),
            P(None, ("row", "col", "gz")),
            P(("row", "col", "gz")),
        ),
        out_specs=(P(None, "gz", "row", "col"), P(None, ("row", "col", "gz"))),
        check_vma=False,
    )
```

```python
import functools

import jax
import jax.numpy as jnp
from jax import lax
from jax.experimental import pallas as pl
from jax.experimental.pallas import tpu as pltpu
from jax.sharding import PartitionSpec as P


OMEGA = 0.8
RELAX = 0.5
SOFTEN = 0.01
H = 8
F32 = jnp.float32


def iota(shape, axis):
    return lax.broadcasted_iota(jnp.int32, shape, axis)


def pick(flag, shape, yes, no):
    return jnp.where(jnp.full(shape, flag, jnp.int32) == 1, yes, no)


def place(me_ref, n_col):
    me = me_ref[0]
    gz = lax.rem(me, 2)
    col = lax.rem(me // 2, n_col)
    row = me // (2 * n_col)
    return row, col, gz


def layer_of(own_ref, other_ref, kind, z, gz, shape):
    mine = pick(gz, shape, 1, 0) == z // 2
    return jnp.where(mine, own_ref[kind, z % 2], other_ref[kind, z % 2])


def col_pack(n_col, me_ref, own_ref, other_ref, a_ref, b_ref):
    _, col, gz = place(me_ref, n_col)
    shape = own_ref.shape[2:]
    lane = iota(shape, 1)
    left = jnp.zeros(shape, F32)
    right = jnp.zeros(shape, F32)
    for s in range(12):
        cell = layer_of(own_ref, other_ref, s // 4, s % 4, gz, shape)
        here = (lane >= 8 * s) & (lane < 8 * s + 8)
        low = pltpu.roll(cell, 8 * s, 1) if s else cell
        left = jnp.where(here, low, left)
        right = jnp.where(here, pltpu.roll(cell, 8 * s + 8, 1), right)
    odd = lax.rem(col, 2)
    a_ref[...] = pick(odd, shape, left, right)
    b_ref[...] = pick(odd, shape, right, left)


def edge_row(from_ref, s, last):
    rows, lanes = from_ref.shape[1:]
    return pick(last, (H, lanes), from_ref[s, rows - H : rows, :], from_ref[s, 0:H, :])


def tuck(side, s, into):
    lane = iota(side.shape, 1)
    moved = pltpu.roll(side, (16 * s + 8) % 128, 1)
    return jnp.where((lane >= 16 * s) & (lane < 16 * s + 16), moved, into)


def untuck(tile, s):
    lane = iota(tile.shape, 1)
    moved = pltpu.roll(tile, (128 - 16 * s - 8) % 128, 1)
    return jnp.where((lane < 8) | (lane >= 120), moved, 0.0)


def write_edges(edge_ref, start, from_ref, count, last):
    for first in range(0, count, 8):
        side = jnp.zeros((H, 128), F32)
        for s in range(first, min(first + 8, count)):
            edge = edge_row(from_ref, s, last)
            edge_ref[start + s] = edge[:, 0:128]
            side = tuck(edge[:, 128:256], s - first, side)
        edge_ref[start + count + first // 8] = side


def read_edge(ref, start, s, count):
    return jnp.concatenate([ref[start + s], untuck(ref[start + count + s // 8], s % 8)], 1)


def near_half(last):
    return (iota((H, 128), 0) // 4) == jnp.full((H, 128), last, jnp.int32)


def halo_rows(a, b, odd):
    return pick(odd, a.shape, a, b), pick(odd, a.shape, b, a)


def row_pack(n_col, me_ref, own_ref, other_ref, a_in, b_in, ext_ref, a_ref, b_ref):
    row, col, gz = place(me_ref, n_col)
    shape = own_ref.shape[2:]
    _, lanes = shape
    lane = iota(shape, 1)
    odd_col = lax.rem(col, 2)
    from_right = pick(odd_col, shape, b_in[...], a_in[...])
    from_left = pick(odd_col, shape, a_in[...], b_in[...])
    for s in range(12):
        cell = layer_of(own_ref, other_ref, s // 4, s % 4, gz, shape)
        low = pltpu.roll(from_right, lanes - 8 * s, 1) if s else from_right
        high = pltpu.roll(from_left, lanes - 8 - 8 * s, 1)
        side = jnp.where(lane < 8, low, jnp.where(lane >= lanes - 8, high, 0.0))
        ext_ref[s, :, 0:lanes] = cell
        ext_ref[s, :, lanes : 2 * lanes] = side
    odd = lax.rem(row, 2)
    write_edges(a_ref, 0, ext_ref, 12, 1 - odd)
    write_edges(b_ref, 0, ext_ref, 12, odd)


def sweep(now_ref, next_ref, force_ref, weight_ref):
    rows, lanes = now_ref.shape[2:]

    def image(m, carry):
        for z in range(4):
            cell = now_ref[m, z]
            beside = pltpu.roll(cell, 1, 0) + pltpu.roll(cell, rows - 1, 0)
            beside = beside + (pltpu.roll(cell, 1, 1) + pltpu.roll(cell, lanes - 1, 1))
            if z > 0:
                beside = beside + now_ref[m, z - 1]
            if z < 3:
                beside = beside + now_ref[m, z + 1]
            next_ref[m, z] = (1.0 - OMEGA) * cell + (force_ref[m, z] + weight_ref[z] * beside)
        return carry

    lax.fori_loop(0, now_ref.shape[0], image, 0, unroll=rows < 64)


def split(x):
    high = x.astype(jnp.bfloat16).astype(F32)
    rest = x - high
    middle = rest.astype(jnp.bfloat16).astype(F32)
    return high, middle, rest - middle


def trace_of(rows, owner, first_row):
    span = rows.shape[0] // 2
    nodes = owner.shape[1]
    line = iota((2 * span, nodes), 0)
    line = line + first_row + jnp.where(line >= span, 64 - span, 0)
    at_row = jnp.where(line == owner // 128, 1.0, 0.0).astype(jnp.bfloat16)
    at_lane = iota((128, nodes), 0) == lax.rem(owner, 128)
    found = sum(
        lax.dot_general(
            part.astype(jnp.bfloat16), at_row, (((0,), (0,)), ((), ())), preferred_element_type=F32
        )
        for part in split(rows)
    )
    return jnp.sum(jnp.where(at_lane, found, 0.0), axis=0, keepdims=True)


def two_layers(field_ref, m, gz, start, size):
    return jnp.concatenate([field_ref[m, 2 * gz + k, start : start + size, 0:128] for k in range(2)], 0)


def prepare(
    table_hbm, source_hbm, class_hbm, owner_hbm, pos_hbm, node_hbm, pack_ref, told_ref,
    table, level_ref, owner_ref, pos_ref, node_ref, sems,
):
    moves = [
        (class_hbm, level_ref),
        (table_hbm, table),
        (owner_hbm, owner_ref),
        (pos_hbm, pos_ref),
        (node_hbm, node_ref),
        (source_hbm, pack_ref.at[0:2]),
    ]
    copies = [pltpu.make_async_copy(a, b, sems.at[k]) for k, (a, b) in enumerate(moves)]
    for copy in copies:
        copy.start()
    for copy in copies:
        copy.wait()
    for k in range(2):
        level = level_ref[k]
        found = jnp.zeros(level.shape, F32)
        for n in range(table.shape[0]):
            found = jnp.where(level == n, table[n], found)
        pack_ref[2, k] = OMEGA / (6.0 + found)
    told_ref[0] = jnp.zeros(told_ref.shape[1:], F32)
    centred = pos_ref[...] - 0.5
    told_ref[0, 2:5, :] = centred
    told_ref[0, 5:6, :] = owner_ref[...].astype(F32)
    told_ref[0, 6:7, :] = node_ref[...]
    told_ref[0, 7:8, :] = jnp.sum(centred * centred, axis=0, keepdims=True)
    for k in range(1, told_ref.shape[0]):
        told_ref[k] = told_ref[0]


def stage(own_ref, out_ref):
    out_ref[...] = own_ref[...]


def first_relax(n_col, me_ref, ext_ref, a_in, b_in, target_ref, full_ref, first_ref, sent_ref, force, spare):
    row, col, gz = place(me_ref, n_col)
    odd = lax.rem(row, 2)
    for s in range(12):
        top, bottom = halo_rows(read_edge(a_in, 0, s, 12), read_edge(b_in, 0, s, 12), odd)
        full_ref[s // 4, s % 4, 0:H, :] = top
        full_ref[s // 4, s % 4, H : H + 64, :] = ext_ref[s]
        full_ref[s // 4, s % 4, H + 64 : 2 * H + 64, :] = bottom
    weight = full_ref.at[2]
    for m in range(2):
        for z in range(4):
            force[m, z] = full_ref[m, z] * weight[z]
    sweep(force, first_ref, force, weight)
    sweep(first_ref, spare, force, weight)
    sweep(spare, first_ref, force, weight)
    info = target_ref[2 * col + gz]
    owner = info[5:6, :].astype(jnp.int32)
    line = iota(info.shape, 0)
    for m in range(2):
        info = jnp.where(line == m, trace_of(two_layers(first_ref, m, gz, H, 64), owner, 0), info)
    for k in range(sent_ref.shape[0]):
        sent_ref[k] = info


def carry_relax(n_col, me_ref, full_ref, first_ref, target_ref, keep_ref, trace_ref, force, spare, other):
    _, col, gz = place(me_ref, n_col)
    weight = full_ref.at[2]
    for m in range(2):
        for z in range(4):
            force[m, z] = (full_ref[m, z] - RELAX * first_ref[m, z]) * weight[z]
    sweep(first_ref, spare, force, weight)
    sweep(spare, other, force, weight)
    sweep(other, spare, force, weight)
    sweep(spare, other, force, weight)
    owner = target_ref[2 * col + gz, 5:6, :].astype(jnp.int32)
    for m in range(2):
        for k in range(2):
            keep_ref[m, k] = other[m, 2 * gz + k, H : H + 64, 0:128]
        trace_ref[m : m + 1, :] = trace_of(two_layers(other, m, gz, H, 64), owner, 0)


def columns(rows, count):
    nodes = rows.shape[1]
    return [jnp.broadcast_to(rows[k : k + 1, :], (nodes, nodes)).T for k in range(count)]


def finish_apply(n_col, col, gz, acc, lined, own, out_ref):
    lined[...] = jnp.zeros_like(lined)
    for t in range(2 * n_col):
        mine = jnp.where(2 * col + gz == t, -0.5, 0.0).astype(F32)
        for m in range(2):
            whole = jnp.sum(acc[m, t], axis=0, keepdims=True)
            lined[m, t + 2 : t + 3, :] = whole + mine * own[m : m + 1, :]
    for c in range(n_col):
        for m in range(2):
            near = lined[m, 2 * c : 2 * c + 8, :]
            out_ref[2 * c, 8 * m : 8 * m + 8, :] = near
            out_ref[2 * c + 1, 8 * m : 8 * m + 8, :] = near


def build_apply(n_col, n_row, me_ref, heard_ref, target_ref, _, pair_ref, out_ref, acc, lined, goal):
    step = pl.program_id(0)
    row, col, gz = place(me_ref, n_col)
    nodes = heard_ref.shape[2]
    blocks = target_ref.shape[0]
    line = iota((8, nodes), 0)
    at_pos = (line >= 2) & (line <= 4)

    @pl.when(step == 0)
    def _():
        acc[...] = jnp.zeros_like(acc)
        for t in range(blocks):
            info = target_ref[t]
            norm = pltpu.roll(info, 1, 0) + SOFTEN
            base = jnp.where(line == 0, norm, jnp.where(at_pos, -2.0 * info, jnp.where(line == 7, 1.0, 0.0)))
            high, middle, low = split(base)
            rows = jnp.concatenate([high, middle, high, low, high, middle], 0)
            goal[:, t * nodes : (t + 1) * nodes] = rows.astype(jnp.bfloat16)

    heard = heard_ref[step]
    base = jnp.where(at_pos | (line == 7), heard, jnp.where(line == 0, 1.0, 0.0))
    high, middle, low = split(base)
    start = jnp.concatenate([high, high, middle, high, low, middle], 0).astype(jnp.bfloat16)
    z_at = columns(heard[4:5, :], 1)[0]
    by = columns(heard[0:2, :] * heard[6:7, :], 2)
    for t in range(0, blocks, 2):
        squares = lax.dot_general(
            start,
            goal[:, t * nodes : (t + 2) * nodes],
            (((0,), (0,)), ((), ())),
            preferred_element_type=F32,
        )
        for k in range(2):
            dz = target_ref[t + k, 4:5, :] - z_at
            inverse = lax.rsqrt(squares[:, k * nodes : (k + 1) * nodes])
            pair = dz * inverse * (inverse * inverse)
            pair_ref[0, :, (t + k) * nodes : (t + k + 1) * nodes] = pair
            for m in range(2):
                acc[m, t + k] = acc[m, t + k] + jnp.sum((pair * by[m]).reshape(nodes // 8, 8, nodes), axis=0)

    @pl.when(step == n_row - 1)
    def _():
        finish_apply(n_col, col, gz, acc, lined, heard_ref[row], out_ref)


def reapply(n_col, steps, me_ref, heard_ref, info_ref, pair_ref, out_ref, acc, lined, trace):
    step = pl.program_id(0)
    row, col, gz = place(me_ref, n_col)
    nodes = heard_ref.shape[2]
    n_row = heard_ref.shape[0]

    @pl.when(step == 0)
    def _():
        acc[...] = jnp.zeros_like(acc)
        for k in range(n_row):
            whole = heard_ref[k, 0:2, :]
            if k + 1 < n_row:
                whole = whole + heard_ref[k + 1, 2:4, :]
            if k > 0:
                whole = whole + heard_ref[k - 1, 4:6, :]
            trace[k, 0:2, :] = whole
            trace[k, 2:4, :] = whole * info_ref[k, 6:7, :]

    for k in range(pair_ref.shape[0]):
        by = columns(trace[step * pair_ref.shape[0] + k, 2:4, :], 2)
        for t in range(2 * n_col):
            pair = pair_ref[k, :, t * nodes : (t + 1) * nodes]
            for m in range(2):
                acc[m, t] = acc[m, t] + jnp.sum((pair * by[m]).reshape(nodes // 8, 8, nodes), axis=0)

    @pl.when(step == steps - 1)
    def _():
        finish_apply(n_col, col, gz, acc, lined, trace[row], out_ref)


def spread_nodes(n_col, col, part_ref, target_ref, spread_ref):
    nodes = part_ref.shape[2]
    blocks = 2 * n_col
    value = part_ref[0]
    for k in range(1, blocks):
        value = value + part_ref[k]
    shape = (128, nodes)
    down = iota(shape, 0)
    weighted, lanes = [], []
    for b in range(6):
        at = jnp.clip(2 * col - 2 + b, 0, blocks - 1)
        owner = target_ref[at, 5:6, :].astype(jnp.int32)
        hit = down == owner // 128
        weighted.append(
            jnp.concatenate([jnp.where(hit, value[8 * m + b : 8 * m + b + 1, :], 0.0) for m in range(2)], 0)
        )
        lane = down == lax.rem(owner, 128)
        if b < 2:
            lane = lane & (down >= 128 - H)
        if b > 3:
            lane = lane & (down < H)
        lanes.append(jnp.where(lane, 1.0, 0.0).astype(jnp.bfloat16))

    def product(a, b):
        parts = jnp.concatenate(split(a), 0).astype(jnp.bfloat16)
        found = lax.dot_general(parts, b, (((1,), (1,)), ((), ())), preferred_element_type=F32)
        count = a.shape[0]
        return found[0:count] + (found[count : 2 * count] + found[2 * count : 3 * count])

    for g in range(2):
        own = product(weighted[2 + g], lanes[2 + g])
        side = product(
            jnp.concatenate([weighted[g], weighted[4 + g]], 1), jnp.concatenate([lanes[g], lanes[4 + g]], 1)
        )
        for m in range(2):
            for k in range(2):
                start = 128 * m + 64 * k
                spread_ref[4 * m + 2 * g + k, :, 0:128] = own[start : start + 64]
                spread_ref[4 * m + 2 * g + k, :, 128:256] = side[start : start + 64]
    return value


def respond(
    n_col, n_row, me_ref, part_ref, target_ref, full_ref, heard_ref, kept_ref,
    spread_ref, sent_ref, second_ref, force, spare, other,
):
    row, col, gz = place(me_ref, n_col)
    weight = full_ref.at[2]
    spread_nodes(n_col, col, part_ref, target_ref, spread_ref)
    empty = jnp.zeros((H, 256), F32)
    for m in range(2):
        for z in range(4):
            force[m, z, 0:H, :] = empty
            force[m, z, H : H + 64, :] = spread_ref[4 * m + z] * weight[z, H : H + 64]
            force[m, z, H + 64 : 2 * H + 64, :] = empty
    sweep(force, spare, force, weight)
    sweep(spare, other, force, weight)
    sweep(other, second_ref, force, weight)
    for m in range(2):
        for z in range(4):
            force[m, z] = (-RELAX * second_ref[m, z]) * weight[z]
    sweep(force, other, force, weight)
    sweep(other, spare, force, weight)
    sweep(spare, other, force, weight)
    own = heard_ref[row, 5:6, :].astype(jnp.int32)
    above = heard_ref[jnp.maximum(row - 1, 0), 5:6, :].astype(jnp.int32)
    below = heard_ref[jnp.minimum(row + 1, n_row - 1), 5:6, :].astype(jnp.int32)
    line = iota((8, own.shape[1]), 0)
    sent = jnp.zeros((8, own.shape[1]), F32)
    for m in range(2):
        here = trace_of(two_layers(other, m, gz, H, 64), own, 0) + kept_ref[m : m + 1, :]
        sent = jnp.where(line == m, here, sent)
        sent = jnp.where(line == 2 + m, trace_of(two_layers(other, m, gz, 0, H), above, 64 - H), sent)
        sent = jnp.where(line == 4 + m, trace_of(two_layers(other, m, gz, H + 64, H), below, 0), sent)
    for k in range(sent_ref.shape[0]):
        sent_ref[k] = sent


def last_spread(n_col, me_ref, part_ref, target_ref, before_ref, spread_ref, a_ref, b_ref, value_ref):
    row, col, gz = place(me_ref, n_col)
    value = spread_nodes(n_col, col, part_ref, target_ref, spread_ref)
    odd = lax.rem(row, 2)
    for edge_ref, last in ((a_ref, 1 - odd), (b_ref, odd)):
        write_edges(edge_ref, 0, before_ref, 8, last)
        near = near_half(last)
        side = jnp.zeros((H, 128), F32)
        for s in range(0, 8, 2):
            one, two = edge_row(spread_ref, s, last), edge_row(spread_ref, s + 1, last)
            edge_ref[9 + s // 2] = jnp.where(near, one[:, 0:128], pltpu.roll(two[:, 0:128], 4, 0))
            side = tuck(one[:, 128:256], s, side)
            side = tuck(two[:, 128:256], s + 1, side)
        edge_ref[13] = side
    for m in range(2):
        value_ref[m : m + 1, :] = pick(
            gz, (1, value.shape[1]), value[8 * m + 3 : 8 * m + 4, :], value[8 * m + 2 : 8 * m + 3, :]
        )


def own_relax(n_col, me_ref, full_ref, second_ref, spread_ref, keep_ref, out_ref, force, spare, other):
    _, _, gz = place(me_ref, n_col)
    weight = full_ref.at[2]
    for m in range(2):
        for z in range(4):
            force[m, z] = (-RELAX * second_ref[m, z]) * weight[z]
            mid = force[m, z, H : H + 64, :]
            force[m, z, H : H + 64, :] = mid + spread_ref[4 * m + z] * weight[z, H : H + 64]
    sweep(second_ref, spare, force, weight)
    sweep(spare, other, force, weight)
    sweep(other, spare, force, weight)
    sweep(spare, other, force, weight)
    for m in range(2):
        for k in range(2):
            out_ref[m, k] = keep_ref[m, k] + other[m, 2 * gz + k, H : H + 64, 0:128]


def last_relax(
    n_col, me_ref, full_ref, a_in, b_in, part_ref, out_ref, weight, force, later, spare, other
):
    row, _, gz = place(me_ref, n_col)
    odd = lax.rem(row, 2)
    empty = jnp.zeros((2 * H, 256), F32)
    for z in range(4):
        weight[z, 0 : 2 * H] = full_ref[2, z, 0 : 2 * H]
        weight[z, 2 * H : 4 * H] = full_ref[2, z, 64 : 64 + 2 * H]
    for s in range(8):
        m, z = s // 4, s % 4
        top, bottom = halo_rows(read_edge(a_in, 0, s, 8), read_edge(b_in, 0, s, 8), odd)
        force[m, z, 0:H] = top * weight[z, 0:H]
        force[m, z, H : 3 * H] = empty
        force[m, z, 3 * H : 4 * H] = bottom * weight[z, 3 * H : 4 * H]
        ends = []
        for ref, last in ((a_in, odd), (b_in, 1 - odd)):
            tile = ref[9 + s // 2]
            main = jnp.where(near_half(last), pltpu.roll(tile, 4, 0) if s % 2 else tile, 0.0)
            ends.append(jnp.concatenate([main, untuck(ref[13], s)], 1))
        top, bottom = halo_rows(ends[0], ends[1], odd)
        later[m, z, 0:H] = top * weight[z, 0:H]
        later[m, z, H : 3 * H] = empty
        later[m, z, 3 * H : 4 * H] = bottom * weight[z, 3 * H : 4 * H]
    sweep(force, spare, force, weight)
    sweep(spare, other, force, weight)
    sweep(other, spare, force, weight)
    for m in range(2):
        for z in range(4):
            later[m, z] = later[m, z] - (RELAX * spare[m, z]) * weight[z]
    sweep(spare, other, later, weight)
    sweep(other, spare, later, weight)
    sweep(spare, other, later, weight)
    sweep(other, spare, later, weight)
    for m in range(2):
        for k in range(2):
            found = spare.at[m, 2 * gz + k]
            out_ref[m, k, 0:H, :] = part_ref[m, k, 0:H, :] + found[H : 2 * H, 0:128]
            out_ref[m, k, H : 64 - H, :] = part_ref[m, k, H : 64 - H, :]
            out_ref[m, k, 64 - H : 64, :] = part_ref[m, k, 64 - H : 64, :] + found[2 * H : 3 * H, 0:128]


SMEM = pl.BlockSpec(memory_space=pltpu.SMEM)
VMEM = pl.BlockSpec(memory_space=pltpu.VMEM)


def size_of(shape):
    return functools.reduce(lambda a, b: a * b, shape)


def run(body, outs, args, scratch=(), flops=0, scalars=1):
    moved = sum(a.size * 4 for a in args) + sum(4 * size_of(o) for o in outs)
    return pl.pallas_call(
        body,
        out_shape=[jax.ShapeDtypeStruct(o, F32) for o in outs],
        in_specs=[SMEM] * scalars + [VMEM] * (len(args) - scalars),
        out_specs=[VMEM] * len(outs),
        scratch_shapes=[pltpu.VMEM(s, F32) for s in scratch],
        compiler_params=pltpu.CompilerParams(vmem_limit_bytes=20 << 20),
        cost_estimate=pl.CostEstimate(flops=flops, bytes_accessed=moved, transcendentals=0),
    )(*args)


def on_device(n_row, n_col, source, cell_class, coeff_table, owner_cell, node_pos, node_weight):
    nodes = owner_cell.shape[0]
    blocks = 2 * n_col
    me = lax.axis_index(("row", "col", "gz")).reshape(1)

    def swaps(axis, size, a, b):
        first = [(i, i ^ 1) for i in range(size)]
        second = [(i + 1, i + 2) for i in range(0, size - 2, 2)]
        second = second + [(j, i) for i, j in second]
        a = lax.ppermute(a, axis, first)
        b = lax.ppermute(b, axis, second)
        return a, b

    packed, told = pl.pallas_call(
        prepare,
        name="prepare",
        out_shape=[jax.ShapeDtypeStruct(o, F32) for o in ((3, 2, 64, 128), (blocks, 8, nodes))],
        in_specs=[pl.BlockSpec(memory_space=pl.ANY)] * 6,
        out_specs=[VMEM] * 2,
        scratch_shapes=[
            pltpu.SMEM(coeff_table.shape, F32),
            pltpu.VMEM(cell_class.shape, jnp.int32),
            pltpu.VMEM((1, nodes), jnp.int32),
            pltpu.VMEM((3, nodes), F32),
            pltpu.VMEM((1, nodes), F32),
            pltpu.SemaphoreType.DMA((6,)),
        ],
        compiler_params=pltpu.CompilerParams(vmem_limit_bytes=60 << 20),
    )(coeff_table, source, cell_class, owner_cell[None, :], node_pos, node_weight[None, :])
    other = lax.ppermute(packed, "gz", [(0, 1), (1, 0)])
    target = lax.all_to_all(told, ("col", "gz"), 0, 0)
    (packed,) = run(stage, [packed.shape], [packed], scalars=0)
    a, b = run(functools.partial(col_pack, n_col), [(64, 128)] * 2, [me, packed, other])
    a, b = swaps("col", n_col, a, b)
    ext, a, b = run(
        functools.partial(row_pack, n_col), [(12, 64, 256), (14, H, 128), (14, H, 128)], [me, packed, other, a, b]
    )
    a, b = swaps("row", n_row, a, b)

    field = (2, 4, 64 + 2 * H, 256)
    full, first, sent = run(
        functools.partial(first_relax, n_col),
        [(3, 4, 64 + 2 * H, 256), field, (n_row, 8, nodes)],
        [me, ext, a, b, target],
        [field] * 2,
    )
    heard = lax.all_to_all(sent, "row", 0, 0)
    keep, kept = run(
        functools.partial(carry_relax, n_col),
        [(2, 2, 64, 128), (2, nodes)],
        [me, full, first, target],
        [field] * 3,
        flops=40 * size_of(field),
    )

    everything = lambda shape: pl.BlockSpec(shape, lambda i: (0,) * len(shape))
    work = n_row * blocks * nodes * nodes
    sums = [pltpu.VMEM((2, blocks, 8, nodes), F32), pltpu.VMEM((2, blocks + 8, nodes), F32)]
    pairs, partial = pl.pallas_call(
        functools.partial(build_apply, n_col, n_row),
        name="build_apply",
        grid=(n_row,),
        out_shape=[
            jax.ShapeDtypeStruct((n_row, nodes, blocks * nodes), F32),
            jax.ShapeDtypeStruct((blocks, 16, nodes), F32),
        ],
        in_specs=[SMEM, everything((n_row, 8, nodes)), everything((blocks, 8, nodes)), everything((2, nodes))],
        out_specs=[
            pl.BlockSpec((1, nodes, blocks * nodes), lambda i: (i, 0, 0)),
            everything((blocks, 16, nodes)),
        ],
        scratch_shapes=sums + [pltpu.VMEM((48, blocks * nodes), jnp.bfloat16)],
        compiler_params=pltpu.CompilerParams(vmem_limit_bytes=16 << 20),
        cost_estimate=pl.CostEstimate(flops=18 * work, bytes_accessed=4 * work, transcendentals=work),
    )(me, heard, target, kept)
    partial = lax.all_to_all(partial, ("col", "gz"), 0, 0)
    before, sent, second = run(
        functools.partial(respond, n_col, n_row),
        [(8, 64, 256), (n_row, 8, nodes), field],
        [me, partial, target, full, heard, kept],
        [field] * 3,
    )
    again = lax.all_to_all(sent, "row", 0, 0)
    group = 2
    partial = pl.pallas_call(
        functools.partial(reapply, n_col, n_row // group),
        name="reapply",
        grid=(n_row // group,),
        out_shape=jax.ShapeDtypeStruct((blocks, 16, nodes), F32),
        in_specs=[
            SMEM,
            everything((n_row, 8, nodes)),
            everything((n_row, 8, nodes)),
            pl.BlockSpec((group, nodes, blocks * nodes), lambda i: (i, 0, 0)),
        ],
        out_specs=everything((blocks, 16, nodes)),
        scratch_shapes=sums + [pltpu.VMEM((n_row, 8, nodes), F32)],
        compiler_params=pltpu.CompilerParams(vmem_limit_bytes=20 << 20),
        cost_estimate=pl.CostEstimate(flops=4 * work, bytes_accessed=4 * work, transcendentals=0),
    )(me, again, heard, pairs)
    partial = lax.all_to_all(partial, ("col", "gz"), 0, 0)
    spread, a, b, values = run(
        functools.partial(last_spread, n_col),
        [(8, 64, 256), (14, H, 128), (14, H, 128), (2, nodes)],
        [me, partial, target, before],
    )
    a, b = swaps("row", n_row, a, b)
    (part,) = run(
        functools.partial(own_relax, n_col),
        [(2, 2, 64, 128)],
        [me, full, second, spread, keep],
        [field] * 3,
        flops=40 * size_of(field),
    )
    strip = (2, 4, 4 * H, 256)
    (potential,) = run(
        functools.partial(last_relax, n_col), [(2, 2, 64, 128)], [me, full, a, b, part], [strip[1:]] + [strip] * 4
    )
    return potential, values


def solution(mesh):
    return jax.shard_map(
        functools.partial(on_device, mesh.shape["row"], mesh.shape["col"]),
        mesh=mesh,
        in_specs=(
            P(None, "gz", "row", "col"),
            P("gz", "row", "col"),
            P(),
            P(("row", "col", "gz")),
            P(None, ("row", "col", "gz")),
            P(("row", "col", "gz")),
        ),
        out_specs=(P(None, "gz", "row", "col"), P(None, ("row", "col", "gz"))),
        check_vma=False,
    )
```

```python
import functools

import jax
import jax.numpy as jnp
from jax import lax
from jax.experimental import pallas as pl
from jax.experimental.pallas import tpu as pltpu
from jax.sharding import PartitionSpec as P


OMEGA = 0.8
RELAX = 0.5
SOFTEN = 0.01
H = 8
F32 = jnp.float32


def iota(shape, axis):
    return lax.broadcasted_iota(jnp.int32, shape, axis)


def pick(flag, shape, yes, no):
    return jnp.where(jnp.full(shape, flag, jnp.int32) == 1, yes, no)


def place(me_ref, n_col):
    me = me_ref[0]
    gz = lax.rem(me, 2)
    col = lax.rem(me // 2, n_col)
    row = me // (2 * n_col)
    return row, col, gz


def layer_of(own_ref, other_ref, kind, z, gz, shape):
    mine = pick(gz, shape, 1, 0) == z // 2
    return jnp.where(mine, own_ref[kind, z % 2], other_ref[kind, z % 2])


def col_pack(n_col, me_ref, own_ref, other_ref, a_ref, b_ref):
    _, col, gz = place(me_ref, n_col)
    shape = own_ref.shape[2:]
    lane = iota(shape, 1)
    left = jnp.zeros(shape, F32)
    right = jnp.zeros(shape, F32)
    for s in range(12):
        cell = layer_of(own_ref, other_ref, s // 4, s % 4, gz, shape)
        here = (lane >= 8 * s) & (lane < 8 * s + 8)
        low = pltpu.roll(cell, 8 * s, 1) if s else cell
        left = jnp.where(here, low, left)
        right = jnp.where(here, pltpu.roll(cell, 8 * s + 8, 1), right)
    odd = lax.rem(col, 2)
    a_ref[...] = pick(odd, shape, left, right)
    b_ref[...] = pick(odd, shape, right, left)


def edge_row(from_ref, s, last):
    rows, lanes = from_ref.shape[1:]
    return pick(last, (H, lanes), from_ref[s, rows - H : rows, :], from_ref[s, 0:H, :])


def tuck(side, s, into):
    lane = iota(side.shape, 1)
    moved = pltpu.roll(side, (16 * s + 8) % 128, 1)
    return jnp.where((lane >= 16 * s) & (lane < 16 * s + 16), moved, into)


def untuck(tile, s):
    lane = iota(tile.shape, 1)
    moved = pltpu.roll(tile, (128 - 16 * s - 8) % 128, 1)
    return jnp.where((lane < 8) | (lane >= 120), moved, 0.0)


def write_edges(edge_ref, start, from_ref, count, last):
    for first in range(0, count, 8):
        side = jnp.zeros((H, 128), F32)
        for s in range(first, min(first + 8, count)):
            edge = edge_row(from_ref, s, last)
            edge_ref[start + s] = edge[:, 0:128]
            side = tuck(edge[:, 128:256], s - first, side)
        edge_ref[start + count + first // 8] = side


def read_edge(ref, start, s, count):
    return jnp.concatenate([ref[start + s], untuck(ref[start + count + s // 8], s % 8)], 1)


def near_half(last):
    return (iota((H, 128), 0) // 4) == jnp.full((H, 128), last, jnp.int32)


def halo_rows(a, b, odd):
    return pick(odd, a.shape, a, b), pick(odd, a.shape, b, a)


def row_pack(n_col, me_ref, own_ref, other_ref, a_in, b_in, ext_ref, a_ref, b_ref):
    row, col, gz = place(me_ref, n_col)
    shape = own_ref.shape[2:]
    _, lanes = shape
    lane = iota(shape, 1)
    odd_col = lax.rem(col, 2)
    from_right = pick(odd_col, shape, b_in[...], a_in[...])
    from_left = pick(odd_col, shape, a_in[...], b_in[...])
    for s in range(12):
        cell = layer_of(own_ref, other_ref, s // 4, s % 4, gz, shape)
        low = pltpu.roll(from_right, lanes - 8 * s, 1) if s else from_right
        high = pltpu.roll(from_left, lanes - 8 - 8 * s, 1)
        side = jnp.where(lane < 8, low, jnp.where(lane >= lanes - 8, high, 0.0))
        ext_ref[s, :, 0:lanes] = cell
        ext_ref[s, :, lanes : 2 * lanes] = side
    odd = lax.rem(row, 2)
    write_edges(a_ref, 0, ext_ref, 12, 1 - odd)
    write_edges(b_ref, 0, ext_ref, 12, odd)


def sweep(now_ref, next_ref, force_ref, weight_ref):
    rows, lanes = now_ref.shape[2:]

    def image(m, carry):
        for z in range(4):
            cell = now_ref[m, z]
            beside = pltpu.roll(cell, 1, 0) + pltpu.roll(cell, rows - 1, 0)
            beside = beside + (pltpu.roll(cell, 1, 1) + pltpu.roll(cell, lanes - 1, 1))
            if z > 0:
                beside = beside + now_ref[m, z - 1]
            if z < 3:
                beside = beside + now_ref[m, z + 1]
            next_ref[m, z] = (1.0 - OMEGA) * cell + (force_ref[m, z] + weight_ref[z] * beside)
        return carry

    lax.fori_loop(0, now_ref.shape[0], image, 0, unroll=rows < 64)


def split(x):
    high = x.astype(jnp.bfloat16).astype(F32)
    rest = x - high
    middle = rest.astype(jnp.bfloat16).astype(F32)
    return high, middle, rest - middle


def trace_of(rows, owner, first_row):
    span = rows.shape[0] // 2
    nodes = owner.shape[1]
    line = iota((2 * span, nodes), 0)
    line = line + first_row + jnp.where(line >= span, 64 - span, 0)
    at_row = jnp.where(line == owner // 128, 1.0, 0.0).astype(jnp.bfloat16)
    at_lane = iota((128, nodes), 0) == lax.rem(owner, 128)
    found = sum(
        lax.dot_general(
            part.astype(jnp.bfloat16), at_row, (((0,), (0,)), ((), ())), preferred_element_type=F32
        )
        for part in split(rows)
    )
    return jnp.sum(jnp.where(at_lane, found, 0.0), axis=0, keepdims=True)


def two_layers(field_ref, m, gz, start, size):
    return jnp.concatenate([field_ref[m, 2 * gz + k, start : start + size, 0:128] for k in range(2)], 0)


def prepare(
    table_hbm, source_hbm, class_hbm, owner_hbm, pos_hbm, node_hbm, pack_ref, told_ref,
    table, level_ref, owner_ref, pos_ref, node_ref, sems,
):
    moves = [
        (class_hbm, level_ref),
        (table_hbm, table),
        (owner_hbm, owner_ref),
        (pos_hbm, pos_ref),
        (node_hbm, node_ref),
        (source_hbm, pack_ref.at[0:2]),
    ]
    copies = [pltpu.make_async_copy(a, b, sems.at[k]) for k, (a, b) in enumerate(moves)]
    for copy in copies:
        copy.start()
    for copy in copies:
        copy.wait()
    for k in range(2):
        level = level_ref[k]
        found = jnp.zeros(level.shape, F32)
        for n in range(table.shape[0]):
            found = jnp.where(level == n, table[n], found)
        pack_ref[2, k] = OMEGA / (6.0 + found)
    told_ref[0] = jnp.zeros(told_ref.shape[1:], F32)
    centred = pos_ref[...] - 0.5
    told_ref[0, 2:5, :] = centred
    told_ref[0, 5:6, :] = owner_ref[...].astype(F32)
    told_ref[0, 6:7, :] = node_ref[...]
    told_ref[0, 7:8, :] = jnp.sum(centred * centred, axis=0, keepdims=True)
    for k in range(1, told_ref.shape[0]):
        told_ref[k] = told_ref[0]


def stage(own_ref, out_ref):
    out_ref[...] = own_ref[...]


def first_relax(n_col, me_ref, ext_ref, a_in, b_in, target_ref, full_ref, first_ref, sent_ref, force, spare):
    row, col, gz = place(me_ref, n_col)
    odd = lax.rem(row, 2)
    for s in range(12):
        top, bottom = halo_rows(read_edge(a_in, 0, s, 12), read_edge(b_in, 0, s, 12), odd)
        full_ref[s // 4, s % 4, 0:H, :] = top
        full_ref[s // 4, s % 4, H : H + 64, :] = ext_ref[s]
        full_ref[s // 4, s % 4, H + 64 : 2 * H + 64, :] = bottom
    weight = full_ref.at[2]
    for m in range(2):
        for z in range(4):
            force[m, z] = full_ref[m, z] * weight[z]
    sweep(force, first_ref, force, weight)
    sweep(first_ref, spare, force, weight)
    sweep(spare, first_ref, force, weight)
    info = target_ref[2 * col + gz]
    owner = info[5:6, :].astype(jnp.int32)
    line = iota(info.shape, 0)
    for m in range(2):
        info = jnp.where(line == m, trace_of(two_layers(first_ref, m, gz, H, 64), owner, 0), info)
    for k in range(sent_ref.shape[0]):
        sent_ref[k] = info


def carry_relax(n_col, me_ref, full_ref, first_ref, target_ref, keep_ref, trace_ref, goal, force, spare, other):
    _, col, gz = place(me_ref, n_col)
    weight = full_ref.at[2]
    for m in range(2):
        for z in range(4):
            force[m, z] = (full_ref[m, z] - RELAX * first_ref[m, z]) * weight[z]
    sweep(first_ref, spare, force, weight)
    sweep(spare, other, force, weight)
    sweep(other, spare, force, weight)
    sweep(spare, other, force, weight)
    owner = target_ref[2 * col + gz, 5:6, :].astype(jnp.int32)
    for m in range(2):
        for k in range(2):
            keep_ref[m, k] = other[m, 2 * gz + k, H : H + 64, 0:128]
        trace_ref[m : m + 1, :] = trace_of(two_layers(other, m, gz, H, 64), owner, 0)
    nodes = target_ref.shape[2]
    line = iota((8, nodes), 0)
    at_pos = (line >= 2) & (line <= 4)
    for t in range(target_ref.shape[0]):
        info = target_ref[t]
        norm = pltpu.roll(info, 1, 0) + SOFTEN
        base = jnp.where(line == 0, norm, jnp.where(at_pos, -2.0 * info, jnp.where(line == 7, 1.0, 0.0)))
        high, middle, low = split(base)
        rows = jnp.concatenate([high, middle, high, low, high, middle], 0)
        goal[:, t * nodes : (t + 1) * nodes] = rows.astype(jnp.bfloat16)


def columns(rows, count):
    nodes = rows.shape[1]
    return [jnp.broadcast_to(rows[k : k + 1, :], (nodes, nodes)).T for k in range(count)]


def finish_apply(n_col, col, gz, acc, lined, own, out_ref):
    lined[...] = jnp.zeros_like(lined)
    for t in range(2 * n_col):
        mine = jnp.where(2 * col + gz == t, -0.5, 0.0).astype(F32)
        for m in range(2):
            whole = jnp.sum(acc[m, t], axis=0, keepdims=True)
            lined[m, t + 2 : t + 3, :] = whole + mine * own[m : m + 1, :]
    for c in range(n_col):
        for m in range(2):
            near = lined[m, 2 * c : 2 * c + 8, :]
            out_ref[2 * c, 8 * m : 8 * m + 8, :] = near
            out_ref[2 * c + 1, 8 * m : 8 * m + 8, :] = near


def build_apply(n_col, n_row, me_ref, heard_ref, target_ref, goal, pair_ref, out_ref, acc, lined):
    step = pl.program_id(0)
    row, col, gz = place(me_ref, n_col)
    nodes = heard_ref.shape[2]
    blocks = target_ref.shape[0]
    line = iota((8, nodes), 0)
    at_pos = (line >= 2) & (line <= 4)

    @pl.when(step == 0)
    def _():
        acc[...] = jnp.zeros_like(acc)

    heard = heard_ref[step]
    base = jnp.where(at_pos | (line == 7), heard, jnp.where(line == 0, 1.0, 0.0))
    high, middle, low = split(base)
    start = jnp.concatenate([high, high, middle, high, low, middle], 0).astype(jnp.bfloat16)
    z_at = columns(heard[4:5, :], 1)[0]
    by = columns(heard[0:2, :] * heard[6:7, :], 2)
    for t in range(0, blocks, 2):
        squares = lax.dot_general(
            start,
            goal[:, t * nodes : (t + 2) * nodes],
            (((0,), (0,)), ((), ())),
            preferred_element_type=F32,
        )
        for k in range(2):
            dz = target_ref[t + k, 4:5, :] - z_at
            inverse = lax.rsqrt(squares[:, k * nodes : (k + 1) * nodes])
            pair = dz * inverse * (inverse * inverse)
            pair_ref[0, :, (t + k) * nodes : (t + k + 1) * nodes] = pair
            for m in range(2):
                acc[m, t + k] = acc[m, t + k] + jnp.sum((pair * by[m]).reshape(nodes // 8, 8, nodes), axis=0)

    @pl.when(step == n_row - 1)
    def _():
        finish_apply(n_col, col, gz, acc, lined, heard_ref[row], out_ref)


def reapply(n_col, steps, me_ref, heard_ref, info_ref, pair_ref, out_ref, acc, lined, trace):
    step = pl.program_id(0)
    row, col, gz = place(me_ref, n_col)
    nodes = heard_ref.shape[2]
    n_row = heard_ref.shape[0]

    @pl.when(step == 0)
    def _():
        acc[...] = jnp.zeros_like(acc)
        for k in range(n_row):
            whole = heard_ref[k, 0:2, :]
            if k + 1 < n_row:
                whole = whole + heard_ref[k + 1, 2:4, :]
            if k > 0:
                whole = whole + heard_ref[k - 1, 4:6, :]
            trace[k, 0:2, :] = whole
            trace[k, 2:4, :] = whole * info_ref[k, 6:7, :]

    for k in range(pair_ref.shape[0]):
        by = columns(trace[step * pair_ref.shape[0] + k, 2:4, :], 2)
        for t in range(2 * n_col):
            pair = pair_ref[k, :, t * nodes : (t + 1) * nodes]
            for m in range(2):
                acc[m, t] = acc[m, t] + jnp.sum((pair * by[m]).reshape(nodes // 8, 8, nodes), axis=0)

    @pl.when(step == steps - 1)
    def _():
        finish_apply(n_col, col, gz, acc, lined, trace[row], out_ref)


def spread_nodes(n_col, col, part_ref, target_ref, spread_ref):
    nodes = part_ref.shape[2]
    blocks = 2 * n_col
    value = part_ref[0]
    for k in range(1, blocks):
        value = value + part_ref[k]
    shape = (128, nodes)
    down = iota(shape, 0)
    weighted, lanes = [], []
    for b in range(6):
        at = jnp.clip(2 * col - 2 + b, 0, blocks - 1)
        owner = target_ref[at, 5:6, :].astype(jnp.int32)
        hit = down == owner // 128
        weighted.append(
            jnp.concatenate([jnp.where(hit, value[8 * m + b : 8 * m + b + 1, :], 0.0) for m in range(2)], 0)
        )
        lane = down == lax.rem(owner, 128)
        if b < 2:
            lane = lane & (down >= 128 - H)
        if b > 3:
            lane = lane & (down < H)
        lanes.append(jnp.where(lane, 1.0, 0.0).astype(jnp.bfloat16))

    def product(a, b):
        parts = jnp.concatenate(split(a), 0).astype(jnp.bfloat16)
        found = lax.dot_general(parts, b, (((1,), (1,)), ((), ())), preferred_element_type=F32)
        count = a.shape[0]
        return found[0:count] + (found[count : 2 * count] + found[2 * count : 3 * count])

    for g in range(2):
        own = product(weighted[2 + g], lanes[2 + g])
        side = product(
            jnp.concatenate([weighted[g], weighted[4 + g]], 1), jnp.concatenate([lanes[g], lanes[4 + g]], 1)
        )
        for m in range(2):
            for k in range(2):
                start = 128 * m + 64 * k
                spread_ref[4 * m + 2 * g + k, :, 0:128] = own[start : start + 64]
                spread_ref[4 * m + 2 * g + k, :, 128:256] = side[start : start + 64]
    return value


def respond(
    n_col, n_row, me_ref, part_ref, target_ref, full_ref, heard_ref, kept_ref,
    spread_ref, sent_ref, second_ref, force, spare, other,
):
    row, col, gz = place(me_ref, n_col)
    weight = full_ref.at[2]
    spread_nodes(n_col, col, part_ref, target_ref, spread_ref)
    empty = jnp.zeros((H, 256), F32)
    for m in range(2):
        for z in range(4):
            force[m, z, 0:H, :] = empty
            force[m, z, H : H + 64, :] = spread_ref[4 * m + z] * weight[z, H : H + 64]
            force[m, z, H + 64 : 2 * H + 64, :] = empty
    sweep(force, spare, force, weight)
    sweep(spare, other, force, weight)
    sweep(other, second_ref, force, weight)
    for m in range(2):
        for z in range(4):
            force[m, z] = (-RELAX * second_ref[m, z]) * weight[z]
    sweep(force, other, force, weight)
    sweep(other, spare, force, weight)
    sweep(spare, other, force, weight)
    own = heard_ref[row, 5:6, :].astype(jnp.int32)
    above = heard_ref[jnp.maximum(row - 1, 0), 5:6, :].astype(jnp.int32)
    below = heard_ref[jnp.minimum(row + 1, n_row - 1), 5:6, :].astype(jnp.int32)
    line = iota((8, own.shape[1]), 0)
    sent = jnp.zeros((8, own.shape[1]), F32)
    for m in range(2):
        here = trace_of(two_layers(other, m, gz, H, 64), own, 0) + kept_ref[m : m + 1, :]
        sent = jnp.where(line == m, here, sent)
        sent = jnp.where(line == 2 + m, trace_of(two_layers(other, m, gz, 0, H), above, 64 - H), sent)
        sent = jnp.where(line == 4 + m, trace_of(two_layers(other, m, gz, H + 64, H), below, 0), sent)
    for k in range(sent_ref.shape[0]):
        sent_ref[k] = sent


def last_spread(n_col, me_ref, part_ref, target_ref, before_ref, spread_ref, a_ref, b_ref, value_ref):
    row, col, gz = place(me_ref, n_col)
    value = spread_nodes(n_col, col, part_ref, target_ref, spread_ref)
    odd = lax.rem(row, 2)
    for edge_ref, last in ((a_ref, 1 - odd), (b_ref, odd)):
        write_edges(edge_ref, 0, before_ref, 8, last)
        near = near_half(last)
        side = jnp.zeros((H, 128), F32)
        for s in range(0, 8, 2):
            one, two = edge_row(spread_ref, s, last), edge_row(spread_ref, s + 1, last)
            edge_ref[9 + s // 2] = jnp.where(near, one[:, 0:128], pltpu.roll(two[:, 0:128], 4, 0))
            side = tuck(one[:, 128:256], s, side)
            side = tuck(two[:, 128:256], s + 1, side)
        edge_ref[13] = side
    for m in range(2):
        value_ref[m : m + 1, :] = pick(
            gz, (1, value.shape[1]), value[8 * m + 3 : 8 * m + 4, :], value[8 * m + 2 : 8 * m + 3, :]
        )


def own_relax(n_col, me_ref, full_ref, second_ref, spread_ref, keep_ref, out_ref, force, spare, other):
    _, _, gz = place(me_ref, n_col)
    weight = full_ref.at[2]
    for m in range(2):
        for z in range(4):
            force[m, z] = (-RELAX * second_ref[m, z]) * weight[z]
            mid = force[m, z, H : H + 64, :]
            force[m, z, H : H + 64, :] = mid + spread_ref[4 * m + z] * weight[z, H : H + 64]
    sweep(second_ref, spare, force, weight)
    sweep(spare, other, force, weight)
    sweep(other, spare, force, weight)
    sweep(spare, other, force, weight)
    for m in range(2):
        for k in range(2):
            out_ref[m, k] = keep_ref[m, k] + other[m, 2 * gz + k, H : H + 64, 0:128]


def last_relax(
    n_col, me_ref, full_ref, a_in, b_in, part_ref, out_ref, weight, force, later, spare, other
):
    row, _, gz = place(me_ref, n_col)
    odd = lax.rem(row, 2)
    empty = jnp.zeros((2 * H, 256), F32)
    for z in range(4):
        weight[z, 0 : 2 * H] = full_ref[2, z, 0 : 2 * H]
        weight[z, 2 * H : 4 * H] = full_ref[2, z, 64 : 64 + 2 * H]
    for s in range(8):
        m, z = s // 4, s % 4
        top, bottom = halo_rows(read_edge(a_in, 0, s, 8), read_edge(b_in, 0, s, 8), odd)
        force[m, z, 0:H] = top * weight[z, 0:H]
        force[m, z, H : 3 * H] = empty
        force[m, z, 3 * H : 4 * H] = bottom * weight[z, 3 * H : 4 * H]
        ends = []
        for ref, last in ((a_in, odd), (b_in, 1 - odd)):
            tile = ref[9 + s // 2]
            main = jnp.where(near_half(last), pltpu.roll(tile, 4, 0) if s % 2 else tile, 0.0)
            ends.append(jnp.concatenate([main, untuck(ref[13], s)], 1))
        top, bottom = halo_rows(ends[0], ends[1], odd)
        later[m, z, 0:H] = top * weight[z, 0:H]
        later[m, z, H : 3 * H] = empty
        later[m, z, 3 * H : 4 * H] = bottom * weight[z, 3 * H : 4 * H]
    sweep(force, spare, force, weight)
    sweep(spare, other, force, weight)
    sweep(other, spare, force, weight)
    for m in range(2):
        for z in range(4):
            later[m, z] = later[m, z] - (RELAX * spare[m, z]) * weight[z]
    sweep(spare, other, later, weight)
    sweep(other, spare, later, weight)
    sweep(spare, other, later, weight)
    sweep(other, spare, later, weight)
    for m in range(2):
        for k in range(2):
            found = spare.at[m, 2 * gz + k]
            out_ref[m, k, 0:H, :] = part_ref[m, k, 0:H, :] + found[H : 2 * H, 0:128]
            out_ref[m, k, H : 64 - H, :] = part_ref[m, k, H : 64 - H, :]
            out_ref[m, k, 64 - H : 64, :] = part_ref[m, k, 64 - H : 64, :] + found[2 * H : 3 * H, 0:128]


SMEM = pl.BlockSpec(memory_space=pltpu.SMEM)
VMEM = pl.BlockSpec(memory_space=pltpu.VMEM)


def size_of(shape):
    return functools.reduce(lambda a, b: a * b, shape)


def run(body, outs, args, scratch=(), flops=0, scalars=1):
    moved = sum(a.size * 4 for a in args) + sum(4 * size_of(o) for o in outs)
    return pl.pallas_call(
        body,
        out_shape=[jax.ShapeDtypeStruct(o, F32) for o in outs],
        in_specs=[SMEM] * scalars + [VMEM] * (len(args) - scalars),
        out_specs=[VMEM] * len(outs),
        scratch_shapes=[pltpu.VMEM(s, F32) for s in scratch],
        compiler_params=pltpu.CompilerParams(vmem_limit_bytes=20 << 20),
        cost_estimate=pl.CostEstimate(flops=flops, bytes_accessed=moved, transcendentals=0),
    )(*args)


def on_device(n_row, n_col, source, cell_class, coeff_table, owner_cell, node_pos, node_weight):
    nodes = owner_cell.shape[0]
    blocks = 2 * n_col
    me = lax.axis_index(("row", "col", "gz")).reshape(1)

    def swaps(axis, size, a, b):
        first = [(i, i ^ 1) for i in range(size)]
        second = [(i + 1, i + 2) for i in range(0, size - 2, 2)]
        second = second + [(j, i) for i, j in second]
        a = lax.ppermute(a, axis, first)
        b = lax.ppermute(b, axis, second)
        return a, b

    packed, told = pl.pallas_call(
        prepare,
        name="prepare",
        out_shape=[jax.ShapeDtypeStruct(o, F32) for o in ((3, 2, 64, 128), (blocks, 8, nodes))],
        in_specs=[pl.BlockSpec(memory_space=pl.ANY)] * 6,
        out_specs=[VMEM] * 2,
        scratch_shapes=[
            pltpu.SMEM(coeff_table.shape, F32),
            pltpu.VMEM(cell_class.shape, jnp.int32),
            pltpu.VMEM((1, nodes), jnp.int32),
            pltpu.VMEM((3, nodes), F32),
            pltpu.VMEM((1, nodes), F32),
            pltpu.SemaphoreType.DMA((6,)),
        ],
        compiler_params=pltpu.CompilerParams(vmem_limit_bytes=60 << 20),
    )(coeff_table, source, cell_class, owner_cell[None, :], node_pos, node_weight[None, :])
    other = lax.ppermute(packed, "gz", [(0, 1), (1, 0)])
    target = lax.all_to_all(told, ("col", "gz"), 0, 0)
    (packed,) = run(stage, [packed.shape], [packed], scalars=0)
    a, b = run(functools.partial(col_pack, n_col), [(64, 128)] * 2, [me, packed, other])
    a, b = swaps("col", n_col, a, b)
    ext, a, b = run(
        functools.partial(row_pack, n_col), [(12, 64, 256), (14, H, 128), (14, H, 128)], [me, packed, other, a, b]
    )
    a, b = swaps("row", n_row, a, b)

    field = (2, 4, 64 + 2 * H, 256)
    full, first, sent = run(
        functools.partial(first_relax, n_col),
        [(3, 4, 64 + 2 * H, 256), field, (n_row, 8, nodes)],
        [me, ext, a, b, target],
        [field] * 2,
    )
    heard = lax.all_to_all(sent, "row", 0, 0)
    keep, kept, goal = pl.pallas_call(
        functools.partial(carry_relax, n_col),
        name="carry_relax",
        out_shape=[
            jax.ShapeDtypeStruct((2, 2, 64, 128), F32),
            jax.ShapeDtypeStruct((2, nodes), F32),
            jax.ShapeDtypeStruct((48, blocks * nodes), jnp.bfloat16),
        ],
        in_specs=[SMEM] + [VMEM] * 3,
        out_specs=[VMEM] * 3,
        scratch_shapes=[pltpu.VMEM(field, F32)] * 3,
        compiler_params=pltpu.CompilerParams(vmem_limit_bytes=20 << 20),
        cost_estimate=pl.CostEstimate(
            flops=40 * size_of(field), bytes_accessed=4 * size_of(field), transcendentals=0
        ),
    )(me, full, first, target)

    everything = lambda shape: pl.BlockSpec(shape, lambda i: (0,) * len(shape))
    work = n_row * blocks * nodes * nodes
    sums = [pltpu.VMEM((2, blocks, 8, nodes), F32), pltpu.VMEM((2, blocks + 8, nodes), F32)]
    pairs, partial = pl.pallas_call(
        functools.partial(build_apply, n_col, n_row),
        name="build_apply",
        grid=(n_row,),
        out_shape=[
            jax.ShapeDtypeStruct((n_row, nodes, blocks * nodes), F32),
            jax.ShapeDtypeStruct((blocks, 16, nodes), F32),
        ],
        in_specs=[SMEM, everything((n_row, 8, nodes)), everything((blocks, 8, nodes)), everything((48, blocks * nodes))],
        out_specs=[
            pl.BlockSpec((1, nodes, blocks * nodes), lambda i: (i, 0, 0)),
            everything((blocks, 16, nodes)),
        ],
        scratch_shapes=sums,
        compiler_params=pltpu.CompilerParams(vmem_limit_bytes=16 << 20),
        cost_estimate=pl.CostEstimate(flops=18 * work, bytes_accessed=4 * work, transcendentals=work),
    )(me, heard, target, goal)
    partial = lax.all_to_all(partial, ("col", "gz"), 0, 0)
    before, sent, second = run(
        functools.partial(respond, n_col, n_row),
        [(8, 64, 256), (n_row, 8, nodes), field],
        [me, partial, target, full, heard, kept],
        [field] * 3,
    )
    again = lax.all_to_all(sent, "row", 0, 0)
    group = 2
    partial = pl.pallas_call(
        functools.partial(reapply, n_col, n_row // group),
        name="reapply",
        grid=(n_row // group,),
        out_shape=jax.ShapeDtypeStruct((blocks, 16, nodes), F32),
        in_specs=[
            SMEM,
            everything((n_row, 8, nodes)),
            everything((n_row, 8, nodes)),
            pl.BlockSpec((group, nodes, blocks * nodes), lambda i: (i, 0, 0)),
        ],
        out_specs=everything((blocks, 16, nodes)),
        scratch_shapes=sums + [pltpu.VMEM((n_row, 8, nodes), F32)],
        compiler_params=pltpu.CompilerParams(vmem_limit_bytes=20 << 20),
        cost_estimate=pl.CostEstimate(flops=4 * work, bytes_accessed=4 * work, transcendentals=0),
    )(me, again, heard, pairs)
    partial = lax.all_to_all(partial, ("col", "gz"), 0, 0)
    spread, a, b, values = run(
        functools.partial(last_spread, n_col),
        [(8, 64, 256), (14, H, 128), (14, H, 128), (2, nodes)],
        [me, partial, target, before],
    )
    a, b = swaps("row", n_row, a, b)
    (part,) = run(
        functools.partial(own_relax, n_col),
        [(2, 2, 64, 128)],
        [me, full, second, spread, keep],
        [field] * 3,
        flops=40 * size_of(field),
    )
    strip = (2, 4, 4 * H, 256)
    (potential,) = run(
        functools.partial(last_relax, n_col), [(2, 2, 64, 128)], [me, full, a, b, part], [strip[1:]] + [strip] * 4
    )
    return potential, values


def solution(mesh):
    return jax.shard_map(
        functools.partial(on_device, mesh.shape["row"], mesh.shape["col"]),
        mesh=mesh,
        in_specs=(
            P(None, "gz", "row", "col"),
            P("gz", "row", "col"),
            P(),
            P(("row", "col", "gz")),
            P(None, ("row", "col", "gz")),
            P(("row", "col", "gz")),
        ),
        out_specs=(P(None, "gz", "row", "col"), P(None, ("row", "col", "gz"))),
        check_vma=False,
    )
```

```python
import functools

import jax
import jax.numpy as jnp
from jax import lax
from jax.experimental import pallas as pl
from jax.experimental.pallas import tpu as pltpu
from jax.sharding import PartitionSpec as P


OMEGA = 0.8
RELAX = 0.5
SOFTEN = 0.01
H = 8
F32 = jnp.float32


def iota(shape, axis):
    return lax.broadcasted_iota(jnp.int32, shape, axis)


def pick(flag, shape, yes, no):
    return jnp.where(jnp.full(shape, flag, jnp.int32) == 1, yes, no)


def place(me_ref, n_col):
    me = me_ref[0]
    gz = lax.rem(me, 2)
    col = lax.rem(me // 2, n_col)
    row = me // (2 * n_col)
    return row, col, gz


def layer_of(own_ref, other_ref, kind, z, gz, shape):
    mine = pick(gz, shape, 1, 0) == z // 2
    return jnp.where(mine, own_ref[kind, z % 2], other_ref[kind, z % 2])


def col_pack(n_col, me_ref, own_ref, other_ref, a_ref, b_ref):
    _, col, gz = place(me_ref, n_col)
    shape = own_ref.shape[2:]
    lane = iota(shape, 1)
    left = jnp.zeros(shape, F32)
    right = jnp.zeros(shape, F32)
    for s in range(12):
        cell = layer_of(own_ref, other_ref, s // 4, s % 4, gz, shape)
        here = (lane >= 8 * s) & (lane < 8 * s + 8)
        low = pltpu.roll(cell, 8 * s, 1) if s else cell
        left = jnp.where(here, low, left)
        right = jnp.where(here, pltpu.roll(cell, 8 * s + 8, 1), right)
    odd = lax.rem(col, 2)
    a_ref[...] = pick(odd, shape, left, right)
    b_ref[...] = pick(odd, shape, right, left)


def edge_row(from_ref, s, last):
    rows, lanes = from_ref.shape[1:]
    return pick(last, (H, lanes), from_ref[s, rows - H : rows, :], from_ref[s, 0:H, :])


def tuck(side, s, into):
    lane = iota(side.shape, 1)
    moved = pltpu.roll(side, (16 * s + 8) % 128, 1)
    return jnp.where((lane >= 16 * s) & (lane < 16 * s + 16), moved, into)


def untuck(tile, s):
    lane = iota(tile.shape, 1)
    moved = pltpu.roll(tile, (128 - 16 * s - 8) % 128, 1)
    return jnp.where((lane < 8) | (lane >= 120), moved, 0.0)


def write_edges(edge_ref, start, from_ref, count, last):
    for first in range(0, count, 8):
        side = jnp.zeros((H, 128), F32)
        for s in range(first, min(first + 8, count)):
            edge = edge_row(from_ref, s, last)
            edge_ref[start + s] = edge[:, 0:128]
            side = tuck(edge[:, 128:256], s - first, side)
        edge_ref[start + count + first // 8] = side


def read_edge(ref, start, s, count):
    return jnp.concatenate([ref[start + s], untuck(ref[start + count + s // 8], s % 8)], 1)


def near_half(last):
    return (iota((H, 128), 0) // 4) == jnp.full((H, 128), last, jnp.int32)


def halo_rows(a, b, odd):
    return pick(odd, a.shape, a, b), pick(odd, a.shape, b, a)


def row_pack(n_col, me_ref, own_ref, other_ref, a_in, b_in, ext_ref, a_ref, b_ref):
    row, col, gz = place(me_ref, n_col)
    shape = own_ref.shape[2:]
    _, lanes = shape
    lane = iota(shape, 1)
    odd_col = lax.rem(col, 2)
    from_right = pick(odd_col, shape, b_in[...], a_in[...])
    from_left = pick(odd_col, shape, a_in[...], b_in[...])
    for s in range(12):
        cell = layer_of(own_ref, other_ref, s // 4, s % 4, gz, shape)
        low = pltpu.roll(from_right, lanes - 8 * s, 1) if s else from_right
        high = pltpu.roll(from_left, lanes - 8 - 8 * s, 1)
        side = jnp.where(lane < 8, low, jnp.where(lane >= lanes - 8, high, 0.0))
        ext_ref[s, :, 0:lanes] = cell
        ext_ref[s, :, lanes : 2 * lanes] = side
    odd = lax.rem(row, 2)
    write_edges(a_ref, 0, ext_ref, 12, 1 - odd)
    write_edges(b_ref, 0, ext_ref, 12, odd)


def sweep(now_ref, next_ref, force_ref, weight_ref):
    rows, lanes = now_ref.shape[2:]
    line = iota((8, lanes), 0)

    def one(m, z, low, high):
        tiles = rows // 8
        cells = [now_ref[m, z, 8 * i : 8 * i + 8, :] for i in range(tiles)]
        downs = [pltpu.roll(cell, 1, 0) for cell in cells]
        ups = [pltpu.roll(cell, 7, 0) for cell in cells]
        for i in range(tiles):
            beside = jnp.where(line == 0, downs[i - 1], downs[i]) + jnp.where(line == 7, ups[(i + 1) % tiles], ups[i])
            beside = beside + (pltpu.roll(cells[i], 1, 1) + pltpu.roll(cells[i], lanes - 1, 1))
            at = slice(8 * i, 8 * i + 8)
            if low is not None:
                beside = beside + now_ref[m, low, at, :]
            if high is not None:
                beside = beside + now_ref[m, high, at, :]
            next_ref[m, z, at, :] = (1.0 - OMEGA) * cells[i] + (force_ref[m, z, at, :] + weight_ref[z, at, :] * beside)

    def image(m, carry):
        for z in range(4):
            one(m, z, z - 1 if z > 0 else None, z + 1 if z < 3 else None)
        return carry

    lax.fori_loop(0, now_ref.shape[0], image, 0, unroll=rows < 64)


def split(x):
    high = x.astype(jnp.bfloat16).astype(F32)
    rest = x - high
    middle = rest.astype(jnp.bfloat16).astype(F32)
    return high, middle, rest - middle


def trace_of(rows, owner, first_row):
    span = rows.shape[0] // 2
    nodes = owner.shape[1]
    line = iota((2 * span, nodes), 0)
    line = line + first_row + jnp.where(line >= span, 64 - span, 0)
    at_row = jnp.where(line == owner // 128, 1.0, 0.0).astype(jnp.bfloat16)
    at_lane = iota((128, nodes), 0) == lax.rem(owner, 128)
    found = sum(
        lax.dot_general(
            part.astype(jnp.bfloat16), at_row, (((0,), (0,)), ((), ())), preferred_element_type=F32
        )
        for part in split(rows)
    )
    return jnp.sum(jnp.where(at_lane, found, 0.0), axis=0, keepdims=True)


def two_layers(field_ref, m, gz, start, size):
    return jnp.concatenate([field_ref[m, 2 * gz + k, start : start + size, 0:128] for k in range(2)], 0)


def prepare(
    table_hbm, source_hbm, class_hbm, owner_hbm, pos_hbm, node_hbm, pack_ref, told_ref,
    table, level_ref, owner_ref, pos_ref, node_ref, sems,
):
    moves = [
        (class_hbm, level_ref),
        (table_hbm, table),
        (owner_hbm, owner_ref),
        (pos_hbm, pos_ref),
        (node_hbm, node_ref),
        (source_hbm, pack_ref.at[0:2]),
    ]
    copies = [pltpu.make_async_copy(a, b, sems.at[k]) for k, (a, b) in enumerate(moves)]
    for copy in copies:
        copy.start()
    for copy in copies:
        copy.wait()
    for k in range(2):
        level = level_ref[k]
        found = jnp.zeros(level.shape, F32)
        for n in range(table.shape[0]):
            found = jnp.where(level == n, table[n], found)
        pack_ref[2, k] = OMEGA / (6.0 + found)
    told_ref[0] = jnp.zeros(told_ref.shape[1:], F32)
    centred = pos_ref[...] - 0.5
    told_ref[0, 2:5, :] = centred
    told_ref[0, 5:6, :] = owner_ref[...].astype(F32)
    told_ref[0, 6:7, :] = node_ref[...]
    told_ref[0, 7:8, :] = jnp.sum(centred * centred, axis=0, keepdims=True)
    for k in range(1, told_ref.shape[0]):
        told_ref[k] = told_ref[0]


def stage(own_ref, out_ref):
    out_ref[...] = own_ref[...]


def first_relax(n_col, me_ref, ext_ref, a_in, b_in, target_ref, full_ref, first_ref, sent_ref, force, spare):
    row, col, gz = place(me_ref, n_col)
    odd = lax.rem(row, 2)
    for s in range(12):
        top, bottom = halo_rows(read_edge(a_in, 0, s, 12), read_edge(b_in, 0, s, 12), odd)
        full_ref[s // 4, s % 4, 0:H, :] = top
        full_ref[s // 4, s % 4, H : H + 64, :] = ext_ref[s]
        full_ref[s // 4, s % 4, H + 64 : 2 * H + 64, :] = bottom
    weight = full_ref.at[2]
    for m in range(2):
        for z in range(4):
            force[m, z] = full_ref[m, z] * weight[z]
    sweep(force, first_ref, force, weight)
    sweep(first_ref, spare, force, weight)
    sweep(spare, first_ref, force, weight)
    info = target_ref[2 * col + gz]
    owner = info[5:6, :].astype(jnp.int32)
    line = iota(info.shape, 0)
    for m in range(2):
        info = jnp.where(line == m, trace_of(two_layers(first_ref, m, gz, H, 64), owner, 0), info)
    for k in range(sent_ref.shape[0]):
        sent_ref[k] = info


def carry_relax(n_col, me_ref, full_ref, first_ref, target_ref, keep_ref, trace_ref, goal, force, spare, other):
    _, col, gz = place(me_ref, n_col)
    weight = full_ref.at[2]
    for m in range(2):
        for z in range(4):
            force[m, z] = (full_ref[m, z] - RELAX * first_ref[m, z]) * weight[z]
    sweep(first_ref, spare, force, weight)
    sweep(spare, other, force, weight)
    sweep(other, spare, force, weight)
    sweep(spare, other, force, weight)
    owner = target_ref[2 * col + gz, 5:6, :].astype(jnp.int32)
    for m in range(2):
        for k in range(2):
            keep_ref[m, k] = other[m, 2 * gz + k, H : H + 64, 0:128]
        trace_ref[m : m + 1, :] = trace_of(two_layers(other, m, gz, H, 64), owner, 0)
    nodes = target_ref.shape[2]
    line = iota((8, nodes), 0)
    at_pos = (line >= 2) & (line <= 4)
    for t in range(target_ref.shape[0]):
        info = target_ref[t]
        norm = pltpu.roll(info, 1, 0) + SOFTEN
        base = jnp.where(line == 0, norm, jnp.where(at_pos, -2.0 * info, jnp.where(line == 7, 1.0, 0.0)))
        high, middle, low = split(base)
        rows = jnp.concatenate([high, middle, high, low, high, middle], 0)
        goal[:, t * nodes : (t + 1) * nodes] = rows.astype(jnp.bfloat16)


def columns(rows, count):
    nodes = rows.shape[1]
    return [jnp.broadcast_to(rows[k : k + 1, :], (nodes, nodes)).T for k in range(count)]


def finish_apply(n_col, col, gz, acc, lined, own, out_ref):
    nodes = own.shape[1]
    lined[...] = jnp.zeros_like(lined)
    for t in range(2 * n_col):
        mine = jnp.where(2 * col + gz == t, -0.5, 0.0).astype(F32)
        for m in range(2):
            whole = jnp.sum(acc[m, t], axis=0, keepdims=True)
            lined[t + 2, m : m + 1, :] = whole + mine * own[m : m + 1, :]
    for c in range(n_col):
        for b in range(6):
            near = lined[2 * c + b]
            out_ref[2 * c, :, b * nodes : (b + 1) * nodes] = near
            out_ref[2 * c + 1, :, b * nodes : (b + 1) * nodes] = near


def build_apply(n_col, steps, me_ref, heard_ref, target_ref, goal, pair_ref, out_ref, acc, lined):
    step = pl.program_id(0)
    row, col, gz = place(me_ref, n_col)
    nodes = heard_ref.shape[2]
    blocks = target_ref.shape[0]
    group = pair_ref.shape[0]
    line = iota((8, nodes), 0)
    at_pos = (line >= 2) & (line <= 4)

    @pl.when(step == 0)
    def _():
        acc[...] = jnp.zeros_like(acc)

    starts, z_at, by = [], [], []
    for g in range(group):
        heard = heard_ref[step * group + g]
        base = jnp.where(at_pos | (line == 7), heard, jnp.where(line == 0, 1.0, 0.0))
        high, middle, low = split(base)
        starts.append(jnp.concatenate([high, high, middle, high, low, middle], 0).astype(jnp.bfloat16))
        z_at.append(columns(heard[4:5, :], 1)[0])
        by.append(columns(heard[0:2, :] * heard[6:7, :], 2))
    for g in range(group):
        for t in range(0, blocks, 2):
            squares = lax.dot_general(
                starts[g],
                goal[:, t * nodes : (t + 2) * nodes],
                (((0,), (0,)), ((), ())),
                preferred_element_type=F32,
            )
            for k in range(2):
                dz = target_ref[t + k, 4:5, :] - z_at[g]
                inverse = lax.rsqrt(squares[:, k * nodes : (k + 1) * nodes])
                pair = dz * inverse * (inverse * inverse)
                pair_ref[g, :, (t + k) * nodes : (t + k + 1) * nodes] = pair
                for m in range(2):
                    part = jnp.sum((pair * by[g][m]).reshape(nodes // 8, 8, nodes), axis=0)
                    acc[m, t + k] = acc[m, t + k] + part

    @pl.when(step == steps - 1)
    def _():
        finish_apply(n_col, col, gz, acc, lined, heard_ref[row], out_ref)


def reapply(n_col, steps, me_ref, heard_ref, info_ref, pair_ref, out_ref, acc, lined, trace):
    step = pl.program_id(0)
    row, col, gz = place(me_ref, n_col)
    nodes = heard_ref.shape[2]
    n_row = heard_ref.shape[0]

    @pl.when(step == 0)
    def _():
        acc[...] = jnp.zeros_like(acc)
        for k in range(n_row):
            whole = heard_ref[k, 0:2, :]
            if k + 1 < n_row:
                whole = whole + heard_ref[k + 1, 2:4, :]
            if k > 0:
                whole = whole + heard_ref[k - 1, 4:6, :]
            trace[k, 0:2, :] = whole
            trace[k, 2:4, :] = whole * info_ref[k, 6:7, :]

    for k in range(pair_ref.shape[0]):
        by = columns(trace[step * pair_ref.shape[0] + k, 2:4, :], 2)
        for t in range(2 * n_col):
            pair = pair_ref[k, :, t * nodes : (t + 1) * nodes]
            for m in range(2):
                acc[m, t] = acc[m, t] + jnp.sum((pair * by[m]).reshape(nodes // 8, 8, nodes), axis=0)

    @pl.when(step == steps - 1)
    def _():
        finish_apply(n_col, col, gz, acc, lined, trace[row], out_ref)


def spread_nodes(n_col, col, part_ref, target_ref, spread_ref):
    blocks = 2 * n_col
    nodes = target_ref.shape[2]
    value = part_ref[0]
    for k in range(1, blocks):
        value = value + part_ref[k]
    shape = (128, nodes)
    down = iota(shape, 0)
    weighted, lanes = [], []
    for b in range(6):
        at = jnp.clip(2 * col - 2 + b, 0, blocks - 1)
        owner = target_ref[at, 5:6, :].astype(jnp.int32)
        hit = down == owner // 128
        weighted.append(
            jnp.concatenate([jnp.where(hit, value[m : m + 1, nodes * b : nodes * (b + 1)], 0.0) for m in range(2)], 0)
        )
        lane = down == lax.rem(owner, 128)
        if b < 2:
            lane = lane & (down >= 128 - H)
        if b > 3:
            lane = lane & (down < H)
        lanes.append(jnp.where(lane, 1.0, 0.0).astype(jnp.bfloat16))

    def product(a, b):
        parts = jnp.concatenate(split(a), 0).astype(jnp.bfloat16)
        found = lax.dot_general(parts, b, (((1,), (1,)), ((), ())), preferred_element_type=F32)
        count = a.shape[0]
        return found[0:count] + (found[count : 2 * count] + found[2 * count : 3 * count])

    for g in range(2):
        own = product(weighted[2 + g], lanes[2 + g])
        side = product(
            jnp.concatenate([weighted[g], weighted[4 + g]], 1), jnp.concatenate([lanes[g], lanes[4 + g]], 1)
        )
        for m in range(2):
            for k in range(2):
                start = 128 * m + 64 * k
                spread_ref[4 * m + 2 * g + k, :, 0:128] = own[start : start + 64]
                spread_ref[4 * m + 2 * g + k, :, 128:256] = side[start : start + 64]
    return value


def respond(
    n_col, n_row, me_ref, part_ref, target_ref, full_ref, heard_ref, kept_ref,
    spread_ref, sent_ref, second_ref, force, spare, other,
):
    row, col, gz = place(me_ref, n_col)
    weight = full_ref.at[2]
    spread_nodes(n_col, col, part_ref, target_ref, spread_ref)
    empty = jnp.zeros((H, 256), F32)
    for m in range(2):
        for z in range(4):
            force[m, z, 0:H, :] = empty
            force[m, z, H : H + 64, :] = spread_ref[4 * m + z] * weight[z, H : H + 64]
            force[m, z, H + 64 : 2 * H + 64, :] = empty
    sweep(force, spare, force, weight)
    sweep(spare, other, force, weight)
    sweep(other, second_ref, force, weight)
    for m in range(2):
        for z in range(4):
            force[m, z] = (-RELAX * second_ref[m, z]) * weight[z]
    sweep(force, other, force, weight)
    sweep(other, spare, force, weight)
    sweep(spare, other, force, weight)
    own = heard_ref[row, 5:6, :].astype(jnp.int32)
    above = heard_ref[jnp.maximum(row - 1, 0), 5:6, :].astype(jnp.int32)
    below = heard_ref[jnp.minimum(row + 1, n_row - 1), 5:6, :].astype(jnp.int32)
    line = iota((8, own.shape[1]), 0)
    sent = jnp.zeros((8, own.shape[1]), F32)
    for m in range(2):
        here = trace_of(two_layers(other, m, gz, H, 64), own, 0) + kept_ref[m : m + 1, :]
        sent = jnp.where(line == m, here, sent)
        sent = jnp.where(line == 2 + m, trace_of(two_layers(other, m, gz, 0, H), above, 64 - H), sent)
        sent = jnp.where(line == 4 + m, trace_of(two_layers(other, m, gz, H + 64, H), below, 0), sent)
    for k in range(sent_ref.shape[0]):
        sent_ref[k] = sent


def last_spread(n_col, me_ref, part_ref, target_ref, before_ref, spread_ref, a_ref, b_ref, value_ref):
    row, col, gz = place(me_ref, n_col)
    value = spread_nodes(n_col, col, part_ref, target_ref, spread_ref)
    odd = lax.rem(row, 2)
    for edge_ref, last in ((a_ref, 1 - odd), (b_ref, odd)):
        write_edges(edge_ref, 0, before_ref, 8, last)
        near = near_half(last)
        side = jnp.zeros((H, 128), F32)
        for s in range(0, 8, 2):
            one, two = edge_row(spread_ref, s, last), edge_row(spread_ref, s + 1, last)
            edge_ref[9 + s // 2] = jnp.where(near, one[:, 0:128], pltpu.roll(two[:, 0:128], 4, 0))
            side = tuck(one[:, 128:256], s, side)
            side = tuck(two[:, 128:256], s + 1, side)
        edge_ref[13] = side
    for m in range(2):
        value_ref[m : m + 1, :] = pick(
            gz,
            (1, value_ref.shape[1]),
            value[m : m + 1, 3 * value_ref.shape[1] : 4 * value_ref.shape[1]],
            value[m : m + 1, 2 * value_ref.shape[1] : 3 * value_ref.shape[1]],
        )


def own_relax(n_col, me_ref, full_ref, second_ref, spread_ref, keep_ref, out_ref, force, spare, other):
    _, _, gz = place(me_ref, n_col)
    weight = full_ref.at[2]
    for m in range(2):
        for z in range(4):
            force[m, z] = (-RELAX * second_ref[m, z]) * weight[z]
            mid = force[m, z, H : H + 64, :]
            force[m, z, H : H + 64, :] = mid + spread_ref[4 * m + z] * weight[z, H : H + 64]
    sweep(second_ref, spare, force, weight)
    sweep(spare, other, force, weight)
    sweep(other, spare, force, weight)
    sweep(spare, other, force, weight)
    for m in range(2):
        for k in range(2):
            out_ref[m, k] = keep_ref[m, k] + other[m, 2 * gz + k, H : H + 64, 0:128]


def last_relax(
    n_col, me_ref, full_ref, a_in, b_in, part_ref, out_ref, weight, force, later, spare, other
):
    row, _, gz = place(me_ref, n_col)
    odd = lax.rem(row, 2)
    empty = jnp.zeros((2 * H, 256), F32)
    for z in range(4):
        weight[z, 0 : 2 * H] = full_ref[2, z, 0 : 2 * H]
        weight[z, 2 * H : 4 * H] = full_ref[2, z, 64 : 64 + 2 * H]
    for s in range(8):
        m, z = s // 4, s % 4
        top, bottom = halo_rows(read_edge(a_in, 0, s, 8), read_edge(b_in, 0, s, 8), odd)
        force[m, z, 0:H] = top * weight[z, 0:H]
        force[m, z, H : 3 * H] = empty
        force[m, z, 3 * H : 4 * H] = bottom * weight[z, 3 * H : 4 * H]
        ends = []
        for ref, last in ((a_in, odd), (b_in, 1 - odd)):
            tile = ref[9 + s // 2]
            main = jnp.where(near_half(last), pltpu.roll(tile, 4, 0) if s % 2 else tile, 0.0)
            ends.append(jnp.concatenate([main, untuck(ref[13], s)], 1))
        top, bottom = halo_rows(ends[0], ends[1], odd)
        later[m, z, 0:H] = top * weight[z, 0:H]
        later[m, z, H : 3 * H] = empty
        later[m, z, 3 * H : 4 * H] = bottom * weight[z, 3 * H : 4 * H]
    sweep(force, spare, force, weight)
    sweep(spare, other, force, weight)
    sweep(other, spare, force, weight)
    for m in range(2):
        for z in range(4):
            later[m, z] = later[m, z] - (RELAX * spare[m, z]) * weight[z]
    sweep(spare, other, later, weight)
    sweep(other, spare, later, weight)
    sweep(spare, other, later, weight)
    sweep(other, spare, later, weight)
    for m in range(2):
        for k in range(2):
            found = spare.at[m, 2 * gz + k]
            out_ref[m, k, 0:H, :] = part_ref[m, k, 0:H, :] + found[H : 2 * H, 0:128]
            out_ref[m, k, H : 64 - H, :] = part_ref[m, k, H : 64 - H, :]
            out_ref[m, k, 64 - H : 64, :] = part_ref[m, k, 64 - H : 64, :] + found[2 * H : 3 * H, 0:128]


SMEM = pl.BlockSpec(memory_space=pltpu.SMEM)
VMEM = pl.BlockSpec(memory_space=pltpu.VMEM)


def size_of(shape):
    return functools.reduce(lambda a, b: a * b, shape)


def run(body, outs, args, scratch=(), flops=0, scalars=1):
    moved = sum(a.size * 4 for a in args) + sum(4 * size_of(o) for o in outs)
    return pl.pallas_call(
        body,
        out_shape=[jax.ShapeDtypeStruct(o, F32) for o in outs],
        in_specs=[SMEM] * scalars + [VMEM] * (len(args) - scalars),
        out_specs=[VMEM] * len(outs),
        scratch_shapes=[pltpu.VMEM(s, F32) for s in scratch],
        compiler_params=pltpu.CompilerParams(vmem_limit_bytes=20 << 20),
        cost_estimate=pl.CostEstimate(flops=flops, bytes_accessed=moved, transcendentals=0),
    )(*args)


def on_device(n_row, n_col, source, cell_class, coeff_table, owner_cell, node_pos, node_weight):
    nodes = owner_cell.shape[0]
    blocks = 2 * n_col
    me = lax.axis_index(("row", "col", "gz")).reshape(1)

    def swaps(axis, size, a, b):
        first = [(i, i ^ 1) for i in range(size)]
        second = [(i + 1, i + 2) for i in range(0, size - 2, 2)]
        second = second + [(j, i) for i, j in second]
        a = lax.ppermute(a, axis, first)
        b = lax.ppermute(b, axis, second)
        return a, b

    packed, told = pl.pallas_call(
        prepare,
        name="prepare",
        out_shape=[jax.ShapeDtypeStruct(o, F32) for o in ((3, 2, 64, 128), (blocks, 8, nodes))],
        in_specs=[pl.BlockSpec(memory_space=pl.ANY)] * 6,
        out_specs=[VMEM] * 2,
        scratch_shapes=[
            pltpu.SMEM(coeff_table.shape, F32),
            pltpu.VMEM(cell_class.shape, jnp.int32),
            pltpu.VMEM((1, nodes), jnp.int32),
            pltpu.VMEM((3, nodes), F32),
            pltpu.VMEM((1, nodes), F32),
            pltpu.SemaphoreType.DMA((6,)),
        ],
        compiler_params=pltpu.CompilerParams(vmem_limit_bytes=60 << 20),
    )(coeff_table, source, cell_class, owner_cell[None, :], node_pos, node_weight[None, :])
    other = lax.ppermute(packed, "gz", [(0, 1), (1, 0)])
    target = lax.all_to_all(told, ("col", "gz"), 0, 0)
    (packed,) = run(stage, [packed.shape], [packed], scalars=0)
    a, b = run(functools.partial(col_pack, n_col), [(64, 128)] * 2, [me, packed, other])
    a, b = swaps("col", n_col, a, b)
    ext, a, b = run(
        functools.partial(row_pack, n_col), [(12, 64, 256), (14, H, 128), (14, H, 128)], [me, packed, other, a, b]
    )
    a, b = swaps("row", n_row, a, b)

    field = (2, 4, 64 + 2 * H, 256)
    full, first, sent = run(
        functools.partial(first_relax, n_col),
        [(3, 4, 64 + 2 * H, 256), field, (n_row, 8, nodes)],
        [me, ext, a, b, target],
        [field] * 2,
    )
    heard = lax.all_to_all(sent, "row", 0, 0)
    keep, kept, goal = pl.pallas_call(
        functools.partial(carry_relax, n_col),
        name="carry_relax",
        out_shape=[
            jax.ShapeDtypeStruct((2, 2, 64, 128), F32),
            jax.ShapeDtypeStruct((2, nodes), F32),
            jax.ShapeDtypeStruct((48, blocks * nodes), jnp.bfloat16),
        ],
        in_specs=[SMEM] + [VMEM] * 3,
        out_specs=[VMEM] * 3,
        scratch_shapes=[pltpu.VMEM(field, F32)] * 3,
        compiler_params=pltpu.CompilerParams(vmem_limit_bytes=20 << 20),
        cost_estimate=pl.CostEstimate(
            flops=40 * size_of(field), bytes_accessed=4 * size_of(field), transcendentals=0
        ),
    )(me, full, first, target)

    everything = lambda shape: pl.BlockSpec(shape, lambda i: (0,) * len(shape))
    work = n_row * blocks * nodes * nodes
    sums = [pltpu.VMEM((2, blocks, 8, nodes), F32), pltpu.VMEM((blocks + 4, 2, nodes), F32)]
    group = min(4, n_row)
    pairs, partial = pl.pallas_call(
        functools.partial(build_apply, n_col, n_row // group),
        name="build_apply",
        grid=(n_row // group,),
        out_shape=[
            jax.ShapeDtypeStruct((n_row, nodes, blocks * nodes), F32),
            jax.ShapeDtypeStruct((blocks, 2, 6 * nodes), F32),
        ],
        in_specs=[SMEM, everything((n_row, 8, nodes)), everything((blocks, 8, nodes)), everything((48, blocks * nodes))],
        out_specs=[
            pl.BlockSpec((group, nodes, blocks * nodes), lambda i: (i, 0, 0)),
            everything((blocks, 2, 6 * nodes)),
        ],
        scratch_shapes=sums,
        compiler_params=pltpu.CompilerParams(vmem_limit_bytes=16 << 20),
        cost_estimate=pl.CostEstimate(flops=18 * work, bytes_accessed=4 * work, transcendentals=work),
    )(me, heard, target, goal)
    partial = lax.all_to_all(partial, ("col", "gz"), 0, 0)
    before, sent, second = run(
        functools.partial(respond, n_col, n_row),
        [(8, 64, 256), (n_row, 8, nodes), field],
        [me, partial, target, full, heard, kept],
        [field] * 3,
    )
    again = lax.all_to_all(sent, "row", 0, 0)
    partial = pl.pallas_call(
        functools.partial(reapply, n_col, n_row // group),
        name="reapply",
        grid=(n_row // group,),
        out_shape=jax.ShapeDtypeStruct((blocks, 2, 6 * nodes), F32),
        in_specs=[
            SMEM,
            everything((n_row, 8, nodes)),
            everything((n_row, 8, nodes)),
            pl.BlockSpec((group, nodes, blocks * nodes), lambda i: (i, 0, 0)),
        ],
        out_specs=everything((blocks, 2, 6 * nodes)),
        scratch_shapes=sums + [pltpu.VMEM((n_row, 8, nodes), F32)],
        compiler_params=pltpu.CompilerParams(vmem_limit_bytes=20 << 20),
        cost_estimate=pl.CostEstimate(flops=4 * work, bytes_accessed=4 * work, transcendentals=0),
    )(me, again, heard, pairs)
    partial = lax.all_to_all(partial, ("col", "gz"), 0, 0)
    spread, a, b, values = run(
        functools.partial(last_spread, n_col),
        [(8, 64, 256), (14, H, 128), (14, H, 128), (2, nodes)],
        [me, partial, target, before],
    )
    a, b = swaps("row", n_row, a, b)
    (part,) = run(
        functools.partial(own_relax, n_col),
        [(2, 2, 64, 128)],
        [me, full, second, spread, keep],
        [field] * 3,
        flops=40 * size_of(field),
    )
    strip = (2, 4, 4 * H, 256)
    (potential,) = run(
        functools.partial(last_relax, n_col), [(2, 2, 64, 128)], [me, full, a, b, part], [strip[1:]] + [strip] * 4
    )
    return potential, values


def solution(mesh):
    return jax.shard_map(
        functools.partial(on_device, mesh.shape["row"], mesh.shape["col"]),
        mesh=mesh,
        in_specs=(
            P(None, "gz", "row", "col"),
            P("gz", "row", "col"),
            P(),
            P(("row", "col", "gz")),
            P(None, ("row", "col", "gz")),
            P(("row", "col", "gz")),
        ),
        out_specs=(P(None, "gz", "row", "col"), P(None, ("row", "col", "gz"))),
        check_vma=False,
    )
```

```python
import functools

import jax
import jax.numpy as jnp
from jax import lax
from jax.experimental import pallas as pl
from jax.experimental.pallas import tpu as pltpu
from jax.sharding import PartitionSpec as P


OMEGA = 0.8
RELAX = 0.5
SOFTEN = 0.01
H = 8
F32 = jnp.float32


def iota(shape, axis):
    return lax.broadcasted_iota(jnp.int32, shape, axis)


def pick(flag, shape, yes, no):
    return jnp.where(jnp.full(shape, flag, jnp.int32) == 1, yes, no)


def place(me_ref, n_col):
    me = me_ref[0]
    gz = lax.rem(me, 2)
    col = lax.rem(me // 2, n_col)
    row = me // (2 * n_col)
    return row, col, gz


def layer_of(own_ref, other_ref, kind, z, gz, shape):
    mine = pick(gz, shape, 1, 0) == z // 2
    return jnp.where(mine, own_ref[kind, z % 2], other_ref[kind, z % 2])


def col_pack(n_col, me_ref, own_ref, other_ref, a_ref, b_ref):
    _, col, gz = place(me_ref, n_col)
    shape = own_ref.shape[2:]
    lane = iota(shape, 1)
    left = jnp.zeros(shape, F32)
    right = jnp.zeros(shape, F32)
    for s in range(12):
        cell = layer_of(own_ref, other_ref, s // 4, s % 4, gz, shape)
        here = (lane >= 8 * s) & (lane < 8 * s + 8)
        low = pltpu.roll(cell, 8 * s, 1) if s else cell
        left = jnp.where(here, low, left)
        right = jnp.where(here, pltpu.roll(cell, 8 * s + 8, 1), right)
    odd = lax.rem(col, 2)
    a_ref[...] = pick(odd, shape, left, right)
    b_ref[...] = pick(odd, shape, right, left)


def edge_row(from_ref, s, last):
    rows, lanes = from_ref.shape[1:]
    return pick(last, (H, lanes), from_ref[s, rows - H : rows, :], from_ref[s, 0:H, :])


def tuck(side, s, into):
    lane = iota(side.shape, 1)
    moved = pltpu.roll(side, (16 * s + 8) % 128, 1)
    return jnp.where((lane >= 16 * s) & (lane < 16 * s + 16), moved, into)


def untuck(tile, s):
    lane = iota(tile.shape, 1)
    moved = pltpu.roll(tile, (128 - 16 * s - 8) % 128, 1)
    return jnp.where((lane < 8) | (lane >= 120), moved, 0.0)


def write_edges(edge_ref, start, from_ref, count, last):
    for first in range(0, count, 8):
        side = jnp.zeros((H, 128), F32)
        for s in range(first, min(first + 8, count)):
            edge = edge_row(from_ref, s, last)
            edge_ref[start + s] = edge[:, 0:128]
            side = tuck(edge[:, 128:256], s - first, side)
        edge_ref[start + count + first // 8] = side


def read_edge(ref, start, s, count):
    return jnp.concatenate([ref[start + s], untuck(ref[start + count + s // 8], s % 8)], 1)


def near_half(last):
    return (iota((H, 128), 0) // 4) == jnp.full((H, 128), last, jnp.int32)


def halo_rows(a, b, odd):
    return pick(odd, a.shape, a, b), pick(odd, a.shape, b, a)


def row_pack(n_col, me_ref, own_ref, other_ref, a_in, b_in, ext_ref, a_ref, b_ref):
    row, col, gz = place(me_ref, n_col)
    shape = own_ref.shape[2:]
    _, lanes = shape
    lane = iota(shape, 1)
    odd_col = lax.rem(col, 2)
    from_right = pick(odd_col, shape, b_in[...], a_in[...])
    from_left = pick(odd_col, shape, a_in[...], b_in[...])
    for s in range(12):
        cell = layer_of(own_ref, other_ref, s // 4, s % 4, gz, shape)
        low = pltpu.roll(from_right, lanes - 8 * s, 1) if s else from_right
        high = pltpu.roll(from_left, lanes - 8 - 8 * s, 1)
        side = jnp.where(lane < 8, low, jnp.where(lane >= lanes - 8, high, 0.0))
        ext_ref[s, :, 0:lanes] = cell
        ext_ref[s, :, lanes : 2 * lanes] = side
    odd = lax.rem(row, 2)
    write_edges(a_ref, 0, ext_ref, 12, 1 - odd)
    write_edges(b_ref, 0, ext_ref, 12, odd)


def sweep(now_ref, next_ref, force_ref, weight_ref):
    rows, lanes = now_ref.shape[2:]
    line = iota((8, lanes), 0)

    def one(m, z, low, high):
        tiles = rows // 8
        cells = [now_ref[m, z, 8 * i : 8 * i + 8, :] for i in range(tiles)]
        downs = [pltpu.roll(cell, 1, 0) for cell in cells]
        ups = [pltpu.roll(cell, 7, 0) for cell in cells]
        for i in range(tiles):
            beside = jnp.where(line == 0, downs[i - 1], downs[i]) + jnp.where(line == 7, ups[(i + 1) % tiles], ups[i])
            beside = beside + (pltpu.roll(cells[i], 1, 1) + pltpu.roll(cells[i], lanes - 1, 1))
            at = slice(8 * i, 8 * i + 8)
            if low is not None:
                beside = beside + now_ref[m, low, at, :]
            if high is not None:
                beside = beside + now_ref[m, high, at, :]
            next_ref[m, z, at, :] = (1.0 - OMEGA) * cells[i] + (force_ref[m, z, at, :] + weight_ref[z, at, :] * beside)

    def image(m, carry):
        for z in range(4):
            one(m, z, z - 1 if z > 0 else None, z + 1 if z < 3 else None)
        return carry

    lax.fori_loop(0, now_ref.shape[0], image, 0, unroll=rows < 64)


def split(x):
    high = x.astype(jnp.bfloat16).astype(F32)
    rest = x - high
    middle = rest.astype(jnp.bfloat16).astype(F32)
    return high, middle, rest - middle


def trace_of(rows, owner, first_row):
    span = rows.shape[0] // 2
    nodes = owner.shape[1]
    line = iota((2 * span, nodes), 0)
    line = line + first_row + jnp.where(line >= span, 64 - span, 0)
    at_row = jnp.where(line == owner // 128, 1.0, 0.0).astype(jnp.bfloat16)
    at_lane = iota((128, nodes), 0) == lax.rem(owner, 128)
    found = sum(
        lax.dot_general(
            part.astype(jnp.bfloat16), at_row, (((0,), (0,)), ((), ())), preferred_element_type=F32
        )
        for part in split(rows)
    )
    return jnp.sum(jnp.where(at_lane, found, 0.0), axis=0, keepdims=True)


def two_layers(field_ref, m, gz, start, size):
    return jnp.concatenate([field_ref[m, 2 * gz + k, start : start + size, 0:128] for k in range(2)], 0)


def prepare(
    table_hbm, source_hbm, class_hbm, owner_hbm, pos_hbm, node_hbm, pack_ref, told_ref,
    table, level_ref, owner_ref, pos_ref, node_ref, sems,
):
    moves = [
        (class_hbm, level_ref),
        (table_hbm, table),
        (owner_hbm, owner_ref),
        (pos_hbm, pos_ref),
        (node_hbm, node_ref),
        (source_hbm, pack_ref.at[0:2]),
    ]
    copies = [pltpu.make_async_copy(a, b, sems.at[k]) for k, (a, b) in enumerate(moves)]
    for copy in copies:
        copy.start()
    for copy in copies:
        copy.wait()
    for k in range(2):
        level = level_ref[k]
        found = jnp.zeros(level.shape, F32)
        for n in range(table.shape[0]):
            found = jnp.where(level == n, table[n], found)
        pack_ref[2, k] = OMEGA / (6.0 + found)
    told_ref[0] = jnp.zeros(told_ref.shape[1:], F32)
    centred = pos_ref[...] - 0.5
    told_ref[0, 2:5, :] = centred
    told_ref[0, 5:6, :] = owner_ref[...].astype(F32)
    told_ref[0, 6:7, :] = node_ref[...]
    told_ref[0, 7:8, :] = jnp.sum(centred * centred, axis=0, keepdims=True)
    for k in range(1, told_ref.shape[0]):
        told_ref[k] = told_ref[0]


def stage(own_ref, out_ref):
    out_ref[...] = own_ref[...]


def first_relax(n_col, me_ref, ext_ref, a_in, b_in, target_ref, full_ref, first_ref, sent_ref, force, spare):
    row, col, gz = place(me_ref, n_col)
    odd = lax.rem(row, 2)
    for s in range(12):
        top, bottom = halo_rows(read_edge(a_in, 0, s, 12), read_edge(b_in, 0, s, 12), odd)
        full_ref[s // 4, s % 4, 0:H, :] = top
        full_ref[s // 4, s % 4, H : H + 64, :] = ext_ref[s]
        full_ref[s // 4, s % 4, H + 64 : 2 * H + 64, :] = bottom
    weight = full_ref.at[2]
    for m in range(2):
        for z in range(4):
            force[m, z] = full_ref[m, z] * weight[z]
    sweep(force, first_ref, force, weight)
    sweep(first_ref, spare, force, weight)
    sweep(spare, first_ref, force, weight)
    info = target_ref[2 * col + gz]
    owner = info[5:6, :].astype(jnp.int32)
    line = iota(info.shape, 0)
    for m in range(2):
        info = jnp.where(line == m, trace_of(two_layers(first_ref, m, gz, H, 64), owner, 0), info)
    for k in range(sent_ref.shape[0]):
        sent_ref[k] = info


def carry_relax(
    n_col, me_ref, full_ref, first_ref, target_ref, ready_ref,
    keep_ref, trace_ref, goal, sent_ref, force, spare, other,
):
    _, col, gz = place(me_ref, n_col)
    weight = full_ref.at[2]
    for m in range(2):
        for z in range(4):
            force[m, z] = (full_ref[m, z] - RELAX * first_ref[m, z]) * weight[z]
    sweep(first_ref, spare, force, weight)
    sweep(spare, other, force, weight)
    sweep(other, spare, force, weight)
    sweep(spare, other, force, weight)
    owner = target_ref[2 * col + gz, 5:6, :].astype(jnp.int32)
    for m in range(2):
        for k in range(2):
            keep_ref[m, k] = other[m, 2 * gz + k, H : H + 64, 0:128]
        trace_ref[m : m + 1, :] = trace_of(two_layers(other, m, gz, H, 64), owner, 0)
    sent_ref[...] = ready_ref[...]
    nodes = target_ref.shape[2]
    line = iota((8, nodes), 0)
    at_pos = (line >= 2) & (line <= 4)
    for t in range(target_ref.shape[0]):
        info = target_ref[t]
        norm = pltpu.roll(info, 1, 0) + SOFTEN
        base = jnp.where(line == 0, norm, jnp.where(at_pos, -2.0 * info, jnp.where(line == 7, 1.0, 0.0)))
        high, middle, low = split(base)
        rows = jnp.concatenate([high, middle, high, low, high, middle], 0)
        goal[:, t * nodes : (t + 1) * nodes] = rows.astype(jnp.bfloat16)


def columns(rows, count):
    nodes = rows.shape[1]
    return [jnp.broadcast_to(rows[k : k + 1, :], (nodes, nodes)).T for k in range(count)]


def finish_apply(n_col, col, gz, acc, lined, own, out_ref):
    nodes = own.shape[1]
    lined[...] = jnp.zeros_like(lined)
    for t in range(2 * n_col):
        mine = jnp.where(2 * col + gz == t, -0.5, 0.0).astype(F32)
        for m in range(2):
            whole = jnp.sum(acc[m, t], axis=0, keepdims=True)
            lined[t + 2, m : m + 1, :] = whole + mine * own[m : m + 1, :]
    for c in range(n_col):
        for b in range(6):
            near = lined[2 * c + b]
            out_ref[2 * c, :, b * nodes : (b + 1) * nodes] = near
            out_ref[2 * c + 1, :, b * nodes : (b + 1) * nodes] = near


def build_apply(n_col, steps, me_ref, heard_ref, target_ref, goal, pair_ref, out_ref, acc, lined):
    step = pl.program_id(0)
    row, col, gz = place(me_ref, n_col)
    nodes = heard_ref.shape[2]
    blocks = target_ref.shape[0]
    group = pair_ref.shape[0]
    line = iota((8, nodes), 0)
    at_pos = (line >= 2) & (line <= 4)

    @pl.when(step == 0)
    def _():
        acc[...] = jnp.zeros_like(acc)

    starts, z_at, by = [], [], []
    for g in range(group):
        heard = heard_ref[step * group + g]
        base = jnp.where(at_pos | (line == 7), heard, jnp.where(line == 0, 1.0, 0.0))
        high, middle, low = split(base)
        starts.append(jnp.concatenate([high, high, middle, high, low, middle], 0).astype(jnp.bfloat16))
        z_at.append(columns(heard[4:5, :], 1)[0])
        by.append(columns(heard[0:2, :] * heard[6:7, :], 2))
    for g in range(group):
        for t in range(0, blocks, 2):
            squares = lax.dot_general(
                starts[g],
                goal[:, t * nodes : (t + 2) * nodes],
                (((0,), (0,)), ((), ())),
                preferred_element_type=F32,
            )
            for k in range(2):
                dz = target_ref[t + k, 4:5, :] - z_at[g]
                inverse = lax.rsqrt(squares[:, k * nodes : (k + 1) * nodes])
                pair = dz * inverse * (inverse * inverse)
                pair_ref[g, :, (t + k) * nodes : (t + k + 1) * nodes] = pair
                for m in range(2):
                    part = jnp.sum((pair * by[g][m]).reshape(nodes // 8, 8, nodes), axis=0)
                    acc[m, t + k] = acc[m, t + k] + part

    @pl.when(step == steps - 1)
    def _():
        finish_apply(n_col, col, gz, acc, lined, heard_ref[row], out_ref)


def reapply(n_col, steps, me_ref, heard_ref, info_ref, pair_ref, out_ref, acc, lined, trace):
    step = pl.program_id(0)
    row, col, gz = place(me_ref, n_col)
    nodes = heard_ref.shape[2]
    n_row = heard_ref.shape[0]

    @pl.when(step == 0)
    def _():
        acc[...] = jnp.zeros_like(acc)
        for k in range(n_row):
            whole = heard_ref[k, 0:2, :]
            if k + 1 < n_row:
                whole = whole + heard_ref[k + 1, 2:4, :]
            if k > 0:
                whole = whole + heard_ref[k - 1, 4:6, :]
            trace[k, 0:2, :] = whole
            trace[k, 2:4, :] = whole * info_ref[k, 6:7, :]

    for k in range(pair_ref.shape[0]):
        by = columns(trace[step * pair_ref.shape[0] + k, 2:4, :], 2)
        for t in range(2 * n_col):
            pair = pair_ref[k, :, t * nodes : (t + 1) * nodes]
            for m in range(2):
                acc[m, t] = acc[m, t] + jnp.sum((pair * by[m]).reshape(nodes // 8, 8, nodes), axis=0)

    @pl.when(step == steps - 1)
    def _():
        finish_apply(n_col, col, gz, acc, lined, trace[row], out_ref)


def spread_nodes(n_col, col, part_ref, target_ref, spread_ref):
    blocks = 2 * n_col
    nodes = target_ref.shape[2]
    value = part_ref[0]
    for k in range(1, blocks):
        value = value + part_ref[k]
    shape = (128, nodes)
    down = iota(shape, 0)
    weighted, lanes = [], []
    for b in range(6):
        at = jnp.clip(2 * col - 2 + b, 0, blocks - 1)
        owner = target_ref[at, 5:6, :].astype(jnp.int32)
        hit = down == owner // 128
        weighted.append(
            jnp.concatenate([jnp.where(hit, value[m : m + 1, nodes * b : nodes * (b + 1)], 0.0) for m in range(2)], 0)
        )
        lane = down == lax.rem(owner, 128)
        if b < 2:
            lane = lane & (down >= 128 - H)
        if b > 3:
            lane = lane & (down < H)
        lanes.append(jnp.where(lane, 1.0, 0.0).astype(jnp.bfloat16))

    def product(a, b):
        parts = jnp.concatenate(split(a), 0).astype(jnp.bfloat16)
        found = lax.dot_general(parts, b, (((1,), (1,)), ((), ())), preferred_element_type=F32)
        count = a.shape[0]
        return found[0:count] + (found[count : 2 * count] + found[2 * count : 3 * count])

    for g in range(2):
        own = product(weighted[2 + g], lanes[2 + g])
        side = product(
            jnp.concatenate([weighted[g], weighted[4 + g]], 1), jnp.concatenate([lanes[g], lanes[4 + g]], 1)
        )
        for m in range(2):
            for k in range(2):
                start = 128 * m + 64 * k
                spread_ref[4 * m + 2 * g + k, :, 0:128] = own[start : start + 64]
                spread_ref[4 * m + 2 * g + k, :, 128:256] = side[start : start + 64]
    return value


def respond(
    n_col, n_row, me_ref, part_ref, target_ref, full_ref, heard_ref, kept_ref,
    spread_ref, sent_ref, second_ref, force, spare, other,
):
    row, col, gz = place(me_ref, n_col)
    weight = full_ref.at[2]
    spread_nodes(n_col, col, part_ref, target_ref, spread_ref)
    empty = jnp.zeros((H, 256), F32)
    for m in range(2):
        for z in range(4):
            force[m, z, 0:H, :] = empty
            force[m, z, H : H + 64, :] = spread_ref[4 * m + z] * weight[z, H : H + 64]
            force[m, z, H + 64 : 2 * H + 64, :] = empty
    sweep(force, spare, force, weight)
    sweep(spare, other, force, weight)
    sweep(other, second_ref, force, weight)
    for m in range(2):
        for z in range(4):
            force[m, z] = (-RELAX * second_ref[m, z]) * weight[z]
    sweep(force, other, force, weight)
    sweep(other, spare, force, weight)
    sweep(spare, other, force, weight)
    own = heard_ref[row, 5:6, :].astype(jnp.int32)
    above = heard_ref[jnp.maximum(row - 1, 0), 5:6, :].astype(jnp.int32)
    below = heard_ref[jnp.minimum(row + 1, n_row - 1), 5:6, :].astype(jnp.int32)
    line = iota((8, own.shape[1]), 0)
    sent = jnp.zeros((8, own.shape[1]), F32)
    for m in range(2):
        here = trace_of(two_layers(other, m, gz, H, 64), own, 0) + kept_ref[m : m + 1, :]
        sent = jnp.where(line == m, here, sent)
        sent = jnp.where(line == 2 + m, trace_of(two_layers(other, m, gz, 0, H), above, 64 - H), sent)
        sent = jnp.where(line == 4 + m, trace_of(two_layers(other, m, gz, H + 64, H), below, 0), sent)
    for k in range(sent_ref.shape[0]):
        sent_ref[k] = sent


def last_spread(n_col, me_ref, part_ref, target_ref, before_ref, spread_ref, a_ref, b_ref, value_ref):
    row, col, gz = place(me_ref, n_col)
    value = spread_nodes(n_col, col, part_ref, target_ref, spread_ref)
    odd = lax.rem(row, 2)
    for edge_ref, last in ((a_ref, 1 - odd), (b_ref, odd)):
        write_edges(edge_ref, 0, before_ref, 8, last)
        near = near_half(last)
        side = jnp.zeros((H, 128), F32)
        for s in range(0, 8, 2):
            one, two = edge_row(spread_ref, s, last), edge_row(spread_ref, s + 1, last)
            edge_ref[9 + s // 2] = jnp.where(near, one[:, 0:128], pltpu.roll(two[:, 0:128], 4, 0))
            side = tuck(one[:, 128:256], s, side)
            side = tuck(two[:, 128:256], s + 1, side)
        edge_ref[13] = side
    for m in range(2):
        value_ref[m : m + 1, :] = pick(
            gz,
            (1, value_ref.shape[1]),
            value[m : m + 1, 3 * value_ref.shape[1] : 4 * value_ref.shape[1]],
            value[m : m + 1, 2 * value_ref.shape[1] : 3 * value_ref.shape[1]],
        )


def own_relax(n_col, me_ref, full_ref, second_ref, spread_ref, keep_ref, out_ref, force, spare, other):
    _, _, gz = place(me_ref, n_col)
    weight = full_ref.at[2]
    for m in range(2):
        for z in range(4):
            force[m, z] = (-RELAX * second_ref[m, z]) * weight[z]
            mid = force[m, z, H : H + 64, :]
            force[m, z, H : H + 64, :] = mid + spread_ref[4 * m + z] * weight[z, H : H + 64]
    sweep(second_ref, spare, force, weight)
    sweep(spare, other, force, weight)
    sweep(other, spare, force, weight)
    sweep(spare, other, force, weight)
    for m in range(2):
        for k in range(2):
            out_ref[m, k] = keep_ref[m, k] + other[m, 2 * gz + k, H : H + 64, 0:128]


def last_relax(
    n_col, me_ref, full_ref, a_in, b_in, part_ref, out_ref, weight, force, later, spare, other
):
    row, _, gz = place(me_ref, n_col)
    odd = lax.rem(row, 2)
    empty = jnp.zeros((2 * H, 256), F32)
    for z in range(4):
        weight[z, 0 : 2 * H] = full_ref[2, z, 0 : 2 * H]
        weight[z, 2 * H : 4 * H] = full_ref[2, z, 64 : 64 + 2 * H]
    for s in range(8):
        m, z = s // 4, s % 4
        top, bottom = halo_rows(read_edge(a_in, 0, s, 8), read_edge(b_in, 0, s, 8), odd)
        force[m, z, 0:H] = top * weight[z, 0:H]
        force[m, z, H : 3 * H] = empty
        force[m, z, 3 * H : 4 * H] = bottom * weight[z, 3 * H : 4 * H]
        ends = []
        for ref, last in ((a_in, odd), (b_in, 1 - odd)):
            tile = ref[9 + s // 2]
            main = jnp.where(near_half(last), pltpu.roll(tile, 4, 0) if s % 2 else tile, 0.0)
            ends.append(jnp.concatenate([main, untuck(ref[13], s)], 1))
        top, bottom = halo_rows(ends[0], ends[1], odd)
        later[m, z, 0:H] = top * weight[z, 0:H]
        later[m, z, H : 3 * H] = empty
        later[m, z, 3 * H : 4 * H] = bottom * weight[z, 3 * H : 4 * H]
    sweep(force, spare, force, weight)
    sweep(spare, other, force, weight)
    sweep(other, spare, force, weight)
    for m in range(2):
        for z in range(4):
            later[m, z] = later[m, z] - (RELAX * spare[m, z]) * weight[z]
    sweep(spare, other, later, weight)
    sweep(other, spare, later, weight)
    sweep(spare, other, later, weight)
    sweep(other, spare, later, weight)
    for m in range(2):
        for k in range(2):
            found = spare.at[m, 2 * gz + k]
            out_ref[m, k, 0:H, :] = part_ref[m, k, 0:H, :] + found[H : 2 * H, 0:128]
            out_ref[m, k, H : 64 - H, :] = part_ref[m, k, H : 64 - H, :]
            out_ref[m, k, 64 - H : 64, :] = part_ref[m, k, 64 - H : 64, :] + found[2 * H : 3 * H, 0:128]


SMEM = pl.BlockSpec(memory_space=pltpu.SMEM)
VMEM = pl.BlockSpec(memory_space=pltpu.VMEM)


def size_of(shape):
    return functools.reduce(lambda a, b: a * b, shape)


def run(body, outs, args, scratch=(), flops=0, scalars=1):
    moved = sum(a.size * 4 for a in args) + sum(4 * size_of(o) for o in outs)
    return pl.pallas_call(
        body,
        out_shape=[jax.ShapeDtypeStruct(o, F32) for o in outs],
        in_specs=[SMEM] * scalars + [VMEM] * (len(args) - scalars),
        out_specs=[VMEM] * len(outs),
        scratch_shapes=[pltpu.VMEM(s, F32) for s in scratch],
        compiler_params=pltpu.CompilerParams(vmem_limit_bytes=20 << 20),
        cost_estimate=pl.CostEstimate(flops=flops, bytes_accessed=moved, transcendentals=0),
    )(*args)


def on_device(n_row, n_col, source, cell_class, coeff_table, owner_cell, node_pos, node_weight):
    nodes = owner_cell.shape[0]
    blocks = 2 * n_col
    me = lax.axis_index(("row", "col", "gz")).reshape(1)

    def swaps(axis, size, a, b):
        first = [(i, i ^ 1) for i in range(size)]
        second = [(i + 1, i + 2) for i in range(0, size - 2, 2)]
        second = second + [(j, i) for i, j in second]
        a = lax.ppermute(a, axis, first)
        b = lax.ppermute(b, axis, second)
        return a, b

    packed, told = pl.pallas_call(
        prepare,
        name="prepare",
        out_shape=[jax.ShapeDtypeStruct(o, F32) for o in ((3, 2, 64, 128), (blocks, 8, nodes))],
        in_specs=[pl.BlockSpec(memory_space=pl.ANY)] * 6,
        out_specs=[VMEM] * 2,
        scratch_shapes=[
            pltpu.SMEM(coeff_table.shape, F32),
            pltpu.VMEM(cell_class.shape, jnp.int32),
            pltpu.VMEM((1, nodes), jnp.int32),
            pltpu.VMEM((3, nodes), F32),
            pltpu.VMEM((1, nodes), F32),
            pltpu.SemaphoreType.DMA((6,)),
        ],
        compiler_params=pltpu.CompilerParams(vmem_limit_bytes=60 << 20),
    )(coeff_table, source, cell_class, owner_cell[None, :], node_pos, node_weight[None, :])
    other = lax.ppermute(packed, "gz", [(0, 1), (1, 0)])
    target = lax.all_to_all(told, ("col", "gz"), 0, 0)
    (packed,) = run(stage, [packed.shape], [packed], scalars=0)
    a, b = run(functools.partial(col_pack, n_col), [(64, 128)] * 2, [me, packed, other])
    a, b = swaps("col", n_col, a, b)
    ext, a, b = run(
        functools.partial(row_pack, n_col), [(12, 64, 256), (14, H, 128), (14, H, 128)], [me, packed, other, a, b]
    )
    a, b = swaps("row", n_row, a, b)

    field = (2, 4, 64 + 2 * H, 256)
    full, first, sent = run(
        functools.partial(first_relax, n_col),
        [(3, 4, 64 + 2 * H, 256), field, (n_row, 8, nodes)],
        [me, ext, a, b, target],
        [field] * 2,
    )
    keep, kept, goal, sent = pl.pallas_call(
        functools.partial(carry_relax, n_col),
        name="carry_relax",
        out_shape=[
            jax.ShapeDtypeStruct((2, 2, 64, 128), F32),
            jax.ShapeDtypeStruct((2, nodes), F32),
            jax.ShapeDtypeStruct((48, blocks * nodes), jnp.bfloat16),
            jax.ShapeDtypeStruct(sent.shape, F32),
        ],
        in_specs=[SMEM] + [VMEM] * 4,
        out_specs=[VMEM] * 4,
        scratch_shapes=[pltpu.VMEM(field, F32)] * 3,
        compiler_params=pltpu.CompilerParams(vmem_limit_bytes=20 << 20),
        cost_estimate=pl.CostEstimate(
            flops=40 * size_of(field), bytes_accessed=4 * size_of(field), transcendentals=0
        ),
    )(me, full, first, target, sent)
    heard = lax.all_to_all(sent, "row", 0, 0)

    everything = lambda shape: pl.BlockSpec(shape, lambda i: (0,) * len(shape))
    work = n_row * blocks * nodes * nodes
    sums = [pltpu.VMEM((2, blocks, 8, nodes), F32), pltpu.VMEM((blocks + 4, 2, nodes), F32)]
    group = min(4, n_row)
    pairs, partial = pl.pallas_call(
        functools.partial(build_apply, n_col, n_row // group),
        name="build_apply",
        grid=(n_row // group,),
        out_shape=[
            jax.ShapeDtypeStruct((n_row, nodes, blocks * nodes), F32),
            jax.ShapeDtypeStruct((blocks, 2, 6 * nodes), F32),
        ],
        in_specs=[SMEM, everything((n_row, 8, nodes)), everything((blocks, 8, nodes)), everything((48, blocks * nodes))],
        out_specs=[
            pl.BlockSpec((group, nodes, blocks * nodes), lambda i: (i, 0, 0)),
            everything((blocks, 2, 6 * nodes)),
        ],
        scratch_shapes=sums,
        compiler_params=pltpu.CompilerParams(vmem_limit_bytes=16 << 20),
        cost_estimate=pl.CostEstimate(flops=18 * work, bytes_accessed=4 * work, transcendentals=work),
    )(me, heard, target, goal)
    partial = lax.all_to_all(partial, ("col", "gz"), 0, 0)
    before, sent, second = run(
        functools.partial(respond, n_col, n_row),
        [(8, 64, 256), (n_row, 8, nodes), field],
        [me, partial, target, full, heard, kept],
        [field] * 3,
    )
    again = lax.all_to_all(sent, "row", 0, 0)
    partial = pl.pallas_call(
        functools.partial(reapply, n_col, n_row // group),
        name="reapply",
        grid=(n_row // group,),
        out_shape=jax.ShapeDtypeStruct((blocks, 2, 6 * nodes), F32),
        in_specs=[
            SMEM,
            everything((n_row, 8, nodes)),
            everything((n_row, 8, nodes)),
            pl.BlockSpec((group, nodes, blocks * nodes), lambda i: (i, 0, 0)),
        ],
        out_specs=everything((blocks, 2, 6 * nodes)),
        scratch_shapes=sums + [pltpu.VMEM((n_row, 8, nodes), F32)],
        compiler_params=pltpu.CompilerParams(vmem_limit_bytes=20 << 20),
        cost_estimate=pl.CostEstimate(flops=4 * work, bytes_accessed=4 * work, transcendentals=0),
    )(me, again, heard, pairs)
    partial = lax.all_to_all(partial, ("col", "gz"), 0, 0)
    spread, a, b, values = run(
        functools.partial(last_spread, n_col),
        [(8, 64, 256), (14, H, 128), (14, H, 128), (2, nodes)],
        [me, partial, target, before],
    )
    a, b = swaps("row", n_row, a, b)
    (part,) = run(
        functools.partial(own_relax, n_col),
        [(2, 2, 64, 128)],
        [me, full, second, spread, keep],
        [field] * 3,
        flops=40 * size_of(field),
    )
    strip = (2, 4, 4 * H, 256)
    (potential,) = run(
        functools.partial(last_relax, n_col), [(2, 2, 64, 128)], [me, full, a, b, part], [strip[1:]] + [strip] * 4
    )
    return potential, values


def solution(mesh):
    return jax.shard_map(
        functools.partial(on_device, mesh.shape["row"], mesh.shape["col"]),
        mesh=mesh,
        in_specs=(
            P(None, "gz", "row", "col"),
            P("gz", "row", "col"),
            P(),
            P(("row", "col", "gz")),
            P(None, ("row", "col", "gz")),
            P(("row", "col", "gz")),
        ),
        out_specs=(P(None, "gz", "row", "col"), P(None, ("row", "col", "gz"))),
        check_vma=False,
    )
```

```python
import functools

import jax
import jax.numpy as jnp
from jax import lax
from jax.experimental import pallas as pl
from jax.experimental.pallas import tpu as pltpu
from jax.sharding import PartitionSpec as P


OMEGA = 0.8
RELAX = 0.5
SOFTEN = 0.01
H = 8
F32 = jnp.float32


def iota(shape, axis):
    return lax.broadcasted_iota(jnp.int32, shape, axis)


def pick(flag, shape, yes, no):
    return jnp.where(jnp.full(shape, flag, jnp.int32) == 1, yes, no)


def place(me_ref, n_col):
    me = me_ref[0]
    gz = lax.rem(me, 2)
    col = lax.rem(me // 2, n_col)
    row = me // (2 * n_col)
    return row, col, gz


def layer_of(own_ref, other_ref, kind, z, gz, shape):
    mine = pick(gz, shape, 1, 0) == z // 2
    return jnp.where(mine, own_ref[kind, z % 2], other_ref[kind, z % 2])


def col_pack(n_col, me_ref, own_ref, other_ref, a_ref, b_ref):
    _, col, gz = place(me_ref, n_col)
    shape = own_ref.shape[2:]
    lane = iota(shape, 1)
    left = jnp.zeros(shape, F32)
    right = jnp.zeros(shape, F32)
    for s in range(12):
        cell = layer_of(own_ref, other_ref, s // 4, s % 4, gz, shape)
        here = (lane >= 8 * s) & (lane < 8 * s + 8)
        low = pltpu.roll(cell, 8 * s, 1) if s else cell
        left = jnp.where(here, low, left)
        right = jnp.where(here, pltpu.roll(cell, 8 * s + 8, 1), right)
    odd = lax.rem(col, 2)
    a_ref[...] = pick(odd, shape, left, right)
    b_ref[...] = pick(odd, shape, right, left)


def edge_row(from_ref, s, last):
    rows, lanes = from_ref.shape[1:]
    return pick(last, (H, lanes), from_ref[s, rows - H : rows, :], from_ref[s, 0:H, :])


def tuck(side, s, into):
    lane = iota(side.shape, 1)
    moved = pltpu.roll(side, (16 * s + 8) % 128, 1)
    return jnp.where((lane >= 16 * s) & (lane < 16 * s + 16), moved, into)


def untuck(tile, s):
    lane = iota(tile.shape, 1)
    moved = pltpu.roll(tile, (128 - 16 * s - 8) % 128, 1)
    return jnp.where((lane < 8) | (lane >= 120), moved, 0.0)


def write_edges(edge_ref, start, from_ref, count, last):
    for first in range(0, count, 8):
        side = jnp.zeros((H, 128), F32)
        for s in range(first, min(first + 8, count)):
            edge = edge_row(from_ref, s, last)
            edge_ref[start + s] = edge[:, 0:128]
            side = tuck(edge[:, 128:256], s - first, side)
        edge_ref[start + count + first // 8] = side


def read_edge(ref, start, s, count):
    return jnp.concatenate([ref[start + s], untuck(ref[start + count + s // 8], s % 8)], 1)


def near_half(last):
    return (iota((H, 128), 0) // 4) == jnp.full((H, 128), last, jnp.int32)


def halo_rows(a, b, odd):
    return pick(odd, a.shape, a, b), pick(odd, a.shape, b, a)


def row_pack(n_col, me_ref, own_ref, other_ref, a_in, b_in, ext_ref, a_ref, b_ref):
    row, col, gz = place(me_ref, n_col)
    shape = own_ref.shape[2:]
    _, lanes = shape
    lane = iota(shape, 1)
    odd_col = lax.rem(col, 2)
    from_right = pick(odd_col, shape, b_in[...], a_in[...])
    from_left = pick(odd_col, shape, a_in[...], b_in[...])
    for s in range(12):
        cell = layer_of(own_ref, other_ref, s // 4, s % 4, gz, shape)
        low = pltpu.roll(from_right, lanes - 8 * s, 1) if s else from_right
        high = pltpu.roll(from_left, lanes - 8 - 8 * s, 1)
        side = jnp.where(lane < 8, low, jnp.where(lane >= lanes - 8, high, 0.0))
        ext_ref[s, :, 0:lanes] = cell
        ext_ref[s, :, lanes : 2 * lanes] = side
    odd = lax.rem(row, 2)
    write_edges(a_ref, 0, ext_ref, 12, 1 - odd)
    write_edges(b_ref, 0, ext_ref, 12, odd)


def sweep(now_ref, next_ref, force_ref, weight_ref, last=False):
    rows, lanes = now_ref.shape[2:]
    line = iota((8, lanes), 0)

    def one(m, z, low, high):
        tiles = rows // 8
        cells = [now_ref[m, z, 8 * i : 8 * i + 8, :] for i in range(tiles)]
        downs = [pltpu.roll(cell, 1, 0) for cell in cells]
        ups = [pltpu.roll(cell, 7, 0) for cell in cells]
        for i in range(1, 3) if last and rows < 64 else range(tiles):
            beside = jnp.where(line == 0, downs[i - 1], downs[i]) + jnp.where(line == 7, ups[(i + 1) % tiles], ups[i])
            beside = beside + (pltpu.roll(cells[i], 1, 1) + pltpu.roll(cells[i], lanes - 1, 1))
            cell = cells[i]
            at = (slice(8 * i, 8 * i + 8), slice(0, lanes))
            if last:
                beside, cell = beside[:, 0:128], cell[:, 0:128]
                at = (slice(8 * i, 8 * i + 8), slice(0, 128))
            if low is not None:
                beside = beside + now_ref[(m, low) + at]
            if high is not None:
                beside = beside + now_ref[(m, high) + at]
            next_ref[(m, z) + at] = (1.0 - OMEGA) * cell + (force_ref[(m, z) + at] + weight_ref[(z,) + at] * beside)

    def image(m, carry):
        for z in range(4):
            one(m, z, z - 1 if z > 0 else None, z + 1 if z < 3 else None)
        return carry

    lax.fori_loop(0, now_ref.shape[0], image, 0, unroll=rows < 64)


def split(x):
    high = x.astype(jnp.bfloat16).astype(F32)
    rest = x - high
    middle = rest.astype(jnp.bfloat16).astype(F32)
    return high, middle, rest - middle


def trace_of(rows, owner, first_row):
    span = rows.shape[0] // 2
    nodes = owner.shape[1]
    line = iota((2 * span, nodes), 0)
    line = line + first_row + jnp.where(line >= span, 64 - span, 0)
    at_row = jnp.where(line == owner // 128, 1.0, 0.0).astype(jnp.bfloat16)
    at_lane = iota((128, nodes), 0) == lax.rem(owner, 128)
    found = sum(
        lax.dot_general(
            part.astype(jnp.bfloat16), at_row, (((0,), (0,)), ((), ())), preferred_element_type=F32
        )
        for part in split(rows)
    )
    return jnp.sum(jnp.where(at_lane, found, 0.0), axis=0, keepdims=True)


def two_layers(field_ref, m, gz, start, size):
    return jnp.concatenate([field_ref[m, 2 * gz + k, start : start + size, 0:128] for k in range(2)], 0)


def prepare(
    table_hbm, source_hbm, class_hbm, owner_hbm, pos_hbm, node_hbm, pack_ref, told_ref,
    table, level_ref, owner_ref, pos_ref, node_ref, sems,
):
    moves = [
        (class_hbm, level_ref),
        (table_hbm, table),
        (owner_hbm, owner_ref),
        (pos_hbm, pos_ref),
        (node_hbm, node_ref),
        (source_hbm, pack_ref.at[0:2]),
    ]
    copies = [pltpu.make_async_copy(a, b, sems.at[k]) for k, (a, b) in enumerate(moves)]
    for copy in copies:
        copy.start()
    for copy in copies:
        copy.wait()
    for k in range(2):
        level = level_ref[k]
        found = jnp.zeros(level.shape, F32)
        for n in range(table.shape[0]):
            found = jnp.where(level == n, table[n], found)
        pack_ref[2, k] = OMEGA / (6.0 + found)
    told_ref[0] = jnp.zeros(told_ref.shape[1:], F32)
    centred = pos_ref[...] - 0.5
    told_ref[0, 2:5, :] = centred
    told_ref[0, 5:6, :] = owner_ref[...].astype(F32)
    told_ref[0, 6:7, :] = node_ref[...]
    told_ref[0, 7:8, :] = jnp.sum(centred * centred, axis=0, keepdims=True)
    for k in range(1, told_ref.shape[0]):
        told_ref[k] = told_ref[0]


def stage(own_ref, out_ref):
    out_ref[...] = own_ref[...]


def first_relax(n_col, me_ref, ext_ref, a_in, b_in, target_ref, full_ref, first_ref, sent_ref, force, spare):
    row, col, gz = place(me_ref, n_col)
    odd = lax.rem(row, 2)
    for s in range(12):
        top, bottom = halo_rows(read_edge(a_in, 0, s, 12), read_edge(b_in, 0, s, 12), odd)
        full_ref[s // 4, s % 4, 0:H, :] = top
        full_ref[s // 4, s % 4, H : H + 64, :] = ext_ref[s]
        full_ref[s // 4, s % 4, H + 64 : 2 * H + 64, :] = bottom
    weight = full_ref.at[2]
    for m in range(2):
        for z in range(4):
            force[m, z] = full_ref[m, z] * weight[z]
    sweep(force, first_ref, force, weight)
    sweep(first_ref, spare, force, weight)
    sweep(spare, first_ref, force, weight)
    info = target_ref[2 * col + gz]
    owner = info[5:6, :].astype(jnp.int32)
    line = iota(info.shape, 0)
    for m in range(2):
        info = jnp.where(line == m, trace_of(two_layers(first_ref, m, gz, H, 64), owner, 0), info)
    for k in range(sent_ref.shape[0]):
        sent_ref[k] = info


def carry_relax(n_col, me_ref, full_ref, first_ref, target_ref, keep_ref, trace_ref, goal, force, spare, other):
    _, col, gz = place(me_ref, n_col)
    weight = full_ref.at[2]
    for m in range(2):
        for z in range(4):
            force[m, z] = (full_ref[m, z] - RELAX * first_ref[m, z]) * weight[z]
    sweep(first_ref, spare, force, weight)
    sweep(spare, other, force, weight)
    sweep(other, spare, force, weight)
    sweep(spare, other, force, weight, True)
    owner = target_ref[2 * col + gz, 5:6, :].astype(jnp.int32)
    for m in range(2):
        for k in range(2):
            keep_ref[m, k] = other[m, 2 * gz + k, H : H + 64, 0:128]
        trace_ref[m : m + 1, :] = trace_of(two_layers(other, m, gz, H, 64), owner, 0)
    nodes = target_ref.shape[2]
    line = iota((8, nodes), 0)
    at_pos = (line >= 2) & (line <= 4)
    for t in range(target_ref.shape[0]):
        info = target_ref[t]
        norm = pltpu.roll(info, 1, 0) + SOFTEN
        base = jnp.where(line == 0, norm, jnp.where(at_pos, -2.0 * info, jnp.where(line == 7, 1.0, 0.0)))
        high, middle, low = split(base)
        rows = jnp.concatenate([high, middle, high, low, high, middle], 0)
        goal[:, t * nodes : (t + 1) * nodes] = rows.astype(jnp.bfloat16)


def columns(rows, count):
    nodes = rows.shape[1]
    return [jnp.broadcast_to(rows[k : k + 1, :], (nodes, nodes)).T for k in range(count)]


def finish_apply(n_col, col, gz, acc, lined, own, out_ref):
    nodes = own.shape[1]
    lined[...] = jnp.zeros_like(lined)
    for t in range(2 * n_col):
        mine = jnp.where(2 * col + gz == t, -0.5, 0.0).astype(F32)
        for m in range(2):
            whole = jnp.sum(acc[m, t], axis=0, keepdims=True)
            lined[t + 2, m : m + 1, :] = whole + mine * own[m : m + 1, :]
    for c in range(n_col):
        for b in range(6):
            near = lined[2 * c + b]
            out_ref[2 * c, :, b * nodes : (b + 1) * nodes] = near
            out_ref[2 * c + 1, :, b * nodes : (b + 1) * nodes] = near


def build_apply(n_col, steps, me_ref, heard_ref, target_ref, goal, pair_ref, out_ref, acc, lined):
    step = pl.program_id(0)
    row, col, gz = place(me_ref, n_col)
    nodes = heard_ref.shape[2]
    blocks = target_ref.shape[0]
    group = pair_ref.shape[0]
    line = iota((8, nodes), 0)
    at_pos = (line >= 2) & (line <= 4)

    @pl.when(step == 0)
    def _():
        acc[...] = jnp.zeros_like(acc)

    starts, z_at, by = [], [], []
    for g in range(group):
        heard = heard_ref[step * group + g]
        base = jnp.where(at_pos | (line == 7), heard, jnp.where(line == 0, 1.0, 0.0))
        high, middle, low = split(base)
        starts.append(jnp.concatenate([high, high, middle, high, low, middle], 0).astype(jnp.bfloat16))
        z_at.append(columns(heard[4:5, :], 1)[0])
        by.append(columns(heard[0:2, :] * heard[6:7, :], 2))
    for g in range(group):
        for t in range(0, blocks, 2):
            squares = lax.dot_general(
                starts[g],
                goal[:, t * nodes : (t + 2) * nodes],
                (((0,), (0,)), ((), ())),
                preferred_element_type=F32,
            )
            for k in range(2):
                dz = target_ref[t + k, 4:5, :] - z_at[g]
                inverse = lax.rsqrt(squares[:, k * nodes : (k + 1) * nodes])
                pair = dz * inverse * (inverse * inverse)
                pair_ref[g, :, (t + k) * nodes : (t + k + 1) * nodes] = pair
                for m in range(2):
                    part = jnp.sum((pair * by[g][m]).reshape(nodes // 8, 8, nodes), axis=0)
                    acc[m, t + k] = acc[m, t + k] + part

    @pl.when(step == steps - 1)
    def _():
        finish_apply(n_col, col, gz, acc, lined, heard_ref[row], out_ref)


def reapply(n_col, steps, me_ref, heard_ref, info_ref, pair_ref, out_ref, acc, lined, trace):
    step = pl.program_id(0)
    row, col, gz = place(me_ref, n_col)
    nodes = heard_ref.shape[2]
    n_row = heard_ref.shape[0]

    @pl.when(step == 0)
    def _():
        acc[...] = jnp.zeros_like(acc)
        for k in range(n_row):
            whole = heard_ref[k, 0:2, :]
            if k + 1 < n_row:
                whole = whole + heard_ref[k + 1, 2:4, :]
            if k > 0:
                whole = whole + heard_ref[k - 1, 4:6, :]
            trace[k, 0:2, :] = whole
            trace[k, 2:4, :] = whole * info_ref[k, 6:7, :]

    for k in range(pair_ref.shape[0]):
        by = columns(trace[step * pair_ref.shape[0] + k, 2:4, :], 2)
        for t in range(2 * n_col):
            pair = pair_ref[k, :, t * nodes : (t + 1) * nodes]
            for m in range(2):
                acc[m, t] = acc[m, t] + jnp.sum((pair * by[m]).reshape(nodes // 8, 8, nodes), axis=0)

    @pl.when(step == steps - 1)
    def _():
        finish_apply(n_col, col, gz, acc, lined, trace[row], out_ref)


def spread_nodes(n_col, col, part_ref, target_ref, spread_ref):
    blocks = 2 * n_col
    nodes = target_ref.shape[2]
    value = part_ref[0]
    for k in range(1, blocks):
        value = value + part_ref[k]
    shape = (128, nodes)
    down = iota(shape, 0)
    weighted, lanes = [], []
    for b in range(6):
        at = jnp.clip(2 * col - 2 + b, 0, blocks - 1)
        owner = target_ref[at, 5:6, :].astype(jnp.int32)
        hit = down == owner // 128
        weighted.append(
            jnp.concatenate([jnp.where(hit, value[m : m + 1, nodes * b : nodes * (b + 1)], 0.0) for m in range(2)], 0)
        )
        lane = down == lax.rem(owner, 128)
        if b < 2:
            lane = lane & (down >= 128 - H)
        if b > 3:
            lane = lane & (down < H)
        lanes.append(jnp.where(lane, 1.0, 0.0).astype(jnp.bfloat16))

    def product(a, b):
        parts = jnp.concatenate(split(a), 0).astype(jnp.bfloat16)
        found = lax.dot_general(parts, b, (((1,), (1,)), ((), ())), preferred_element_type=F32)
        count = a.shape[0]
        return found[0:count] + (found[count : 2 * count] + found[2 * count : 3 * count])

    for g in range(2):
        own = product(weighted[2 + g], lanes[2 + g])
        side = product(
            jnp.concatenate([weighted[g], weighted[4 + g]], 1), jnp.concatenate([lanes[g], lanes[4 + g]], 1)
        )
        for m in range(2):
            for k in range(2):
                start = 128 * m + 64 * k
                spread_ref[4 * m + 2 * g + k, :, 0:128] = own[start : start + 64]
                spread_ref[4 * m + 2 * g + k, :, 128:256] = side[start : start + 64]
    return value


def respond(
    n_col, n_row, me_ref, part_ref, target_ref, full_ref, heard_ref, kept_ref,
    spread_ref, sent_ref, second_ref, force, spare, other,
):
    row, col, gz = place(me_ref, n_col)
    weight = full_ref.at[2]
    spread_nodes(n_col, col, part_ref, target_ref, spread_ref)
    empty = jnp.zeros((H, 256), F32)
    for m in range(2):
        for z in range(4):
            force[m, z, 0:H, :] = empty
            force[m, z, H : H + 64, :] = spread_ref[4 * m + z] * weight[z, H : H + 64]
            force[m, z, H + 64 : 2 * H + 64, :] = empty
    sweep(force, spare, force, weight)
    sweep(spare, other, force, weight)
    sweep(other, second_ref, force, weight)
    for m in range(2):
        for z in range(4):
            force[m, z] = (-RELAX * second_ref[m, z]) * weight[z]
    sweep(force, other, force, weight)
    sweep(other, spare, force, weight)
    sweep(spare, other, force, weight, True)
    own = heard_ref[row, 5:6, :].astype(jnp.int32)
    above = heard_ref[jnp.maximum(row - 1, 0), 5:6, :].astype(jnp.int32)
    below = heard_ref[jnp.minimum(row + 1, n_row - 1), 5:6, :].astype(jnp.int32)
    line = iota((8, own.shape[1]), 0)
    sent = jnp.zeros((8, own.shape[1]), F32)
    for m in range(2):
        here = trace_of(two_layers(other, m, gz, H, 64), own, 0) + kept_ref[m : m + 1, :]
        sent = jnp.where(line == m, here, sent)
        sent = jnp.where(line == 2 + m, trace_of(two_layers(other, m, gz, 0, H), above, 64 - H), sent)
        sent = jnp.where(line == 4 + m, trace_of(two_layers(other, m, gz, H + 64, H), below, 0), sent)
    for k in range(sent_ref.shape[0]):
        sent_ref[k] = sent


def last_spread(n_col, me_ref, part_ref, target_ref, before_ref, spread_ref, a_ref, b_ref, value_ref):
    row, col, gz = place(me_ref, n_col)
    value = spread_nodes(n_col, col, part_ref, target_ref, spread_ref)
    odd = lax.rem(row, 2)
    for edge_ref, last in ((a_ref, 1 - odd), (b_ref, odd)):
        write_edges(edge_ref, 0, before_ref, 8, last)
        near = near_half(last)
        side = jnp.zeros((H, 128), F32)
        for s in range(0, 8, 2):
            one, two = edge_row(spread_ref, s, last), edge_row(spread_ref, s + 1, last)
            edge_ref[9 + s // 2] = jnp.where(near, one[:, 0:128], pltpu.roll(two[:, 0:128], 4, 0))
            side = tuck(one[:, 128:256], s, side)
            side = tuck(two[:, 128:256], s + 1, side)
        edge_ref[13] = side
    for m in range(2):
        value_ref[m : m + 1, :] = pick(
            gz,
            (1, value_ref.shape[1]),
            value[m : m + 1, 3 * value_ref.shape[1] : 4 * value_ref.shape[1]],
            value[m : m + 1, 2 * value_ref.shape[1] : 3 * value_ref.shape[1]],
        )


def own_relax(n_col, me_ref, full_ref, second_ref, spread_ref, keep_ref, out_ref, force, spare, other):
    _, _, gz = place(me_ref, n_col)
    weight = full_ref.at[2]
    for m in range(2):
        for z in range(4):
            force[m, z] = (-RELAX * second_ref[m, z]) * weight[z]
            mid = force[m, z, H : H + 64, :]
            force[m, z, H : H + 64, :] = mid + spread_ref[4 * m + z] * weight[z, H : H + 64]
    sweep(second_ref, spare, force, weight)
    sweep(spare, other, force, weight)
    sweep(other, spare, force, weight)
    sweep(spare, other, force, weight, True)
    for m in range(2):
        for k in range(2):
            out_ref[m, k] = keep_ref[m, k] + other[m, 2 * gz + k, H : H + 64, 0:128]


def last_relax(
    n_col, me_ref, full_ref, a_in, b_in, part_ref, out_ref, weight, force, later, spare, other
):
    row, _, gz = place(me_ref, n_col)
    odd = lax.rem(row, 2)
    empty = jnp.zeros((2 * H, 256), F32)
    for z in range(4):
        weight[z, 0 : 2 * H] = full_ref[2, z, 0 : 2 * H]
        weight[z, 2 * H : 4 * H] = full_ref[2, z, 64 : 64 + 2 * H]
    for s in range(8):
        m, z = s // 4, s % 4
        top, bottom = halo_rows(read_edge(a_in, 0, s, 8), read_edge(b_in, 0, s, 8), odd)
        force[m, z, 0:H] = top * weight[z, 0:H]
        force[m, z, H : 3 * H] = empty
        force[m, z, 3 * H : 4 * H] = bottom * weight[z, 3 * H : 4 * H]
        ends = []
        for ref, last in ((a_in, odd), (b_in, 1 - odd)):
            tile = ref[9 + s // 2]
            main = jnp.where(near_half(last), pltpu.roll(tile, 4, 0) if s % 2 else tile, 0.0)
            ends.append(jnp.concatenate([main, untuck(ref[13], s)], 1))
        top, bottom = halo_rows(ends[0], ends[1], odd)
        later[m, z, 0:H] = top * weight[z, 0:H]
        later[m, z, H : 3 * H] = empty
        later[m, z, 3 * H : 4 * H] = bottom * weight[z, 3 * H : 4 * H]
    sweep(force, spare, force, weight)
    sweep(spare, other, force, weight)
    sweep(other, spare, force, weight)
    for m in range(2):
        for z in range(4):
            later[m, z] = later[m, z] - (RELAX * spare[m, z]) * weight[z]
    sweep(spare, other, later, weight)
    sweep(other, spare, later, weight)
    sweep(spare, other, later, weight)
    sweep(other, spare, later, weight, True)
    for m in range(2):
        for k in range(2):
            found = spare.at[m, 2 * gz + k]
            out_ref[m, k, 0:H, :] = part_ref[m, k, 0:H, :] + found[H : 2 * H, 0:128]
            out_ref[m, k, H : 64 - H, :] = part_ref[m, k, H : 64 - H, :]
            out_ref[m, k, 64 - H : 64, :] = part_ref[m, k, 64 - H : 64, :] + found[2 * H : 3 * H, 0:128]


SMEM = pl.BlockSpec(memory_space=pltpu.SMEM)
VMEM = pl.BlockSpec(memory_space=pltpu.VMEM)


def size_of(shape):
    return functools.reduce(lambda a, b: a * b, shape)


def run(body, outs, args, scratch=(), flops=0, scalars=1):
    moved = sum(a.size * 4 for a in args) + sum(4 * size_of(o) for o in outs)
    return pl.pallas_call(
        body,
        out_shape=[jax.ShapeDtypeStruct(o, F32) for o in outs],
        in_specs=[SMEM] * scalars + [VMEM] * (len(args) - scalars),
        out_specs=[VMEM] * len(outs),
        scratch_shapes=[pltpu.VMEM(s, F32) for s in scratch],
        compiler_params=pltpu.CompilerParams(vmem_limit_bytes=20 << 20),
        cost_estimate=pl.CostEstimate(flops=flops, bytes_accessed=moved, transcendentals=0),
    )(*args)


def on_device(n_row, n_col, source, cell_class, coeff_table, owner_cell, node_pos, node_weight):
    nodes = owner_cell.shape[0]
    blocks = 2 * n_col
    me = lax.axis_index(("row", "col", "gz")).reshape(1)

    def swaps(axis, size, a, b):
        first = [(i, i ^ 1) for i in range(size)]
        second = [(i + 1, i + 2) for i in range(0, size - 2, 2)]
        second = second + [(j, i) for i, j in second]
        a = lax.ppermute(a, axis, first)
        b = lax.ppermute(b, axis, second)
        return a, b

    packed, told = pl.pallas_call(
        prepare,
        name="prepare",
        out_shape=[jax.ShapeDtypeStruct(o, F32) for o in ((3, 2, 64, 128), (blocks, 8, nodes))],
        in_specs=[pl.BlockSpec(memory_space=pl.ANY)] * 6,
        out_specs=[VMEM] * 2,
        scratch_shapes=[
            pltpu.SMEM(coeff_table.shape, F32),
            pltpu.VMEM(cell_class.shape, jnp.int32),
            pltpu.VMEM((1, nodes), jnp.int32),
            pltpu.VMEM((3, nodes), F32),
            pltpu.VMEM((1, nodes), F32),
            pltpu.SemaphoreType.DMA((6,)),
        ],
        compiler_params=pltpu.CompilerParams(vmem_limit_bytes=60 << 20),
    )(coeff_table, source, cell_class, owner_cell[None, :], node_pos, node_weight[None, :])
    other = lax.ppermute(packed, "gz", [(0, 1), (1, 0)])
    target = lax.all_to_all(told, ("col", "gz"), 0, 0)
    (packed,) = run(stage, [packed.shape], [packed], scalars=0)
    a, b = run(functools.partial(col_pack, n_col), [(64, 128)] * 2, [me, packed, other])
    a, b = swaps("col", n_col, a, b)
    ext, a, b = run(
        functools.partial(row_pack, n_col), [(12, 64, 256), (14, H, 128), (14, H, 128)], [me, packed, other, a, b]
    )
    a, b = swaps("row", n_row, a, b)

    field = (2, 4, 64 + 2 * H, 256)
    full, first, sent = run(
        functools.partial(first_relax, n_col),
        [(3, 4, 64 + 2 * H, 256), field, (n_row, 8, nodes)],
        [me, ext, a, b, target],
        [field] * 2,
    )
    heard = lax.all_to_all(sent, "row", 0, 0)
    keep, kept, goal = pl.pallas_call(
        functools.partial(carry_relax, n_col),
        name="carry_relax",
        out_shape=[
            jax.ShapeDtypeStruct((2, 2, 64, 128), F32),
            jax.ShapeDtypeStruct((2, nodes), F32),
            jax.ShapeDtypeStruct((48, blocks * nodes), jnp.bfloat16),
        ],
        in_specs=[SMEM] + [VMEM] * 3,
        out_specs=[VMEM] * 3,
        scratch_shapes=[pltpu.VMEM(field, F32)] * 3,
        compiler_params=pltpu.CompilerParams(vmem_limit_bytes=20 << 20),
        cost_estimate=pl.CostEstimate(
            flops=40 * size_of(field), bytes_accessed=4 * size_of(field), transcendentals=0
        ),
    )(me, full, first, target)

    everything = lambda shape: pl.BlockSpec(shape, lambda i: (0,) * len(shape))
    work = n_row * blocks * nodes * nodes
    sums = [pltpu.VMEM((2, blocks, 8, nodes), F32), pltpu.VMEM((blocks + 4, 2, nodes), F32)]
    group = min(4, n_row)
    pairs, partial = pl.pallas_call(
        functools.partial(build_apply, n_col, n_row // group),
        name="build_apply",
        grid=(n_row // group,),
        out_shape=[
            jax.ShapeDtypeStruct((n_row, nodes, blocks * nodes), F32),
            jax.ShapeDtypeStruct((blocks, 2, 6 * nodes), F32),
        ],
        in_specs=[SMEM, everything((n_row, 8, nodes)), everything((blocks, 8, nodes)), everything((48, blocks * nodes))],
        out_specs=[
            pl.BlockSpec((group, nodes, blocks * nodes), lambda i: (i, 0, 0)),
            everything((blocks, 2, 6 * nodes)),
        ],
        scratch_shapes=sums,
        compiler_params=pltpu.CompilerParams(vmem_limit_bytes=16 << 20),
        cost_estimate=pl.CostEstimate(flops=18 * work, bytes_accessed=4 * work, transcendentals=work),
    )(me, heard, target, goal)
    partial = lax.all_to_all(partial, ("col", "gz"), 0, 0)
    before, sent, second = run(
        functools.partial(respond, n_col, n_row),
        [(8, 64, 256), (n_row, 8, nodes), field],
        [me, partial, target, full, heard, kept],
        [field] * 3,
    )
    again = lax.all_to_all(sent, "row", 0, 0)
    partial = pl.pallas_call(
        functools.partial(reapply, n_col, n_row // group),
        name="reapply",
        grid=(n_row // group,),
        out_shape=jax.ShapeDtypeStruct((blocks, 2, 6 * nodes), F32),
        in_specs=[
            SMEM,
            everything((n_row, 8, nodes)),
            everything((n_row, 8, nodes)),
            pl.BlockSpec((group, nodes, blocks * nodes), lambda i: (i, 0, 0)),
        ],
        out_specs=everything((blocks, 2, 6 * nodes)),
        scratch_shapes=sums + [pltpu.VMEM((n_row, 8, nodes), F32)],
        compiler_params=pltpu.CompilerParams(vmem_limit_bytes=20 << 20),
        cost_estimate=pl.CostEstimate(flops=4 * work, bytes_accessed=4 * work, transcendentals=0),
    )(me, again, heard, pairs)
    partial = lax.all_to_all(partial, ("col", "gz"), 0, 0)
    spread, a, b, values = run(
        functools.partial(last_spread, n_col),
        [(8, 64, 256), (14, H, 128), (14, H, 128), (2, nodes)],
        [me, partial, target, before],
    )
    a, b = swaps("row", n_row, a, b)
    (part,) = run(
        functools.partial(own_relax, n_col),
        [(2, 2, 64, 128)],
        [me, full, second, spread, keep],
        [field] * 3,
        flops=40 * size_of(field),
    )
    strip = (2, 4, 4 * H, 256)
    (potential,) = run(
        functools.partial(last_relax, n_col), [(2, 2, 64, 128)], [me, full, a, b, part], [strip[1:]] + [strip] * 4
    )
    return potential, values


def solution(mesh):
    return jax.shard_map(
        functools.partial(on_device, mesh.shape["row"], mesh.shape["col"]),
        mesh=mesh,
        in_specs=(
            P(None, "gz", "row", "col"),
            P("gz", "row", "col"),
            P(),
            P(("row", "col", "gz")),
            P(None, ("row", "col", "gz")),
            P(("row", "col", "gz")),
        ),
        out_specs=(P(None, "gz", "row", "col"), P(None, ("row", "col", "gz"))),
        check_vma=False,
    )
```
